32 devices in a mesh: members: 2 (over y), lat: 4 (over z), lon: 2 (over x), lev: 2 (over core).
Axes of the slice: x: 2, y: 2, z: 4, core: 2. Of those that a mesh axis runs over, the one named last changes fastest.
Arguments:
- wind_east: float32 [8, 360, 2880], P(('members', 'lev'), 'lat', 'lon'), parts along dimension 0, may hold values from -6 to 6
- wind_north: float32 [8, 360, 2880], P(('members', 'lev'), 'lat', 'lon'), parts along dimension 0, may hold values from -6 to 6
- thickness: float32 [8, 360, 2880], P(('members', 'lev'), 'lat', 'lon'), parts along dimension 0, may hold values from -6 to 6
- geopot: float32 [8, 360, 2880], P(('members', 'lev'), 'lat', 'lon'), parts along dimension 0, may hold values from -6 to 6
- surface_geopot: float32 [360, 2880], P('lat', 'lon'), may hold values from -6 to 6
- mean_depth: float32 [4], P('lev'), may hold values from 0.5 to 2
- kept_modes: int32 [180], replicated, may hold values from 1 to 360
- slot_table: int32 [180], replicated, may hold values from 0 to 179, as said below
Outputs:
- east_final: float32 [8, 360, 2880], P(('members', 'lev'), 'lat', 'lon'), parts along dimension 0
- north_final: float32 [8, 360, 2880], P(('members', 'lev'), 'lat', 'lon'), parts along dimension 0
- thick_new: float32 [8, 360, 2880], P(('members', 'lev'), 'lat', 'lon'), parts along dimension 0
- geo_new: float32 [8, 360, 2880], P(('members', 'lev'), 'lat', 'lon'), parts along dimension 0
- spectra: float32 [2, 8, 180, 720], P(None, ('members', 'lev'), 'lat', 'lon'), parts along dimension 1
The draws below stay inside these ranges and needn't reach their ends.
There are 2 independent parts, one for each index of `members`. The reference program is written for one: setup_inputs(seed, part) draws one part's arguments, and reference() takes and returns one part's arrays. A program takes and returns all parts, laid end to end along the dimension named above; an argument that names none is the same for every part. Nothing has to cross between parts.
Inputs may be any that keep to these rules, and one draw needn't show every extreme that they name: `slot_table`: every slot 0 to 179 is named once; slot s belongs to latitude device s // 45. Of the 90 polar rows held by latitude device d, 45 name slots of device d and 45 name slots of the device half the lat axis away, (d + 4 / 2) mod 4.
All inputs are finite; a program needn't handle non-finite values.
Results may differ from the reference program's by a relative error of at most 0.00019.
Values sent between devices are 32-bit elements; how exact they have to be, the bound alone decides.
A program may use at most 64 MiB of HBM per device.

```python
import math
import jax
import jax.numpy as jnp

NLON = 2880
KMAX = 360
LAT_DEV = 90
NLAT = 360
LEVELS = 4
NP = 90
HELP = 45


def draw_kept_modes(key, part):
    row_rank = jnp.arange(2 * NP, dtype=jnp.int32)
    from_pole = jnp.where(row_rank < NP, row_rank, 2 * NP - 1 - row_rank)
    ramp_value = 1 + (KMAX - 1) * from_pole // (NP - 1)
    jitter_span = max(1, KMAX // 16)
    jitter = jax.random.randint(jax.random.fold_in(key, 7), (2 * NP,), -jitter_span, jitter_span + 1)
    kept_count = jnp.clip(ramp_value + jitter, 1, KMAX)
    kept_count = jnp.where(from_pole == NP - 1, KMAX, kept_count)
    kept_count = jnp.where(from_pole == 0, 1, kept_count)
    return kept_count.astype(jnp.int32)


def draw_slot_table(key, part):
    lat_devices = NLAT // LAT_DEV
    owners = 2 * NP // LAT_DEV
    split_keys = jax.random.split(jax.random.fold_in(key, 12), owners)
    row_ranks = jax.vmap(lambda one_key: jax.random.permutation(one_key, LAT_DEV))(split_keys)
    row_ranks = row_ranks.reshape(-1).astype(jnp.int32)
    owner_block = jnp.arange(2 * NP, dtype=jnp.int32) // LAT_DEV
    owner_device = jnp.where(owner_block < lat_devices // 4, owner_block, owner_block + lat_devices // 2)
    partner_device = (owner_device + lat_devices // 2) % lat_devices
    target_device = jnp.where(row_ranks < HELP, owner_device, partner_device)
    position = row_ranks % HELP
    return (target_device * HELP + position).astype(jnp.int32)


def levels(own_key, shape, cuts, least, top_value):
    gain, own = 1.0, jax.random.fold_in(own_key, 6)
    for dim, parts in cuts:
        draws = jnp.exp(jax.random.uniform(jax.random.fold_in(own, dim), (parts,), jnp.float32, least / len(cuts), top_value / len(cuts)))
        gain = gain * jnp.repeat(draws, shape[dim] // parts).reshape([-1 if axis == dim else 1 for axis in range(len(shape))])
    return gain


def normal_values(key, extent, scale, most, cuts=(), kind=jnp.bfloat16):
    values = scale * jax.random.normal(key, extent, jnp.float32)
    if cuts:
        values = values * levels(key, extent, cuts, -0.22, 0.18)
    return jnp.clip(values, -most, most).astype(kind)


def setup_inputs(seed: int = 0, part: int = 0) -> dict:
    streams_of = jax.random.split(jax.random.key(seed), 9)
    part_splits = jax.random.split(jax.random.fold_in(streams_of[8], part), 9)
    return {
        "wind_east": normal_values(part_splits[0], (LEVELS, NLAT, NLON), 1.0, 6.0, ((0, 2), (1, 4), (2, 2)), jnp.float32),
        "wind_north": normal_values(part_splits[1], (LEVELS, NLAT, NLON), 1.0, 6.0, ((0, 2), (1, 4), (2, 2)), jnp.float32),
        "thickness": normal_values(part_splits[2], (LEVELS, NLAT, NLON), 1.0, 6.0, ((0, 2), (1, 4), (2, 2)), jnp.float32),
        "geopot": normal_values(part_splits[3], (LEVELS, NLAT, NLON), 1.0, 6.0, ((0, 2), (1, 4), (2, 2)), jnp.float32),
        "surface_geopot": normal_values(streams_of[4], (NLAT, NLON), 1.0, 6.0, ((0, 4), (1, 2)), jnp.float32),
        "mean_depth": jnp.clip(jnp.exp(math.log(2.0) - 1.3862944 * jax.random.uniform(streams_of[5], (LEVELS,), jnp.float32) ** levels(streams_of[5], (LEVELS,), ((0, 2),), -0.2, 0.2)), 0.5, 2.0),
        "kept_modes": draw_kept_modes(jax.random.fold_in(streams_of[8], 71), part),
        "slot_table": draw_slot_table(jax.random.fold_in(streams_of[8], 71), part),
    }


STEP_FACTOR = 0.15
CORIOLIS = 0.2
GRAVITY = 0.25


def east_diff(stacked):
    return jnp.roll(stacked, -1, axis=-1) - jnp.roll(stacked, 1, axis=-1)


def north_diff(stacked):
    padded = jnp.pad(stacked, ((0, 0), (1, 1), (0, 0)))
    return padded[:, 2:, :] - padded[:, :-2, :]


def reference(wind_east, wind_north, thickness, geopot, surface_geopot, mean_depth, kept_modes, slot_table):
    lam_step = 2.0 * math.pi / NLON
    phi_step = math.pi / NLAT
    latitude = -0.5 * math.pi + (jnp.arange(NLAT, dtype=jnp.float32) + 0.5) * phi_step
    coslat = jnp.cos(latitude)[:, None]
    sinlat = jnp.sin(latitude)[:, None]
    east_coef = STEP_FACTOR / coslat
    north_coef = STEP_FACTOR * lam_step / phi_step
    east_new = wind_east - east_coef * east_diff(geopot) + CORIOLIS * sinlat * wind_north
    north_new = wind_north - north_coef * north_diff(geopot) - CORIOLIS * sinlat * wind_east
    polar_rows = jnp.concatenate([jnp.arange(NP), jnp.arange(NLAT - NP, NLAT)]).astype(jnp.int32)
    wind_pair = jnp.stack([east_new, north_new])
    polar_part = wind_pair[:, :, polar_rows, :]
    transform = jnp.fft.rfft(polar_part, axis=-1)[..., :KMAX]
    wavenumber = jnp.arange(KMAX)
    weight = jnp.where(wavenumber == 0, 1.0, 2.0) / NLON
    keep_mask = wavenumber[None, :] < kept_modes[:, None]
    factor = jnp.where(keep_mask, weight[None, :], 0.0)
    cos_part = jnp.real(transform) * factor
    sin_part = -jnp.imag(transform) * factor
    ordered = jnp.concatenate([cos_part, sin_part], axis=-1)
    spectra = jnp.zeros_like(ordered).at[:, :, slot_table, :].set(ordered)
    masked = jnp.where(keep_mask, transform, jnp.zeros_like(transform))
    masked = jnp.pad(masked, ((0, 0), (0, 0), (0, 0), (0, NLON // 2 + 1 - KMAX)))
    filtered = jnp.fft.irfft(masked, n=NLON, axis=-1)
    wind_pair = wind_pair.at[:, :, polar_rows, :].set(filtered)
    east_final = wind_pair[0]
    north_final = wind_pair[1]
    divergence = east_coef * east_diff(east_final) + (north_coef / coslat) * north_diff(north_final * coslat)
    thick_new = thickness - mean_depth[:, None, None] * divergence
    column = jnp.cumsum(thick_new[::-1], axis=0)[::-1]
    geo_new = surface_geopot[None] + GRAVITY * column
    return (east_final, north_final, thick_new, geo_new, spectra)
```

```python
import math

import functools

import jax
import numpy as np
import jax.numpy as jnp
from jax import lax
from jax.experimental import pallas as pl
from jax.experimental.pallas import tpu as pltpu
from jax.sharding import PartitionSpec as P

KMAX = 360


STEP_FACTOR = 0.15
CORIOLIS = 0.2
GRAVITY = 0.25


def edges(block, axis, dim, periodic):
    count = lax.axis_size(axis)
    first = lax.slice_in_dim(block, 0, 1, axis=dim)
    last = lax.slice_in_dim(block, block.shape[dim] - 1, block.shape[dim], axis=dim)
    if periodic and count == 2:
        both = lax.ppermute(jnp.concatenate([last, first], axis=dim), axis, [(0, 1), (1, 0)])
        return lax.slice_in_dim(both, 0, 1, axis=dim), lax.slice_in_dim(both, 1, 2, axis=dim)
    forward = [(i, i + 1) for i in range(count - 1)]
    if periodic:
        forward.append((count - 1, 0))
    backward = [(target, source) for source, target in forward]
    return lax.ppermute(last, axis, forward), lax.ppermute(first, axis, backward)


def diff(block, low, high, dim):
    size = block.shape[dim]
    up = jnp.concatenate([lax.slice_in_dim(block, 1, size, axis=dim), high], axis=dim)
    down = jnp.concatenate([low, lax.slice_in_dim(block, 0, size - 1, axis=dim)], axis=dim)
    return up - down


def local_basis(count, nlon_total):
    fine = next(f for f in (24, 20, 18, 16, 12, 8, 6, 5, 4, 3, 2, 1) if count % f == 0)
    k = np.arange(KMAX, dtype=np.int64)[None, :]
    angle = 2.0 * np.pi / nlon_total

    def table(columns):
        phase = (columns[:, None] * k % nlon_total) * angle
        return np.cos(phase).astype(np.float32), np.sin(phase).astype(np.float32)

    cc, cs = (jnp.asarray(t)[:, None] for t in table(np.arange(0, count, fine)))
    fc, fs = (jnp.asarray(t)[None] for t in table(np.arange(fine)))
    return (
        (cc * fc - cs * fs).reshape(count, KMAX),
        (cs * fc + cc * fs).reshape(count, KMAX),
    )


def turned(pair, cos_shift, sin_shift):
    cos_part, sin_part = pair[..., :KMAX], pair[..., KMAX:]
    return jnp.concatenate(
        [cos_shift * cos_part - sin_shift * sin_part, sin_shift * cos_part + cos_shift * sin_part],
        axis=-1,
    )


def local(
    wind_east, wind_north, thickness, geopot, surface_geopot, mean_depth, kept_modes, slot_table
):
    lev_dev, lat_dev, lon_dev = thickness.shape
    lat_count = lax.axis_size("lat")
    lon_count = lax.axis_size("lon")
    lev_count = lax.axis_size("lev")
    lat_index = lax.axis_index("lat")
    lon_index = lax.axis_index("lon")
    nlat_total = lat_dev * lat_count
    nlon_total = lon_dev * lon_count
    polar_count = nlat_total // 4
    slot_count = 2 * polar_count
    help_rows = lat_dev // 2
    half_axis = lat_count // 2
    lam_step = 2.0 * math.pi / nlon_total
    phi_step = math.pi / nlat_total
    global_rows = lat_index * lat_dev + jnp.arange(lat_dev, dtype=jnp.int32)
    latitude = -0.5 * math.pi + (global_rows.astype(jnp.float32) + 0.5) * phi_step
    coslat = jnp.cos(latitude)[:, None]
    sinlat = jnp.sin(latitude)[:, None]
    east_coef = STEP_FACTOR / coslat
    north_coef = STEP_FACTOR * lam_step / phi_step
    geo_west, geo_east = edges(geopot, "lon", 2, True)
    geo_south, geo_north = edges(geopot, "lat", 1, False)
    east_new = (
        wind_east
        - east_coef * diff(geopot, geo_west, geo_east, 2)
        + CORIOLIS * sinlat * wind_north
    )
    north_new = (
        wind_north
        - north_coef * diff(geopot, geo_south, geo_north, 1)
        - CORIOLIS * sinlat * wind_east
    )
    is_polar = (lat_index < lat_count // 4) | (lat_index >= lat_count - lat_count // 4)
    first_row = lat_index * lat_dev
    first_rank = jnp.where(lat_index < lat_count // 4, first_row, first_row - (nlat_total - slot_count))
    first_rank = jnp.clip(first_rank, 0, slot_count - lat_dev)
    kept = lax.dynamic_slice(kept_modes, (first_rank,), (lat_dev,))
    slots = lax.dynamic_slice(slot_table, (first_rank,), (lat_dev,))
    wavenumber = jnp.arange(2 * KMAX, dtype=jnp.int32) % KMAX
    weight = (jnp.where(wavenumber == 0, 1.0, 2.0) / nlon_total).astype(jnp.float32)
    factor = jnp.where(wavenumber[None, :] < kept[:, None], weight[None, :], 0.0)
    cos_basis, sin_basis = local_basis(lon_dev, nlon_total)
    basis = jnp.concatenate([cos_basis, sin_basis], axis=1)
    shift = (lon_index * jnp.arange(KMAX, dtype=jnp.int32) % lon_count).astype(jnp.float32)
    shift = shift * (2.0 * math.pi / lon_count)
    if lon_count == 2:
        cos_shift = 1.0 - 2.0 * (lon_index * jnp.arange(KMAX, dtype=jnp.int32) % 2).astype(jnp.float32)
        sin_shift = jnp.zeros_like(cos_shift)
    else:
        cos_shift, sin_shift = jnp.cos(shift), jnp.sin(shift)
    pieces = [wind[level] for level in range(lev_dev) for wind in (east_new, north_new)]
    both_sums = []
    for piece in range(lev_dev):
        rows = jnp.concatenate(pieces[2 * piece : 2 * piece + 2], axis=0)
        part = jnp.dot(rows, basis, precision=lax.Precision.HIGH)
        part = turned(part, cos_shift, sin_shift)
        if lon_count == 2:
            sums = part + lax.ppermute(part, "lon", [(0, 1), (1, 0)])
        else:
            sums = lax.psum(part, "lon")
        both_sums.append(sums.reshape(2, lat_dev, 2 * KMAX) * factor[None])
    filtered = []
    for sums in both_sums:
        turned_back = turned(sums, cos_shift, -sin_shift)
        rows = lax.dot_general(
            turned_back.reshape(2 * lat_dev, 2 * KMAX),
            basis,
            (((1,), (1,)), ((), ())),
            precision=lax.Precision.HIGH,
        )
        filtered.append(rows.reshape(2, lat_dev, lon_dev))
    filtered = jnp.stack(filtered, axis=1)
    east_final = jnp.where(is_polar, filtered[0], east_new)
    north_final = jnp.where(is_polar, filtered[1], north_new)

    slice_width = 2 * KMAX // lon_count
    kept_sums = jnp.stack(both_sums, axis=1)
    own = lax.dynamic_slice_in_dim(kept_sums, lon_index * slice_width, slice_width, 3)
    places = jnp.arange(help_rows, dtype=jnp.int32)
    partner = (lat_index + half_axis) % lat_count

    def rows_named(device):
        match = slots[None, :] == (device * help_rows + places)[:, None]
        return jnp.einsum(
            "sr,abrc->absc", match.astype(jnp.float32), own, precision=lax.Precision.HIGHEST
        )

    route = [((i - half_axis) % lat_count, i) for i in range(lat_count)]
    route = [(s, t) for s, t in route if s < lat_count // 4 or s >= lat_count - lat_count // 4]
    arrived = lax.ppermute(rows_named(partner), "lat", route)
    spectra = jnp.where(is_polar, rows_named(lat_index), arrived)

    rim_west, rim_east = edges(east_final, "lon", 2, True)
    flux = north_final * coslat
    rim_south, rim_north = edges(flux, "lat", 1, False)
    divergence = east_coef * diff(east_final, rim_west, rim_east, 2) + north_coef / coslat * diff(
        flux, rim_south, rim_north, 1
    )
    thick_new = thickness - mean_depth[:, None, None] * divergence
    columns = [thick_new[lev_dev - 1]]
    for level in range(lev_dev - 2, -1, -1):
        columns.append(columns[-1] + thick_new[level])
    columns = columns[::-1]
    deeper = jnp.zeros_like(columns[0])
    for distance in range(1, lev_count):
        deeper = deeper + lax.ppermute(
            columns[0], "lev", [(i + distance, i) for i in range(lev_count - distance)]
        )
    geo_new = surface_geopot[None] + GRAVITY * (jnp.stack(columns) + deeper[None])
    return (east_final, north_final, thick_new, geo_new, spectra)


FINE = 32
VMEM_MIB = 30
CHUNK = 128
BLOCK = 16
PIECES = (
    (((0, 40),), ((176, 184),), ((40, 72), (112, 64))),
    (((176, 184),), (), ((0, 88), (88, 88))),
    (((176, 184),), (), ((0, 88), (88, 88))),
)


def angle_tables(width, count, nlon_total):
    k = np.arange(count, dtype=np.int64)[None, :]
    angle = 2.0 * np.pi / nlon_total

    def table(columns):
        phase = (columns[:, None] * k % nlon_total) * angle
        return np.stack([np.cos(phase), np.sin(phase)]).astype(np.float32)

    starts = np.arange(0, width, FINE)
    starts[-1] = -FINE
    return table(starts), table(np.arange(FINE))


def split(x):
    high = x.astype(jnp.bfloat16)
    return high, (x - high.astype(jnp.float32)).astype(jnp.bfloat16)


def dot(a, b, dims):
    return lax.dot_general(a, b, (dims, ((), ())), preferred_element_type=jnp.float32)


def substep_kernel(
    sizes,
    depth_hbm, kept_hbm, slot_hbm, coarse_hbm, fine_hbm,
    we_hbm, wn_hbm, th_hbm, geo_hbm, sg_hbm,
    east_out, north_out, thick_out, geo_out, spectra_out,
    depth_ref, kept_ref, slot_ref, coarse_ref, fine_ref,
    geo, sg,
    xs, high_ref, low_ref, part, came, hop, held_sums, acc, flux,
    lon_put, lon_got, lat_put, lat_got, column_put, column_got, fix_put, fix_got,
    spec_put, spec_got, table_ref,
    in_sem, lon_sem, lat_sem, direct_sem, hop_sem, column_sem, fix_sem, spec_sem,
):
    lat_count, nlon_total, phi_step, north_coef = sizes
    lev_dev, lat_dev, lon_dev = east_out.shape
    help_rows = spectra_out.shape[2]
    _, pad_rows, width = acc.shape
    half_rows = spec_put.shape[2]
    chunks = len(PIECES)
    lon = lax.axis_index("lon")
    lat = lax.axis_index("lat")
    lev = lax.axis_index("lev")
    polar = (lat == 0) | (lat == lat_count - 1)
    inner = jnp.logical_not(polar)
    low_side = lat < lat_count // 2
    band = {"lat": lat + 1 - 2 * lax.rem(lat, 2)}
    across = {"lon": 1 - lon, **band}
    other_lon = {"lon": 1 - lon}
    other_lev = {"lev": 1 - lev}
    middle = {"lat": lat_count - 1 - lat}
    partner = lax.rem(lat + lat_count // 2, lat_count)
    far = {"lat": partner}
    MESH = pl.DeviceIdType.MESH

    barrier = pltpu.get_barrier_semaphore()
    for target in (other_lon, other_lev, band, across):
        pl.semaphore_signal(barrier, inc=1, device_id=target, device_id_type=MESH)

    @pl.when(inner)
    def _():
        pl.semaphore_signal(barrier, inc=1, device_id=middle, device_id_type=MESH)

    tile = width - 128
    for level in range(lev_dev):
        for ref in (geo, flux):
            start = 8 + lat_dev // 8 * 8
            ref[level, start:, :] = jnp.zeros((ref.shape[1] - start, width), jnp.float32)
            ref[level, 0:8, :] = jnp.zeros((8, width), jnp.float32)
        geo[level, :, tile:] = jnp.zeros((geo.shape[1], 128), jnp.float32)

    def load(src, dst, i, j):
        copy = pltpu.make_async_copy(src, dst, in_sem.at[i, j])
        copy.start()
        return copy

    loads = {}
    loads["tables"] = [load(coarse_hbm, coarse_ref, 0, 0), load(fine_hbm, fine_ref, 0, 1)]
    for i, (name, src, dst) in enumerate(
        (("geo", geo_hbm, geo_out), ("we", we_hbm, east_out), ("wn", wn_hbm, north_out), ("th", th_hbm, thick_out))
    ):
        loads[name] = [load(src.at[:, level, :], dst.at[level], 1 + i, level) for level in range(lev_dev)]
    loads["sg"] = [load(sg_hbm, sg, 5, 0), load(depth_hbm, depth_ref, 5, 1)]
    loads["rows"] = [load(kept_hbm, kept_ref, 6, 0), load(slot_hbm, slot_ref, 6, 1)]

    def arrive(*names):
        for name in names:
            for copy in loads[name]:
                copy.wait()

    def remote(src, dst, sems, target):
        return pltpu.make_async_remote_copy(
            src_ref=src, dst_ref=dst, send_sem=sems.at[0], recv_sem=sems.at[1],
            device_id=target, device_id_type=MESH,
        )

    row_id = lax.broadcasted_iota(jnp.int32, (pad_rows, 1), 0) + lat * lat_dev
    latitude = -0.5 * math.pi + (row_id.astype(jnp.float32) + 0.5) * phi_step
    cos_lat = jnp.cos(latitude)
    sin_lat = jnp.sin(latitude)
    east_coef = STEP_FACTOR / cos_lat
    flux_coef = north_coef / cos_lat
    turn_coef = CORIOLIS * sin_lat
    starts = range(0, pad_rows, BLOCK)

    def east_diff(x):
        return pltpu.roll(x, width - 1, 1) - pltpu.roll(x, 1, 1)

    def kept_rows(r):
        return slice(r, min(r + BLOCK, lat_dev)), min(BLOCK, lat_dev - r)

    def padded(x):
        count = x.shape[0]
        x = jnp.concatenate([x, jnp.zeros((count, width - lon_dev), jnp.float32)], axis=1)
        if count < BLOCK:
            x = jnp.concatenate([x, jnp.zeros((BLOCK - count, width), jnp.float32)], axis=0)
        return x

    def take_geo():
        arrive("geo")
        for level in range(lev_dev):
            geo[level, 8 : 8 + lat_dev, 0:lon_dev] = geo_out[level]

    def east_rows(level, r):
        at = slice(r, r + BLOCK)
        rows, _ = kept_rows(r)
        winds = east_out[level, rows, :] + turn_coef[rows] * north_out[level, rows, :]
        return padded(winds) - east_coef[at] * east_diff(geo[level, 8 + r : 8 + r + BLOCK, :])

    def north_rows(level, r):
        rows, _ = kept_rows(r)
        winds = north_out[level, rows, :] - turn_coef[rows] * east_out[level, rows, :]
        step = geo[level, 9 + r : 9 + r + BLOCK, :] - geo[level, 7 + r : 7 + r + BLOCK, :]
        return padded(winds) - north_coef * step

    def lat_pair(turn):
        south = remote(lat_put.at[turn, 0], lat_got.at[turn, 1], lat_sem.at[turn, 0], {"lat": lat - 1})
        north = remote(lat_put.at[turn, 1], lat_got.at[turn, 0], lat_sem.at[turn, 1], {"lat": lat + 1})
        return south, north

    has_south = lat > 0
    has_north = lat < lat_count - 1

    def send_lat(turn, firsts, lasts):
        for level in range(lev_dev):
            lat_put[turn, 0, level : level + 1, :] = firsts[level]
            lat_put[turn, 1, level : level + 1, :] = lasts[level]
        south, north = lat_pair(turn)

        @pl.when(has_south)
        def _():
            south.start()

        @pl.when(has_north)
        def _():
            north.start()

    def sent_lat(turn):
        south, north = lat_pair(turn)

        @pl.when(has_south)
        def _():
            south.wait_send()

        @pl.when(has_north)
        def _():
            north.wait_send()

    def from_south(turn, ref):
        lat_pair(turn)[1].wait_recv()
        for level in range(lev_dev):
            ref[level, 7:8, :] = lat_got[turn, 0, level : level + 1, :]

    def from_north(turn, ref):
        lat_pair(turn)[0].wait_recv()
        for level in range(lev_dev):
            ref[level, 8 + lat_dev : 9 + lat_dev, :] = lat_got[turn, 1, level : level + 1, :]

    def send_geo_rows():
        send_lat(
            0,
            [geo[level, 8:9, :] for level in range(lev_dev)],
            [geo[level, 7 + lat_dev : 8 + lat_dev, :] for level in range(lev_dev)],
        )

    def send_flux_rows():
        send_lat(
            1,
            [acc[lev_dev + level, 0:1, :] * cos_lat[0:1] for level in range(lev_dev)],
            [
                acc[lev_dev + level, lat_dev - 1 : lat_dev, :] * cos_lat[lat_dev - 1 : lat_dev]
                for level in range(lev_dev)
            ],
        )

    edge_lane = lax.broadcasted_iota(jnp.int32, (lat_dev, 128), 1)

    def lon_copy(turn):
        return remote(lon_put.at[turn], lon_got.at[turn], lon_sem.at[turn], other_lon)

    def send_lon(turn, ref, top):
        held = jnp.zeros((lat_dev, 128), jnp.float32)
        for level in range(lev_dev):
            rows = slice(top, top + lat_dev)
            held = jnp.where(edge_lane == 2 * level, ref[level, rows, 0:1], held)
            held = jnp.where(edge_lane == 2 * level + 1, ref[level, rows, lon_dev - 1 : lon_dev], held)
        lon_put[turn, :, 0:lat_dev] = jnp.transpose(held)[0:8]
        lon_copy(turn).start()

    def from_lon(turn, ref, top):
        lon_copy(turn).wait()
        rims = jnp.transpose(lon_got[turn])[0:lat_dev]
        for level in range(lev_dev):
            rows = slice(top, top + lat_dev)
            last = ref[level, rows, tile:]
            last = jnp.where(edge_lane == lon_dev - tile, rims[:, 2 * level : 2 * level + 1], last)
            last = jnp.where(edge_lane == 127, rims[:, 2 * level + 1 : 2 * level + 2], last)
            ref[level, rows, tile:] = last

    def make_basis(chunk):
        at = slice(chunk * CHUNK, (chunk + 1) * CHUNK)

        def body(block, _):
            p = coarse_ref[0, pl.ds(block, 1), :][:, at]
            q = coarse_ref[1, pl.ds(block, 1), :][:, at]
            f, g = fine_ref[0, :, at], fine_ref[1, :, at]
            rows = pl.ds(pl.multiple_of(block * FINE, FINE), FINE)
            for place, values in enumerate((p * f - q * g, q * f + p * g)):
                high, low = split(values)
                high_ref[chunk, rows, place * CHUNK : (place + 1) * CHUNK] = high
                low_ref[chunk, rows, place * CHUNK : (place + 1) * CHUNK] = low
            return _

        lax.fori_loop(0, width // FINE, body, 0)

    stack = lev_dev * pad_rows

    def make_terms(wind, rows):
        for level in range(lev_dev):
            for r in starts:
                high, low = split(rows(level, r))
                at = level * pad_rows + r
                xs[wind, at : at + BLOCK, :] = high
                xs[wind, stack + at : stack + at + BLOCK, :] = low

    def forward(chunk, wind):
        sums = dot(xs[wind], high_ref[chunk], ((1,), (0,)))
        sums = sums[0:stack] + sums[stack:] + dot(xs[wind, 0:stack, :], low_ref[chunk], ((1,), (0,)))
        for level in range(lev_dev):
            at = (wind * lev_dev + level) * lat_dev
            part[chunk, at : at + lat_dev, :] = sums[level * pad_rows : level * pad_rows + lat_dev]

    directs, hops = [], []
    for chunk, (first, second, relayed) in enumerate(PIECES):
        directs.append(
            [
                remote(
                    part.at[chunk, pl.ds(start, size)], came.at[chunk, pl.ds(start, size)],
                    direct_sem.at[chunk, i], other_lon,
                )
                for i, (start, size) in enumerate(first + second)
            ]
        )
        base = relayed[0][0]
        pairs = []
        for i, (start, size) in enumerate(relayed):
            full, held = pl.ds(start, size), pl.ds(start - base, size)
            pairs.append(
                (
                    remote(part.at[chunk, full], hop.at[chunk, held], hop_sem.at[chunk, i, 0], across),
                    remote(hop.at[chunk, held], came.at[chunk, full], hop_sem.at[chunk, i, 1], band),
                )
            )
        hops.append(pairs)

    def relay(chunk):
        for out, back in hops[chunk]:
            out.wait_recv()
            back.start()

    spec_copies = [remote(spec_put.at[c], spec_got.at[c], spec_sem.at[c], far) for c in range(chunks)]

    def spectra_width(chunk):
        return min(CHUNK, spectra_out.shape[3] - chunk * CHUNK)

    column_rows = 2 * BLOCK
    column_copies = [
        remote(
            column_put.at[pl.ds(r, column_rows)], column_got.at[pl.ds(r, column_rows)],
            column_sem.at[r // column_rows], other_lev,
        )
        for r in range(0, pad_rows, column_rows)
    ]

    def make_flux():
        for level in range(lev_dev):
            for r in starts:
                rows, count = kept_rows(r)
                north = acc[lev_dev + level, r : r + BLOCK, :]
                north_out[level, rows, :] = north[0:count, 0:lon_dev]
                flux[level, 8 + r : 8 + r + count, :] = (north * cos_lat[r : r + BLOCK])[0:count]

    def finish():
        for r in starts:
            at = slice(r, r + BLOCK)
            rows, count = kept_rows(r)
            below = None
            for level in range(lev_dev - 1, -1, -1):
                east = acc[level, at, :]
                step = flux[level, 9 + r : 9 + r + BLOCK, :] - flux[level, 7 + r : 7 + r + BLOCK, :]
                divergence = east_coef[at] * east_diff(east) + flux_coef[at] * step
                divergence = divergence[0:count, 0:lon_dev]
                thick = thick_out[level, rows, :] - depth_ref[0:1, level : level + 1] * divergence
                below = thick if below is None else below + thick
                east_out[level, rows, :] = east[0:count, 0:lon_dev]
                thick_out[level, rows, :] = thick
                geo_out[level, rows, :] = sg[rows, :] + GRAVITY * below
            column_put[rows, :] = below
            if (r + BLOCK) % column_rows == 0:

                @pl.when(lev == 1)
                def _():
                    column_copies[r // column_rows].start()

    def deepen():
        @pl.when(lev == 0)
        def _():
            for i, copy in enumerate(column_copies):
                copy.wait_recv()
                for r in range(i * column_rows, (i + 1) * column_rows, BLOCK):
                    rows, _ = kept_rows(r)
                    for level in range(lev_dev):
                        geo_out[level, rows, :] += GRAVITY * column_got[rows, :]

        @pl.when(lev == 1)
        def _():
            for copy in column_copies:
                copy.wait_send()

    @pl.when(polar)
    def _():
        arrive("tables")
        make_basis(0)
        take_geo()
        arrive("we", "wn")
        make_terms(0, east_rows)
        forward(0, 0)

    @pl.when(inner)
    def _():
        take_geo()

    pl.semaphore_wait(barrier, 4 + inner.astype(jnp.int32))

    @pl.when(inner)
    def _():
        send_geo_rows()
        send_lon(0, geo, 8)
        arrive("we", "wn")
        from_lon(0, geo, 8)
        from_south(0, geo)
        from_north(0, geo)
        for level in range(lev_dev):
            for r in starts:
                acc[level, r : r + BLOCK, :] = east_rows(level, r)
                acc[lev_dev + level, r : r + BLOCK, :] = north_rows(level, r)
        send_flux_rows()
        send_lon(1, acc, 0)
        relay(0)
        make_flux()
        from_lon(1, acc, 0)

        @pl.when(low_side)
        def _():
            from_north(1, flux)

        @pl.when(jnp.logical_not(low_side))
        def _():
            from_south(1, flux)

        arrive("th", "sg")
        finish()
        relay(1)
        deepen()

    @pl.when(polar)
    def _():
        for copy in directs[0][: len(PIECES[0][0])]:
            copy.start()
        for out, _ in hops[0]:
            out.start()
        send_geo_rows()

        @pl.when(low_side)
        def _():
            from_north(0, geo)

        @pl.when(jnp.logical_not(low_side))
        def _():
            from_south(0, geo)

        make_terms(1, north_rows)
        forward(0, 1)
        for copy in directs[0][len(PIECES[0][0]) :]:
            copy.start()
        for chunk in range(1, chunks):
            make_basis(chunk)
            forward(chunk, 0)
            for out, _ in hops[chunk]:
                out.start()
            forward(chunk, 1)
            for copy in directs[chunk]:
                copy.start()

        arrive("rows")
        sides = lax.broadcasted_iota(jnp.int32, table_ref.shape, 0)
        table_ref[...] = jnp.where(sides == 1, -1.0, 0.0)
        for side, here in enumerate((low_side, jnp.logical_not(low_side))):
            columns = slice(side * lat_dev, (side + 1) * lat_dev)

            @pl.when(here)
            def _():
                table_ref[0:1, 0:lat_dev] = kept_ref[:, columns].astype(jnp.float32)
                table_ref[1:2, 0:lat_dev] = slot_ref[:, columns].astype(jnp.float32)

        table = jnp.transpose(table_ref[...])
        kept = table[0:pad_rows, 0:1].astype(jnp.int32)
        slots = table[0:pad_rows, 1:2].astype(jnp.int32)
        place = lax.broadcasted_iota(jnp.int32, (pad_rows, 2 * half_rows), 1)
        own = place >= half_rows
        place = jnp.where(own, place - half_rows, place)
        named = jnp.where(own, lat, partner) * help_rows + place
        match = ((slots == named) & (place < help_rows)).astype(jnp.float32).astype(jnp.bfloat16)
        column = lax.broadcasted_iota(jnp.int32, (pad_rows, 2 * CHUNK), 1)
        local_number = jnp.where(column < CHUNK, column, column - CHUNK)
        odd = 1.0 - 2.0 * lax.rem(local_number[0:1], 2).astype(jnp.float32)
        groups = 2 * lev_dev
        total = groups * pad_rows

        for chunk in range(chunks):
            number = local_number + chunk * CHUNK
            weight = jnp.where(number == 0, 1.0 / nlon_total, 2.0 / nlon_total)
            for copy in directs[chunk]:
                copy.wait_recv()
            for _, back in hops[chunk]:
                back.wait_recv()
            picked = []
            for group in range(groups):
                rows = slice(group * lat_dev, group * lat_dev + pad_rows)
                sums = (part[chunk, rows, :] + odd * came[chunk, rows, :]) * weight
                sums = jnp.where(number < kept, sums, 0.0)
                high, low = split(sums)
                at = group * pad_rows
                held_sums[at : at + pad_rows, :] = high
                held_sums[total + at : total + at + pad_rows, :] = low
                picked.append(jnp.where(lon == 0, sums[:, 0:CHUNK], (sums * odd)[:, CHUNK:]))
            picked = jnp.concatenate(picked, axis=1)
            high, rest = picked.astype(jnp.bfloat16), None
            rest = picked - high.astype(jnp.float32)
            mid, low = split(rest)
            placed = dot(match, high, ((0,), (0,))) + dot(match, mid, ((0,), (0,))) + dot(match, low, ((0,), (0,)))
            for group in range(groups):
                spec_put[chunk, group] = placed[0:half_rows, group * CHUNK : (group + 1) * CHUNK]
            spec_copies[chunk].start()
            count = spectra_width(chunk)
            for group in range(groups):
                spectra_out[group // lev_dev, group % lev_dev, :, chunk * CHUNK : chunk * CHUNK + count] = placed[
                    half_rows : half_rows + help_rows, group * CHUNK : group * CHUNK + count
                ]
            for at in range(0, width, 512):
                columns = slice(at, at + 512)
                both = dot(held_sums[...], high_ref[chunk, columns, :], ((1,), (1,)))
                rest = dot(held_sums[0:total, :], low_ref[chunk, columns, :], ((1,), (1,)))
                values = both[0:total] + both[total:] + rest
                for group in range(groups):
                    piece = values[group * pad_rows : (group + 1) * pad_rows]
                    if chunk:
                        piece = piece + acc[group, :, columns]
                    acc[group, :, columns] = piece

        sent_lat(0)
        send_flux_rows()
        make_flux()

        @pl.when(low_side)
        def _():
            from_north(1, flux)

        @pl.when(jnp.logical_not(low_side))
        def _():
            from_south(1, flux)

        arrive("th", "sg")
        finish()
        deepen()
        for chunk in range(chunks):
            spec_copies[chunk].wait_send()
            for copy in directs[chunk]:
                copy.wait_send()
            for out, _ in hops[chunk]:
                out.wait_send()
        sent_lat(1)

    @pl.when(inner)
    def _():
        arrive("tables", "rows")
        for chunk in range(chunks):
            if chunk > 1:
                relay(chunk)
            spec_copies[chunk].wait_recv()
            count = spectra_width(chunk)
            for group in range(2 * lev_dev):
                spectra_out[group // lev_dev, group % lev_dev, :, chunk * CHUNK : chunk * CHUNK + count] = spec_got[
                    chunk, group, 0:help_rows, 0:count
                ]
        for pairs in hops:
            for _, back in pairs:
                back.wait_send()
        sent_lat(0)
        sent_lat(1)
        fix_copy = remote(fix_put, fix_got, fix_sem, other_lev)

        def fix(side, row, sign):
            at = slice(row, row + 1)
            deltas = [
                depth_ref[0:1, level : level + 1]
                * (sign * flux_coef[at])
                * lat_got[1, side, level : level + 1, :]
                for level in range(lev_dev)
            ]
            below = None
            for level in range(lev_dev - 1, -1, -1):
                below = deltas[level] if below is None else below + deltas[level]
                thick_out[level, at, :] += deltas[level][:, 0:lon_dev]
                geo_out[level, at, :] += GRAVITY * below[:, 0:lon_dev]
            fix_put[...] = below

            @pl.when(lev == 1)
            def _():
                fix_copy.start()
                fix_copy.wait_send()

            @pl.when(lev == 0)
            def _():
                fix_copy.wait_recv()
                for level in range(lev_dev):
                    geo_out[level, at, :] += GRAVITY * fix_got[:, 0:lon_dev]

        @pl.when(low_side)
        def _():
            lat_pair(1)[1].wait_recv()
            fix(0, 0, 1.0)

        @pl.when(jnp.logical_not(low_side))
        def _():
            lat_pair(1)[0].wait_recv()
            fix(1, lat_dev - 1, -1.0)


def hand_on_kernel(*refs):
    half = (len(refs) - 1) // 2
    sems = refs[-1]
    copies = []
    for index, (src, dst) in enumerate(zip(refs[:half], refs[half:-1])):
        levels = src.shape[-3]
        for level in range(levels):
            if len(src.shape) == 3:
                pairs = [(src.at[level], dst.at[:, level, :])]
            else:
                pairs = [(src.at[wind, level], dst.at[wind, :, level, :]) for wind in range(src.shape[0])]
            for wind, (part, place) in enumerate(pairs):
                copies.append(pltpu.make_async_copy(part, place, sems.at[index, wind * levels + level]))
    for copy in copies:
        copy.start()
    for copy in copies:
        copy.wait()


def handed_on(held):
    def shape(x):
        return jax.ShapeDtypeStruct((*x.shape[:-3], x.shape[-2], x.shape[-3], x.shape[-1]), x.dtype)

    return pl.pallas_call(
        hand_on_kernel,
        out_shape=[shape(x) for x in held],
        in_specs=[pl.BlockSpec(memory_space=pltpu.VMEM)] * len(held),
        out_specs=[pl.BlockSpec(memory_space=pl.ANY)] * len(held),
        scratch_shapes=[pltpu.SemaphoreType.DMA((len(held), 2 * held[0].shape[0]))],
        compiler_params=pltpu.CompilerParams(vmem_limit_bytes=4 * 2**20),
    )(*(pltpu.with_memory_space_constraint(x, pltpu.VMEM) for x in held))


def one_kernel(
    wind_east, wind_north, thickness, geopot, surface_geopot, mean_depth, kept_modes, slot_table
):
    lev_dev, lat_dev, lon_dev = thickness.shape
    lat_count = lax.axis_size("lat")
    nlat_total = lat_dev * lat_count
    nlon_total = 2 * lon_dev
    help_rows = lat_dev // 2
    lam_step = 2.0 * math.pi / nlon_total
    phi_step = math.pi / nlat_total
    north_coef = STEP_FACTOR * lam_step / phi_step
    width = -(-(lon_dev + 2) // 512) * 512
    pad_rows = -(-lat_dev // 32) * 32
    half_rows = pad_rows // 2
    chunks = len(PIECES)
    coarse, fine = angle_tables(width, chunks * CHUNK, nlon_total)
    f32 = jnp.float32
    field = pltpu.VMEM((lev_dev, lat_dev, lon_dev), f32)
    tall = pltpu.VMEM((lev_dev, pad_rows + 16, width), f32)
    groups = 2 * lev_dev
    basis = pltpu.VMEM((chunks, width, 2 * CHUNK), jnp.bfloat16)
    sums = pltpu.VMEM((chunks, groups * lat_dev + 8, 2 * CHUNK), f32)
    relayed = max(sum(size for _, size in pieces[2]) for pieces in PIECES)
    lat_rows = pltpu.VMEM((2, 2, lev_dev, width), f32)
    lon_rows = pltpu.VMEM((2, 8, 128), f32)
    column = pltpu.VMEM((pad_rows, lon_dev), f32)
    row = pltpu.VMEM((1, width), f32)
    specs = pltpu.VMEM((chunks, groups, half_rows, CHUNK), f32)
    dma = pltpu.SemaphoreType.DMA
    operands = (
        mean_depth.reshape(1, -1),
        kept_modes.reshape(1, -1),
        slot_table.reshape(1, -1),
        jnp.asarray(coarse),
        jnp.asarray(fine),
        *(jnp.transpose(x, (1, 0, 2)) for x in (wind_east, wind_north, thickness, geopot)),
        surface_geopot,
    )
    held = pl.pallas_call(
        functools.partial(substep_kernel, (lat_count, nlon_total, phi_step, north_coef)),
        out_shape=(field,) * 4 + (pltpu.VMEM((2, lev_dev, help_rows, KMAX), f32),),
        in_specs=[pl.BlockSpec(memory_space=pl.ANY)] * len(operands),
        out_specs=(pl.BlockSpec(memory_space=pltpu.VMEM),) * 5,
        scratch_shapes=[
            pltpu.VMEM((1, lev_dev), f32),
            pltpu.VMEM((1, kept_modes.shape[0]), jnp.int32),
            pltpu.VMEM((1, slot_table.shape[0]), jnp.int32),
            pltpu.VMEM(coarse.shape, f32),
            pltpu.VMEM(fine.shape, f32),
            tall,
            pltpu.VMEM((lat_dev, lon_dev), f32),
            pltpu.VMEM((2, 2 * lev_dev * pad_rows, width), jnp.bfloat16),
            basis, basis, sums, sums,
            pltpu.VMEM((chunks, relayed, 2 * CHUNK), f32),
            pltpu.VMEM((2 * groups * pad_rows, 2 * CHUNK), jnp.bfloat16),
            pltpu.VMEM((groups, pad_rows, width), f32),
            tall,
            lon_rows, lon_rows, lat_rows, lat_rows, column, column, row, row, specs, specs,
            pltpu.VMEM((8, 128), f32),
            dma((7, 2)), dma((2, 2)), dma((2, 2, 2)), dma((chunks, 2, 2)), dma((chunks, 3, 2, 2)),
            dma((pad_rows // (2 * BLOCK), 2)), dma((2,)), dma((chunks, 2)),
        ],
        compiler_params=pltpu.CompilerParams(
            collective_id=0, has_side_effects=True, vmem_limit_bytes=VMEM_MIB * 2**20
        ),
    )(*(pltpu.with_memory_space_constraint(x, pltpu.HBM) for x in operands))
    *fields, spectra = handed_on(held)
    return (*(jnp.transpose(x, (1, 0, 2)) for x in fields), jnp.transpose(spectra, (0, 2, 1, 3)))


def solution(mesh):
    body = one_kernel if dict(mesh.shape, members=2) == dict(members=2, lat=4, lon=2, lev=2) else local
    return jax.shard_map(
        body,
        mesh=mesh,
        in_specs=(
            P(("members", "lev"), "lat", "lon"),
            P(("members", "lev"), "lat", "lon"),
            P(("members", "lev"), "lat", "lon"),
            P(("members", "lev"), "lat", "lon"),
            P("lat", "lon"),
            P("lev"),
            P(),
            P(),
        ),
        out_specs=(
            P(("members", "lev"), "lat", "lon"),
            P(("members", "lev"), "lat", "lon"),
            P(("members", "lev"), "lat", "lon"),
            P(("members", "lev"), "lat", "lon"),
            P(None, ("members", "lev"), "lat", "lon"),
        ),
        check_vma=False,
    )
```

```python
import math

import functools

import jax
import numpy as np
import jax.numpy as jnp
from jax import lax
from jax.experimental import pallas as pl
from jax.experimental.pallas import tpu as pltpu
from jax.sharding import PartitionSpec as P

KMAX = 360


STEP_FACTOR = 0.15
CORIOLIS = 0.2
GRAVITY = 0.25


def edges(block, axis, dim, periodic):
    count = lax.axis_size(axis)
    first = lax.slice_in_dim(block, 0, 1, axis=dim)
    last = lax.slice_in_dim(block, block.shape[dim] - 1, block.shape[dim], axis=dim)
    if periodic and count == 2:
        both = lax.ppermute(jnp.concatenate([last, first], axis=dim), axis, [(0, 1), (1, 0)])
        return lax.slice_in_dim(both, 0, 1, axis=dim), lax.slice_in_dim(both, 1, 2, axis=dim)
    forward = [(i, i + 1) for i in range(count - 1)]
    if periodic:
        forward.append((count - 1, 0))
    backward = [(target, source) for source, target in forward]
    return lax.ppermute(last, axis, forward), lax.ppermute(first, axis, backward)


def diff(block, low, high, dim):
    size = block.shape[dim]
    up = jnp.concatenate([lax.slice_in_dim(block, 1, size, axis=dim), high], axis=dim)
    down = jnp.concatenate([low, lax.slice_in_dim(block, 0, size - 1, axis=dim)], axis=dim)
    return up - down


def local_basis(count, nlon_total):
    fine = next(f for f in (24, 20, 18, 16, 12, 8, 6, 5, 4, 3, 2, 1) if count % f == 0)
    k = np.arange(KMAX, dtype=np.int64)[None, :]
    angle = 2.0 * np.pi / nlon_total

    def table(columns):
        phase = (columns[:, None] * k % nlon_total) * angle
        return np.cos(phase).astype(np.float32), np.sin(phase).astype(np.float32)

    cc, cs = (jnp.asarray(t)[:, None] for t in table(np.arange(0, count, fine)))
    fc, fs = (jnp.asarray(t)[None] for t in table(np.arange(fine)))
    return (
        (cc * fc - cs * fs).reshape(count, KMAX),
        (cs * fc + cc * fs).reshape(count, KMAX),
    )


def turned(pair, cos_shift, sin_shift):
    cos_part, sin_part = pair[..., :KMAX], pair[..., KMAX:]
    return jnp.concatenate(
        [cos_shift * cos_part - sin_shift * sin_part, sin_shift * cos_part + cos_shift * sin_part],
        axis=-1,
    )


def local(
    wind_east, wind_north, thickness, geopot, surface_geopot, mean_depth, kept_modes, slot_table
):
    lev_dev, lat_dev, lon_dev = thickness.shape
    lat_count = lax.axis_size("lat")
    lon_count = lax.axis_size("lon")
    lev_count = lax.axis_size("lev")
    lat_index = lax.axis_index("lat")
    lon_index = lax.axis_index("lon")
    nlat_total = lat_dev * lat_count
    nlon_total = lon_dev * lon_count
    polar_count = nlat_total // 4
    slot_count = 2 * polar_count
    help_rows = lat_dev // 2
    half_axis = lat_count // 2
    lam_step = 2.0 * math.pi / nlon_total
    phi_step = math.pi / nlat_total
    global_rows = lat_index * lat_dev + jnp.arange(lat_dev, dtype=jnp.int32)
    latitude = -0.5 * math.pi + (global_rows.astype(jnp.float32) + 0.5) * phi_step
    coslat = jnp.cos(latitude)[:, None]
    sinlat = jnp.sin(latitude)[:, None]
    east_coef = STEP_FACTOR / coslat
    north_coef = STEP_FACTOR * lam_step / phi_step
    geo_west, geo_east = edges(geopot, "lon", 2, True)
    geo_south, geo_north = edges(geopot, "lat", 1, False)
    east_new = (
        wind_east
        - east_coef * diff(geopot, geo_west, geo_east, 2)
        + CORIOLIS * sinlat * wind_north
    )
    north_new = (
        wind_north
        - north_coef * diff(geopot, geo_south, geo_north, 1)
        - CORIOLIS * sinlat * wind_east
    )
    is_polar = (lat_index < lat_count // 4) | (lat_index >= lat_count - lat_count // 4)
    first_row = lat_index * lat_dev
    first_rank = jnp.where(lat_index < lat_count // 4, first_row, first_row - (nlat_total - slot_count))
    first_rank = jnp.clip(first_rank, 0, slot_count - lat_dev)
    kept = lax.dynamic_slice(kept_modes, (first_rank,), (lat_dev,))
    slots = lax.dynamic_slice(slot_table, (first_rank,), (lat_dev,))
    wavenumber = jnp.arange(2 * KMAX, dtype=jnp.int32) % KMAX
    weight = (jnp.where(wavenumber == 0, 1.0, 2.0) / nlon_total).astype(jnp.float32)
    factor = jnp.where(wavenumber[None, :] < kept[:, None], weight[None, :], 0.0)
    cos_basis, sin_basis = local_basis(lon_dev, nlon_total)
    basis = jnp.concatenate([cos_basis, sin_basis], axis=1)
    shift = (lon_index * jnp.arange(KMAX, dtype=jnp.int32) % lon_count).astype(jnp.float32)
    shift = shift * (2.0 * math.pi / lon_count)
    if lon_count == 2:
        cos_shift = 1.0 - 2.0 * (lon_index * jnp.arange(KMAX, dtype=jnp.int32) % 2).astype(jnp.float32)
        sin_shift = jnp.zeros_like(cos_shift)
    else:
        cos_shift, sin_shift = jnp.cos(shift), jnp.sin(shift)
    pieces = [wind[level] for level in range(lev_dev) for wind in (east_new, north_new)]
    both_sums = []
    for piece in range(lev_dev):
        rows = jnp.concatenate(pieces[2 * piece : 2 * piece + 2], axis=0)
        part = jnp.dot(rows, basis, precision=lax.Precision.HIGH)
        part = turned(part, cos_shift, sin_shift)
        if lon_count == 2:
            sums = part + lax.ppermute(part, "lon", [(0, 1), (1, 0)])
        else:
            sums = lax.psum(part, "lon")
        both_sums.append(sums.reshape(2, lat_dev, 2 * KMAX) * factor[None])
    filtered = []
    for sums in both_sums:
        turned_back = turned(sums, cos_shift, -sin_shift)
        rows = lax.dot_general(
            turned_back.reshape(2 * lat_dev, 2 * KMAX),
            basis,
            (((1,), (1,)), ((), ())),
            precision=lax.Precision.HIGH,
        )
        filtered.append(rows.reshape(2, lat_dev, lon_dev))
    filtered = jnp.stack(filtered, axis=1)
    east_final = jnp.where(is_polar, filtered[0], east_new)
    north_final = jnp.where(is_polar, filtered[1], north_new)

    slice_width = 2 * KMAX // lon_count
    kept_sums = jnp.stack(both_sums, axis=1)
    own = lax.dynamic_slice_in_dim(kept_sums, lon_index * slice_width, slice_width, 3)
    places = jnp.arange(help_rows, dtype=jnp.int32)
    partner = (lat_index + half_axis) % lat_count

    def rows_named(device):
        match = slots[None, :] == (device * help_rows + places)[:, None]
        return jnp.einsum(
            "sr,abrc->absc", match.astype(jnp.float32), own, precision=lax.Precision.HIGHEST
        )

    route = [((i - half_axis) % lat_count, i) for i in range(lat_count)]
    route = [(s, t) for s, t in route if s < lat_count // 4 or s >= lat_count - lat_count // 4]
    arrived = lax.ppermute(rows_named(partner), "lat", route)
    spectra = jnp.where(is_polar, rows_named(lat_index), arrived)

    rim_west, rim_east = edges(east_final, "lon", 2, True)
    flux = north_final * coslat
    rim_south, rim_north = edges(flux, "lat", 1, False)
    divergence = east_coef * diff(east_final, rim_west, rim_east, 2) + north_coef / coslat * diff(
        flux, rim_south, rim_north, 1
    )
    thick_new = thickness - mean_depth[:, None, None] * divergence
    columns = [thick_new[lev_dev - 1]]
    for level in range(lev_dev - 2, -1, -1):
        columns.append(columns[-1] + thick_new[level])
    columns = columns[::-1]
    deeper = jnp.zeros_like(columns[0])
    for distance in range(1, lev_count):
        deeper = deeper + lax.ppermute(
            columns[0], "lev", [(i + distance, i) for i in range(lev_count - distance)]
        )
    geo_new = surface_geopot[None] + GRAVITY * (jnp.stack(columns) + deeper[None])
    return (east_final, north_final, thick_new, geo_new, spectra)


FINE = 32
VMEM_MIB = 30
CHUNK = 128
BLOCK = 16
DIRECT = 61


def unit_order(chunks):
    last = chunks - 1
    return [(c, w) for w in range(2) for c in range(last)] + [(last, 0), (last, 1)]


def shares(rows):
    direct = rows * DIRECT // 100 // 8 * 8
    first = direct + (rows - direct) // 16 * 8
    return direct, ((direct, first - direct), (first, rows - first))


def angle_tables(width, count, nlon_total):
    k = np.arange(count, dtype=np.int64)[None, :]
    angle = 2.0 * np.pi / nlon_total

    def table(columns):
        phase = (columns[:, None] * k % nlon_total) * angle
        return np.stack([np.cos(phase), np.sin(phase)]).astype(np.float32)

    starts = np.arange(0, width, FINE)
    starts[-1] = -FINE
    return table(starts), table(np.arange(FINE))


def split(x):
    high = x.astype(jnp.bfloat16)
    return high, (x - high.astype(jnp.float32)).astype(jnp.bfloat16)


def dot(a, b, dims):
    return lax.dot_general(a, b, (dims, ((), ())), preferred_element_type=jnp.float32)


def substep_kernel(
    sizes,
    depth_hbm, kept_hbm, slot_hbm, coarse_hbm, fine_hbm,
    we_hbm, wn_hbm, th_hbm, geo_hbm, sg_hbm,
    east_out, north_out, thick_out, geo_out, spectra_out,
    depth_ref, kept_ref, slot_ref, coarse_ref, fine_ref,
    geo, sg,
    xs, high_ref, low_ref, part, came, hop, held_sums, acc, flux,
    lon_put, lon_got, lat_put, lat_got, column_put, column_got, fix_put, fix_got,
    spec_put, spec_got, table_ref,
    in_sem, lon_sem, lat_sem, direct_sem, hop_sem, column_sem, fix_sem, spec_sem,
):
    lat_count, nlon_total, phi_step, north_coef = sizes
    lev_dev, lat_dev, lon_dev = east_out.shape
    help_rows = spectra_out.shape[2]
    _, pad_rows, width = acc.shape
    half_rows = spec_put.shape[-2]
    chunks = high_ref.shape[0]
    units = unit_order(chunks)
    lon = lax.axis_index("lon")
    lat = lax.axis_index("lat")
    lev = lax.axis_index("lev")
    polar = (lat == 0) | (lat == lat_count - 1)
    inner = jnp.logical_not(polar)
    low_side = lat < lat_count // 2
    band = {"lat": lat + 1 - 2 * lax.rem(lat, 2)}
    across = {"lon": 1 - lon, **band}
    aside = {"lev": 1 - lev, **band}
    other_lon = {"lon": 1 - lon}
    other_lev = {"lev": 1 - lev}
    middle = {"lat": lat_count - 1 - lat}
    partner = lax.rem(lat + lat_count // 2, lat_count)
    far = {"lat": partner}
    MESH = pl.DeviceIdType.MESH

    barrier = pltpu.get_barrier_semaphore()
    for target in (other_lon, other_lev, band, across, aside):
        pl.semaphore_signal(barrier, inc=1, device_id=target, device_id_type=MESH)

    @pl.when(inner)
    def _():
        pl.semaphore_signal(barrier, inc=1, device_id=middle, device_id_type=MESH)

    tile = width - 128
    for level in range(lev_dev):
        for ref in (geo, flux):
            start = 8 + lat_dev // 8 * 8
            ref[level, start:, :] = jnp.zeros((ref.shape[1] - start, width), jnp.float32)
            ref[level, 0:8, :] = jnp.zeros((8, width), jnp.float32)
        geo[level, :, tile:] = jnp.zeros((geo.shape[1], 128), jnp.float32)

    def load(src, dst, i, j):
        return pltpu.make_async_copy(src, dst, in_sem.at[i, j])

    def fetch(*names):
        for name in names:
            for copy in loads[name]:
                copy.start()

    loads = {}
    loads["tables"] = [load(coarse_hbm, coarse_ref, 0, 0), load(fine_hbm, fine_ref, 0, 1)]
    for i, (name, src, dst) in enumerate(
        (("geo", geo_hbm, geo_out), ("we", we_hbm, east_out), ("wn", wn_hbm, north_out), ("th", th_hbm, thick_out))
    ):
        loads[name] = [load(src.at[:, level, :], dst.at[level], 1 + i, level) for level in range(lev_dev)]
    loads["sg"] = [load(sg_hbm, sg, 5, 0), load(depth_hbm, depth_ref, 5, 1)]
    loads["rows"] = [load(kept_hbm, kept_ref, 6, 0), load(slot_hbm, slot_ref, 6, 1)]

    fetch("tables", "geo", "we", "wn")

    def arrive(*names):
        for name in names:
            for copy in loads[name]:
                copy.wait()

    def remote(src, dst, sems, target):
        return pltpu.make_async_remote_copy(
            src_ref=src, dst_ref=dst, send_sem=sems.at[0], recv_sem=sems.at[1],
            device_id=target, device_id_type=MESH,
        )

    row_id = lax.broadcasted_iota(jnp.int32, (pad_rows, 1), 0) + lat * lat_dev
    latitude = -0.5 * math.pi + (row_id.astype(jnp.float32) + 0.5) * phi_step
    cos_lat = jnp.cos(latitude)
    sin_lat = jnp.sin(latitude)
    east_coef = STEP_FACTOR / cos_lat
    flux_coef = north_coef / cos_lat
    turn_coef = CORIOLIS * sin_lat
    starts = range(0, pad_rows, BLOCK)

    def east_diff(x):
        return pltpu.roll(x, width - 1, 1) - pltpu.roll(x, 1, 1)

    def kept_rows(r):
        return slice(r, min(r + BLOCK, lat_dev)), min(BLOCK, lat_dev - r)

    def padded(x):
        count = x.shape[0]
        x = jnp.concatenate([x, jnp.zeros((count, width - lon_dev), jnp.float32)], axis=1)
        if count < BLOCK:
            x = jnp.concatenate([x, jnp.zeros((BLOCK - count, width), jnp.float32)], axis=0)
        return x

    def take_geo():
        arrive("geo")
        for level in range(lev_dev):
            geo[level, 8 : 8 + lat_dev, 0:lon_dev] = geo_out[level]

    def east_rows(level, r):
        at = slice(r, r + BLOCK)
        rows, _ = kept_rows(r)
        winds = east_out[level, rows, :] + turn_coef[rows] * north_out[level, rows, :]
        return padded(winds) - east_coef[at] * east_diff(geo[level, 8 + r : 8 + r + BLOCK, :])

    def north_rows(level, r):
        rows, _ = kept_rows(r)
        winds = north_out[level, rows, :] - turn_coef[rows] * east_out[level, rows, :]
        step = geo[level, 9 + r : 9 + r + BLOCK, :] - geo[level, 7 + r : 7 + r + BLOCK, :]
        return padded(winds) - north_coef * step

    def lat_pair(turn):
        south = remote(lat_put.at[turn, 0], lat_got.at[turn, 1], lat_sem.at[turn, 0], {"lat": lat - 1})
        north = remote(lat_put.at[turn, 1], lat_got.at[turn, 0], lat_sem.at[turn, 1], {"lat": lat + 1})
        return south, north

    has_south = lat > 0
    has_north = lat < lat_count - 1

    def send_lat(turn, firsts, lasts):
        for level in range(lev_dev):
            lat_put[turn, 0, level : level + 1, :] = firsts[level]
            lat_put[turn, 1, level : level + 1, :] = lasts[level]
        south, north = lat_pair(turn)

        @pl.when(has_south)
        def _():
            south.start()

        @pl.when(has_north)
        def _():
            north.start()

    def sent_lat(turn):
        south, north = lat_pair(turn)

        @pl.when(has_south)
        def _():
            south.wait_send()

        @pl.when(has_north)
        def _():
            north.wait_send()

    def from_south(turn, ref):
        lat_pair(turn)[1].wait_recv()
        for level in range(lev_dev):
            ref[level, 7:8, :] = lat_got[turn, 0, level : level + 1, :]

    def from_north(turn, ref):
        lat_pair(turn)[0].wait_recv()
        for level in range(lev_dev):
            ref[level, 8 + lat_dev : 9 + lat_dev, :] = lat_got[turn, 1, level : level + 1, :]

    def send_geo_rows():
        send_lat(
            0,
            [geo[level, 8:9, :] for level in range(lev_dev)],
            [geo[level, 7 + lat_dev : 8 + lat_dev, :] for level in range(lev_dev)],
        )

    def send_flux_rows():
        send_lat(
            1,
            [acc[lev_dev + level, 0:1, :] * cos_lat[0:1] for level in range(lev_dev)],
            [
                acc[lev_dev + level, lat_dev - 1 : lat_dev, :] * cos_lat[lat_dev - 1 : lat_dev]
                for level in range(lev_dev)
            ],
        )

    fix_copy = remote(fix_put, fix_got, fix_sem, aside)

    def send_fix():
        below = None
        for level in range(lev_dev):
            row = jnp.where(low_side, lat_put[1, 1, level : level + 1, :], lat_put[1, 0, level : level + 1, :])
            row = depth_ref[0:1, level : level + 1] * row
            below = row if below is None else below + row
        fix_put[...] = below

        @pl.when(lev == 1)
        def _():
            fix_copy.start()

    edge_lane = lax.broadcasted_iota(jnp.int32, (lat_dev, 128), 1)

    def lon_copy(turn):
        return remote(lon_put.at[turn], lon_got.at[turn], lon_sem.at[turn], other_lon)

    def send_lon(turn, ref, top):
        held = jnp.zeros((lat_dev, 128), jnp.float32)
        for level in range(lev_dev):
            rows = slice(top, top + lat_dev)
            held = jnp.where(edge_lane == 2 * level, ref[level, rows, 0:1], held)
            held = jnp.where(edge_lane == 2 * level + 1, ref[level, rows, lon_dev - 1 : lon_dev], held)
        lon_put[turn, :, 0:lat_dev] = jnp.transpose(held)[0:8]
        lon_copy(turn).start()

    def from_lon(turn, ref, top):
        lon_copy(turn).wait()
        rims = jnp.transpose(lon_got[turn])[0:lat_dev]
        for level in range(lev_dev):
            rows = slice(top, top + lat_dev)
            last = ref[level, rows, tile:]
            last = jnp.where(edge_lane == lon_dev - tile, rims[:, 2 * level : 2 * level + 1], last)
            last = jnp.where(edge_lane == 127, rims[:, 2 * level + 1 : 2 * level + 2], last)
            ref[level, rows, tile:] = last

    def make_basis(chunk):
        at = slice(chunk * CHUNK, (chunk + 1) * CHUNK)

        def body(block, _):
            p = coarse_ref[0, pl.ds(block, 1), :][:, at]
            q = coarse_ref[1, pl.ds(block, 1), :][:, at]
            f, g = fine_ref[0, :, at], fine_ref[1, :, at]
            rows = pl.ds(pl.multiple_of(block * FINE, FINE), FINE)
            for place, values in enumerate((p * f - q * g, q * f + p * g)):
                high, low = split(values)
                high_ref[chunk, rows, place * CHUNK : (place + 1) * CHUNK] = high
                low_ref[chunk, rows, place * CHUNK : (place + 1) * CHUNK] = low
            return _

        lax.fori_loop(0, width // FINE, body, 0)

    stack = lev_dev * pad_rows

    def make_terms(wind, rows):
        for level in range(lev_dev):
            for r in starts:
                high, low = split(rows(level, r))
                at = level * pad_rows + r
                xs[wind, at : at + BLOCK, :] = high
                xs[wind, stack + at : stack + at + BLOCK, :] = low

    def forward(chunk, wind):
        sums = dot(xs[wind], high_ref[chunk], ((1,), (0,)))
        sums = sums[0:stack] + sums[stack:] + dot(xs[wind, 0:stack, :], low_ref[chunk], ((1,), (0,)))
        for level in range(lev_dev):
            at = level * lat_dev
            part[chunk, wind, at : at + lat_dev, :] = sums[level * pad_rows : level * pad_rows + lat_dev]

    def inverse(chunk, wind):
        for at in range(0, width, 512):
            columns = slice(at, at + 512)
            values = dot(held_sums[wind], high_ref[chunk, columns, :], ((1,), (1,)))
            rest = dot(held_sums[wind, 0:stack, :], low_ref[chunk, columns, :], ((1,), (1,)))
            values = values[0:stack] + values[stack:] + rest
            for level in range(lev_dev):
                group = wind * lev_dev + level
                piece = values[level * pad_rows : (level + 1) * pad_rows]
                if chunk:
                    piece = piece + acc[group, :, columns]
                acc[group, :, columns] = piece

    directs, hops = {}, {}
    sent_rows = -(-lev_dev * lat_dev // 8) * 8
    for unit in units:
        direct, relayed = shares(sent_rows)
        ahead = pl.ds(0, direct)
        directs[unit] = remote(part.at[(*unit, ahead)], came.at[(*unit, ahead)], direct_sem.at[unit], other_lon)
        hops[unit] = []
        for i, (start, size) in enumerate(relayed):
            full, held = pl.ds(start, size), pl.ds(start - direct, size)
            hops[unit].append(
                (
                    remote(part.at[(*unit, full)], hop.at[(*unit, held)], hop_sem.at[(*unit, i, 0)], across),
                    remote(hop.at[(*unit, held)], came.at[(*unit, full)], hop_sem.at[(*unit, i, 1)], band),
                )
            )
    relays = [pair for unit in units for pair in hops[unit]]

    def send(unit):
        for out, _ in hops[unit]:
            out.start()
        directs[unit].start()

    def relay(first, last):
        for out, back in relays[first:last]:
            out.wait_recv()
            back.start()

    spec_copies = {unit: remote(spec_put.at[unit], spec_got.at[unit], spec_sem.at[unit], far) for unit in units}

    def spectra_width(chunk):
        return min(CHUNK, spectra_out.shape[3] - chunk * CHUNK)

    column_rows = 2 * BLOCK
    column_copies = [
        remote(
            column_put.at[pl.ds(r, column_rows)], column_got.at[pl.ds(r, column_rows)],
            column_sem.at[r // column_rows], other_lev,
        )
        for r in range(0, pad_rows, column_rows)
    ]

    def make_flux():
        for level in range(lev_dev):
            for r in starts:
                rows, count = kept_rows(r)
                north = acc[lev_dev + level, r : r + BLOCK, :]
                north_out[level, rows, :] = north[0:count, 0:lon_dev]
                flux[level, 8 + r : 8 + r + count, :] = (north * cos_lat[r : r + BLOCK])[0:count]

    def finish_east(levels):
        for level in levels:
            for r in starts:
                at = slice(r, r + BLOCK)
                rows, count = kept_rows(r)
                east = acc[level, at, :]
                east_out[level, rows, :] = east[0:count, 0:lon_dev]
                step = (east_coef[at] * east_diff(east))[0:count, 0:lon_dev]
                thick_out[level, rows, :] = thick_out[level, rows, :] - depth_ref[0:1, level : level + 1] * step

    def finish(some):
        for r in some:
            at = slice(r, r + BLOCK)
            rows, count = kept_rows(r)
            below = None
            for level in range(lev_dev - 1, -1, -1):
                step = flux[level, 9 + r : 9 + r + BLOCK, :] - flux[level, 7 + r : 7 + r + BLOCK, :]
                step = (flux_coef[at] * step)[0:count, 0:lon_dev]
                thick = thick_out[level, rows, :] - depth_ref[0:1, level : level + 1] * step
                below = thick if below is None else below + thick
                thick_out[level, rows, :] = thick
                geo_out[level, rows, :] = sg[rows, :] + GRAVITY * below
            column_put[rows, :] = below
            if (r + BLOCK) % column_rows == 0:

                @pl.when(lev == 1)
                def _():
                    column_copies[r // column_rows].start()

    def deepen():
        @pl.when(lev == 0)
        def _():
            for i, copy in enumerate(column_copies):
                copy.wait_recv()
                for r in range(i * column_rows, (i + 1) * column_rows, BLOCK):
                    rows, _ = kept_rows(r)
                    for level in range(lev_dev):
                        geo_out[level, rows, :] += GRAVITY * column_got[rows, :]

        @pl.when(lev == 1)
        def _():
            for copy in column_copies:
                copy.wait_send()

    @pl.when(polar)
    def _():
        arrive("tables")
        make_basis(0)

    take_geo()
    pl.semaphore_wait(barrier, 5 + inner.astype(jnp.int32))
    send_geo_rows()

    @pl.when(inner)
    def _():
        send_lon(0, geo, 8)
        fetch("rows", "th", "sg")
        arrive("we", "wn")
        from_lon(0, geo, 8)
        from_south(0, geo)
        from_north(0, geo)
        for level in range(lev_dev):
            for r in starts:
                acc[level, r : r + BLOCK, :] = east_rows(level, r)
                acc[lev_dev + level, r : r + BLOCK, :] = north_rows(level, r)
        send_flux_rows()
        send_lon(1, acc, 0)
        make_flux()
        relay(0, 1)
        from_lon(1, acc, 0)
        relay(1, 2)
        arrive("th", "sg")
        done = 2
        for level in range(lev_dev):
            finish_east([level])
            relay(done, done + 1)
            done += 1

        @pl.when(low_side)
        def _():
            from_north(1, flux)

        @pl.when(jnp.logical_not(low_side))
        def _():
            from_south(1, flux)

        for r in range(0, pad_rows, column_rows):
            finish(range(r, r + column_rows, BLOCK))
            relay(done, done + 1)
            done += 1
        relay(done, done + 1)
        deepen()
        relay(done + 1, len(relays))

    @pl.when(polar)
    def _():
        arrive("we", "wn")
        make_terms(0, east_rows)
        forward(0, 0)
        send((0, 0))
        fetch("rows", "th", "sg")
        made = {0}
        for unit in units[1:]:
            chunk, wind = unit
            if chunk not in made:
                make_basis(chunk)
                made.add(chunk)
            if unit == (0, 1):

                @pl.when(low_side)
                def _():
                    from_north(0, geo)

                @pl.when(jnp.logical_not(low_side))
                def _():
                    from_south(0, geo)

                make_terms(1, north_rows)
            forward(chunk, wind)
            send(unit)

        arrive("rows", "sg")
        sides = lax.broadcasted_iota(jnp.int32, table_ref.shape, 0)
        table_ref[...] = jnp.where(sides == 1, -1.0, 0.0)
        for side, here in enumerate((low_side, jnp.logical_not(low_side))):
            columns = slice(side * lat_dev, (side + 1) * lat_dev)

            @pl.when(here)
            def _():
                table_ref[0:1, 0:lat_dev] = kept_ref[:, columns].astype(jnp.float32)
                table_ref[1:2, 0:lat_dev] = slot_ref[:, columns].astype(jnp.float32)

        table = jnp.transpose(table_ref[...])
        kept = table[0:pad_rows, 0:1].astype(jnp.int32)
        slots = table[0:pad_rows, 1:2].astype(jnp.int32)
        place = lax.broadcasted_iota(jnp.int32, (pad_rows, 2 * half_rows), 1)
        own = place >= half_rows
        place = jnp.where(own, place - half_rows, place)
        named = jnp.where(own, lat, partner) * help_rows + place
        match = ((slots == named) & (place < help_rows)).astype(jnp.float32).astype(jnp.bfloat16)
        column = lax.broadcasted_iota(jnp.int32, (pad_rows, 2 * CHUNK), 1)
        local_number = jnp.where(column < CHUNK, column, column - CHUNK)
        odd = 1.0 - 2.0 * lax.rem(local_number[0:1], 2).astype(jnp.float32)
        for chunk, wind in units:
            unit = (chunk, wind)
            number = local_number + chunk * CHUNK
            weight = jnp.where(number == 0, 1.0 / nlon_total, 2.0 / nlon_total)
            directs[unit].wait_recv()
            for _, back in hops[unit]:
                back.wait_recv()
            picked = []
            for level in range(lev_dev):
                rows = slice(level * lat_dev, level * lat_dev + pad_rows)
                sums = (part[chunk, wind, rows, :] + odd * came[chunk, wind, rows, :]) * weight
                sums = jnp.where(number < kept, sums, 0.0)
                high, low = split(sums)
                at = level * pad_rows
                held_sums[wind, at : at + pad_rows, :] = high
                held_sums[wind, stack + at : stack + at + pad_rows, :] = low
                picked.append(jnp.where(lon == 0, sums[:, 0:CHUNK], (sums * odd)[:, CHUNK:]))
            picked = jnp.concatenate(picked, axis=1)
            high = picked.astype(jnp.bfloat16)
            mid, low = split(picked - high.astype(jnp.float32))
            placed = dot(match, high, ((0,), (0,))) + dot(match, mid, ((0,), (0,))) + dot(match, low, ((0,), (0,)))
            for level in range(lev_dev):
                spec_put[chunk, wind, level] = placed[0:half_rows, level * CHUNK : (level + 1) * CHUNK]
            spec_copies[unit].start()
            inverse(chunk, wind)
            if unit == units[-1]:
                send_flux_rows()
                send_fix()
            count = spectra_width(chunk)
            for level in range(lev_dev):
                spectra_out[wind, level, :, chunk * CHUNK : chunk * CHUNK + count] = placed[
                    half_rows : half_rows + help_rows, level * CHUNK : level * CHUNK + count
                ]
            if unit == (chunks - 1, 0):
                arrive("th")
                finish_east(range(lev_dev))

        sent_lat(0)
        make_flux()

        @pl.when(low_side)
        def _():
            from_north(1, flux)

        @pl.when(jnp.logical_not(low_side))
        def _():
            from_south(1, flux)

        finish(starts)
        deepen()
        for unit in units:
            spec_copies[unit].wait_send()
            directs[unit].wait_send()
            for out, _ in hops[unit]:
                out.wait_send()
        sent_lat(1)

        @pl.when(lev == 1)
        def _():
            fix_copy.wait_send()

    @pl.when(inner)
    def _():
        arrive("tables", "rows")
        for chunk, wind in units:
            spec_copies[(chunk, wind)].wait_recv()
            count = spectra_width(chunk)
            for level in range(lev_dev):
                spectra_out[wind, level, :, chunk * CHUNK : chunk * CHUNK + count] = spec_got[
                    chunk, wind, level, 0:help_rows, 0:count
                ]
        for _, back in relays:
            back.wait_send()
        sent_lat(0)
        sent_lat(1)

        def fix(side, row, sign):
            at = slice(row, row + 1)
            coef = sign * flux_coef[at]
            below = None
            for level in range(lev_dev - 1, -1, -1):
                delta = depth_ref[0:1, level : level + 1] * coef * lat_got[1, side, level : level + 1, :]
                below = delta if below is None else below + delta
                thick_out[level, at, :] += delta[:, 0:lon_dev]
                geo_out[level, at, :] += GRAVITY * below[:, 0:lon_dev]

            @pl.when(lev == 0)
            def _():
                fix_copy.wait_recv()
                for level in range(lev_dev):
                    geo_out[level, at, :] += (GRAVITY * coef * fix_got[...])[:, 0:lon_dev]

        @pl.when(low_side)
        def _():
            lat_pair(1)[1].wait_recv()
            fix(0, 0, 1.0)

        @pl.when(jnp.logical_not(low_side))
        def _():
            lat_pair(1)[0].wait_recv()
            fix(1, lat_dev - 1, -1.0)


def hand_on_kernel(*refs):
    half = (len(refs) - 1) // 2
    sems = refs[-1]
    copies = []
    for index, (src, dst) in enumerate(zip(refs[:half], refs[half:-1])):
        levels = src.shape[-3]
        for level in range(levels):
            if len(src.shape) == 3:
                pairs = [(src.at[level], dst.at[:, level, :])]
            else:
                pairs = [(src.at[wind, level], dst.at[wind, :, level, :]) for wind in range(src.shape[0])]
            for wind, (part, place) in enumerate(pairs):
                copies.append(pltpu.make_async_copy(part, place, sems.at[index, wind * levels + level]))
    for copy in copies:
        copy.start()
    for copy in copies:
        copy.wait()


def handed_on(held):
    def shape(x):
        return jax.ShapeDtypeStruct((*x.shape[:-3], x.shape[-2], x.shape[-3], x.shape[-1]), x.dtype)

    return pl.pallas_call(
        hand_on_kernel,
        out_shape=[shape(x) for x in held],
        in_specs=[pl.BlockSpec(memory_space=pltpu.VMEM)] * len(held),
        out_specs=[pl.BlockSpec(memory_space=pl.ANY)] * len(held),
        scratch_shapes=[pltpu.SemaphoreType.DMA((len(held), 2 * held[0].shape[0]))],
        compiler_params=pltpu.CompilerParams(vmem_limit_bytes=4 * 2**20),
    )(*(pltpu.with_memory_space_constraint(x, pltpu.VMEM) for x in held))


def one_kernel(
    wind_east, wind_north, thickness, geopot, surface_geopot, mean_depth, kept_modes, slot_table
):
    lev_dev, lat_dev, lon_dev = thickness.shape
    lat_count = lax.axis_size("lat")
    nlat_total = lat_dev * lat_count
    nlon_total = 2 * lon_dev
    help_rows = lat_dev // 2
    lam_step = 2.0 * math.pi / nlon_total
    phi_step = math.pi / nlat_total
    north_coef = STEP_FACTOR * lam_step / phi_step
    width = -(-(lon_dev + 2) // 512) * 512
    pad_rows = -(-lat_dev // 32) * 32
    half_rows = pad_rows // 2
    chunks = -(-KMAX // CHUNK)
    coarse, fine = angle_tables(width, chunks * CHUNK, nlon_total)
    f32 = jnp.float32
    field = pltpu.VMEM((lev_dev, lat_dev, lon_dev), f32)
    tall = pltpu.VMEM((lev_dev, pad_rows + 16, width), f32)
    groups = 2 * lev_dev
    basis = pltpu.VMEM((chunks, width, 2 * CHUNK), jnp.bfloat16)
    sums = pltpu.VMEM((chunks, 2, lev_dev * pad_rows, 2 * CHUNK), f32)
    sent_rows = -(-lev_dev * lat_dev // 8) * 8
    relayed = sent_rows - shares(sent_rows)[0]
    lat_rows = pltpu.VMEM((2, 2, lev_dev, width), f32)
    lon_rows = pltpu.VMEM((2, 8, 128), f32)
    column = pltpu.VMEM((pad_rows, lon_dev), f32)
    row = pltpu.VMEM((1, width), f32)
    specs = pltpu.VMEM((chunks, 2, lev_dev, half_rows, CHUNK), f32)
    dma = pltpu.SemaphoreType.DMA
    operands = (
        mean_depth.reshape(1, -1),
        kept_modes.reshape(1, -1),
        slot_table.reshape(1, -1),
        jnp.asarray(coarse),
        jnp.asarray(fine),
        *(jnp.transpose(x, (1, 0, 2)) for x in (wind_east, wind_north, thickness, geopot)),
        surface_geopot,
    )
    held = pl.pallas_call(
        functools.partial(substep_kernel, (lat_count, nlon_total, phi_step, north_coef)),
        out_shape=(field,) * 4 + (pltpu.VMEM((2, lev_dev, help_rows, KMAX), f32),),
        in_specs=[pl.BlockSpec(memory_space=pl.ANY)] * len(operands),
        out_specs=(pl.BlockSpec(memory_space=pltpu.VMEM),) * 5,
        scratch_shapes=[
            pltpu.VMEM((1, lev_dev), f32),
            pltpu.VMEM((1, kept_modes.shape[0]), jnp.int32),
            pltpu.VMEM((1, slot_table.shape[0]), jnp.int32),
            pltpu.VMEM(coarse.shape, f32),
            pltpu.VMEM(fine.shape, f32),
            tall,
            pltpu.VMEM((lat_dev, lon_dev), f32),
            pltpu.VMEM((2, 2 * lev_dev * pad_rows, width), jnp.bfloat16),
            basis, basis, sums, sums,
            pltpu.VMEM((chunks, 2, relayed, 2 * CHUNK), f32),
            pltpu.VMEM((2, groups * pad_rows, 2 * CHUNK), jnp.bfloat16),
            pltpu.VMEM((groups, pad_rows, width), f32),
            tall,
            lon_rows, lon_rows, lat_rows, lat_rows, column, column, row, row, specs, specs,
            pltpu.VMEM((8, 128), f32),
            dma((7, 2)), dma((2, 2)), dma((2, 2, 2)), dma((chunks, 2, 2)), dma((chunks, 2, 2, 2, 2)),
            dma((pad_rows // (2 * BLOCK), 2)), dma((2,)), dma((chunks, 2, 2)),
        ],
        compiler_params=pltpu.CompilerParams(
            collective_id=0, has_side_effects=True, vmem_limit_bytes=VMEM_MIB * 2**20
        ),
    )(*(pltpu.with_memory_space_constraint(x, pltpu.HBM) for x in operands))
    *fields, spectra = handed_on(held)
    return (*(jnp.transpose(x, (1, 0, 2)) for x in fields), jnp.transpose(spectra, (0, 2, 1, 3)))


def solution(mesh):
    body = one_kernel if dict(mesh.shape, members=2) == dict(members=2, lat=4, lon=2, lev=2) else local
    return jax.shard_map(
        body,
        mesh=mesh,
        in_specs=(
            P(("members", "lev"), "lat", "lon"),
            P(("members", "lev"), "lat", "lon"),
            P(("members", "lev"), "lat", "lon"),
            P(("members", "lev"), "lat", "lon"),
            P("lat", "lon"),
            P("lev"),
            P(),
            P(),
        ),
        out_specs=(
            P(("members", "lev"), "lat", "lon"),
            P(("members", "lev"), "lat", "lon"),
            P(("members", "lev"), "lat", "lon"),
            P(("members", "lev"), "lat", "lon"),
            P(None, ("members", "lev"), "lat", "lon"),
        ),
        check_vma=False,
    )
```

```python
import math

import functools

import jax
import numpy as np
import jax.numpy as jnp
from jax import lax
from jax.experimental import pallas as pl
from jax.experimental.pallas import tpu as pltpu
from jax.sharding import PartitionSpec as P

KMAX = 360


STEP_FACTOR = 0.15
CORIOLIS = 0.2
GRAVITY = 0.25


def edges(block, axis, dim, periodic):
    count = lax.axis_size(axis)
    first = lax.slice_in_dim(block, 0, 1, axis=dim)
    last = lax.slice_in_dim(block, block.shape[dim] - 1, block.shape[dim], axis=dim)
    if periodic and count == 2:
        both = lax.ppermute(jnp.concatenate([last, first], axis=dim), axis, [(0, 1), (1, 0)])
        return lax.slice_in_dim(both, 0, 1, axis=dim), lax.slice_in_dim(both, 1, 2, axis=dim)
    forward = [(i, i + 1) for i in range(count - 1)]
    if periodic:
        forward.append((count - 1, 0))
    backward = [(target, source) for source, target in forward]
    return lax.ppermute(last, axis, forward), lax.ppermute(first, axis, backward)


def diff(block, low, high, dim):
    size = block.shape[dim]
    up = jnp.concatenate([lax.slice_in_dim(block, 1, size, axis=dim), high], axis=dim)
    down = jnp.concatenate([low, lax.slice_in_dim(block, 0, size - 1, axis=dim)], axis=dim)
    return up - down


def local_basis(count, nlon_total):
    fine = next(f for f in (24, 20, 18, 16, 12, 8, 6, 5, 4, 3, 2, 1) if count % f == 0)
    k = np.arange(KMAX, dtype=np.int64)[None, :]
    angle = 2.0 * np.pi / nlon_total

    def table(columns):
        phase = (columns[:, None] * k % nlon_total) * angle
        return np.cos(phase).astype(np.float32), np.sin(phase).astype(np.float32)

    cc, cs = (jnp.asarray(t)[:, None] for t in table(np.arange(0, count, fine)))
    fc, fs = (jnp.asarray(t)[None] for t in table(np.arange(fine)))
    return (
        (cc * fc - cs * fs).reshape(count, KMAX),
        (cs * fc + cc * fs).reshape(count, KMAX),
    )


def turned(pair, cos_shift, sin_shift):
    cos_part, sin_part = pair[..., :KMAX], pair[..., KMAX:]
    return jnp.concatenate(
        [cos_shift * cos_part - sin_shift * sin_part, sin_shift * cos_part + cos_shift * sin_part],
        axis=-1,
    )


def local(
    wind_east, wind_north, thickness, geopot, surface_geopot, mean_depth, kept_modes, slot_table
):
    lev_dev, lat_dev, lon_dev = thickness.shape
    lat_count = lax.axis_size("lat")
    lon_count = lax.axis_size("lon")
    lev_count = lax.axis_size("lev")
    lat_index = lax.axis_index("lat")
    lon_index = lax.axis_index("lon")
    nlat_total = lat_dev * lat_count
    nlon_total = lon_dev * lon_count
    polar_count = nlat_total // 4
    slot_count = 2 * polar_count
    help_rows = lat_dev // 2
    half_axis = lat_count // 2
    lam_step = 2.0 * math.pi / nlon_total
    phi_step = math.pi / nlat_total
    global_rows = lat_index * lat_dev + jnp.arange(lat_dev, dtype=jnp.int32)
    latitude = -0.5 * math.pi + (global_rows.astype(jnp.float32) + 0.5) * phi_step
    coslat = jnp.cos(latitude)[:, None]
    sinlat = jnp.sin(latitude)[:, None]
    east_coef = STEP_FACTOR / coslat
    north_coef = STEP_FACTOR * lam_step / phi_step
    geo_west, geo_east = edges(geopot, "lon", 2, True)
    geo_south, geo_north = edges(geopot, "lat", 1, False)
    east_new = (
        wind_east
        - east_coef * diff(geopot, geo_west, geo_east, 2)
        + CORIOLIS * sinlat * wind_north
    )
    north_new = (
        wind_north
        - north_coef * diff(geopot, geo_south, geo_north, 1)
        - CORIOLIS * sinlat * wind_east
    )
    is_polar = (lat_index < lat_count // 4) | (lat_index >= lat_count - lat_count // 4)
    first_row = lat_index * lat_dev
    first_rank = jnp.where(lat_index < lat_count // 4, first_row, first_row - (nlat_total - slot_count))
    first_rank = jnp.clip(first_rank, 0, slot_count - lat_dev)
    kept = lax.dynamic_slice(kept_modes, (first_rank,), (lat_dev,))
    slots = lax.dynamic_slice(slot_table, (first_rank,), (lat_dev,))
    wavenumber = jnp.arange(2 * KMAX, dtype=jnp.int32) % KMAX
    weight = (jnp.where(wavenumber == 0, 1.0, 2.0) / nlon_total).astype(jnp.float32)
    factor = jnp.where(wavenumber[None, :] < kept[:, None], weight[None, :], 0.0)
    cos_basis, sin_basis = local_basis(lon_dev, nlon_total)
    basis = jnp.concatenate([cos_basis, sin_basis], axis=1)
    shift = (lon_index * jnp.arange(KMAX, dtype=jnp.int32) % lon_count).astype(jnp.float32)
    shift = shift * (2.0 * math.pi / lon_count)
    if lon_count == 2:
        cos_shift = 1.0 - 2.0 * (lon_index * jnp.arange(KMAX, dtype=jnp.int32) % 2).astype(jnp.float32)
        sin_shift = jnp.zeros_like(cos_shift)
    else:
        cos_shift, sin_shift = jnp.cos(shift), jnp.sin(shift)
    pieces = [wind[level] for level in range(lev_dev) for wind in (east_new, north_new)]
    both_sums = []
    for piece in range(lev_dev):
        rows = jnp.concatenate(pieces[2 * piece : 2 * piece + 2], axis=0)
        part = jnp.dot(rows, basis, precision=lax.Precision.HIGH)
        part = turned(part, cos_shift, sin_shift)
        if lon_count == 2:
            sums = part + lax.ppermute(part, "lon", [(0, 1), (1, 0)])
        else:
            sums = lax.psum(part, "lon")
        both_sums.append(sums.reshape(2, lat_dev, 2 * KMAX) * factor[None])
    filtered = []
    for sums in both_sums:
        turned_back = turned(sums, cos_shift, -sin_shift)
        rows = lax.dot_general(
            turned_back.reshape(2 * lat_dev, 2 * KMAX),
            basis,
            (((1,), (1,)), ((), ())),
            precision=lax.Precision.HIGH,
        )
        filtered.append(rows.reshape(2, lat_dev, lon_dev))
    filtered = jnp.stack(filtered, axis=1)
    east_final = jnp.where(is_polar, filtered[0], east_new)
    north_final = jnp.where(is_polar, filtered[1], north_new)

    slice_width = 2 * KMAX // lon_count
    kept_sums = jnp.stack(both_sums, axis=1)
    own = lax.dynamic_slice_in_dim(kept_sums, lon_index * slice_width, slice_width, 3)
    places = jnp.arange(help_rows, dtype=jnp.int32)
    partner = (lat_index + half_axis) % lat_count

    def rows_named(device):
        match = slots[None, :] == (device * help_rows + places)[:, None]
        return jnp.einsum(
            "sr,abrc->absc", match.astype(jnp.float32), own, precision=lax.Precision.HIGHEST
        )

    route = [((i - half_axis) % lat_count, i) for i in range(lat_count)]
    route = [(s, t) for s, t in route if s < lat_count // 4 or s >= lat_count - lat_count // 4]
    arrived = lax.ppermute(rows_named(partner), "lat", route)
    spectra = jnp.where(is_polar, rows_named(lat_index), arrived)

    rim_west, rim_east = edges(east_final, "lon", 2, True)
    flux = north_final * coslat
    rim_south, rim_north = edges(flux, "lat", 1, False)
    divergence = east_coef * diff(east_final, rim_west, rim_east, 2) + north_coef / coslat * diff(
        flux, rim_south, rim_north, 1
    )
    thick_new = thickness - mean_depth[:, None, None] * divergence
    columns = [thick_new[lev_dev - 1]]
    for level in range(lev_dev - 2, -1, -1):
        columns.append(columns[-1] + thick_new[level])
    columns = columns[::-1]
    deeper = jnp.zeros_like(columns[0])
    for distance in range(1, lev_count):
        deeper = deeper + lax.ppermute(
            columns[0], "lev", [(i + distance, i) for i in range(lev_count - distance)]
        )
    geo_new = surface_geopot[None] + GRAVITY * (jnp.stack(columns) + deeper[None])
    return (east_final, north_final, thick_new, geo_new, spectra)


FINE = 32
VMEM_MIB = 30
CHUNK = 128
BLOCK = 16
DIRECT = 61


def unit_order(chunks):
    last = chunks - 1
    return [(c, w) for w in range(2) for c in range(last)] + [(last, 0), (last, 1)]


def shares(rows):
    direct = rows * DIRECT // 100 // 8 * 8
    first = direct + (rows - direct) // 16 * 8
    return direct, ((direct, first - direct), (first, rows - first))


def angle_tables(width, count, nlon_total):
    k = np.arange(count, dtype=np.int64)[None, :]
    angle = 2.0 * np.pi / nlon_total

    def table(columns):
        phase = (columns[:, None] * k % nlon_total) * angle
        return np.stack([np.cos(phase), np.sin(phase)]).astype(np.float32)

    starts = np.arange(0, width, FINE)
    starts[-1] = -FINE
    return table(starts), table(np.arange(FINE))


def split(x):
    high = x.astype(jnp.bfloat16)
    return high, (x - high.astype(jnp.float32)).astype(jnp.bfloat16)


def dot(a, b, dims):
    return lax.dot_general(a, b, (dims, ((), ())), preferred_element_type=jnp.float32)


def substep_kernel(
    sizes,
    depth_hbm, kept_hbm, slot_hbm, coarse_hbm, fine_hbm,
    we_hbm, wn_hbm, th_hbm, geo_hbm, sg_hbm,
    east_out, north_out, thick_out, geo_out, spectra_out,
    depth_ref, kept_ref, slot_ref, coarse_ref, fine_ref,
    geo, sg,
    xs, high_ref, low_ref, part, came, hop, held_sums, acc, flux,
    lon_put, lon_got, lat_put, lat_got, column_put, column_got, fix_put, fix_got,
    spec_put, spec_got, table_ref,
    in_sem, lon_sem, lat_sem, direct_sem, hop_sem, column_sem, fix_sem, spec_sem,
):
    lat_count, nlon_total, phi_step, north_coef = sizes
    lev_dev, lat_dev, lon_dev = east_out.shape
    help_rows = spectra_out.shape[2]
    _, pad_rows, width = acc.shape
    half_rows = spec_put.shape[-2]
    chunks = high_ref.shape[0]
    units = unit_order(chunks)
    lon = lax.axis_index("lon")
    lat = lax.axis_index("lat")
    lev = lax.axis_index("lev")
    polar = (lat == 0) | (lat == lat_count - 1)
    inner = jnp.logical_not(polar)
    low_side = lat < lat_count // 2
    band = {"lat": lat + 1 - 2 * lax.rem(lat, 2)}
    across = {"lon": 1 - lon, **band}
    aside = {"lev": 1 - lev, **band}
    other_lon = {"lon": 1 - lon}
    other_lev = {"lev": 1 - lev}
    middle = {"lat": lat_count - 1 - lat}
    partner = lax.rem(lat + lat_count // 2, lat_count)
    far = {"lat": partner}
    MESH = pl.DeviceIdType.MESH

    barrier = pltpu.get_barrier_semaphore()
    for target in (other_lon, other_lev, band, across, aside):
        pl.semaphore_signal(barrier, inc=1, device_id=target, device_id_type=MESH)

    @pl.when(inner)
    def _():
        pl.semaphore_signal(barrier, inc=1, device_id=middle, device_id_type=MESH)

    tile = width - 128
    for level in range(lev_dev):
        for ref in (geo, flux):
            start = 8 + lat_dev // 8 * 8
            ref[level, start:, :] = jnp.zeros((ref.shape[1] - start, width), jnp.float32)
            ref[level, 0:8, :] = jnp.zeros((8, width), jnp.float32)
        geo[level, :, tile:] = jnp.zeros((geo.shape[1], 128), jnp.float32)

    def load(src, dst, i, j):
        return pltpu.make_async_copy(src, dst, in_sem.at[i, j])

    def fetch(*names):
        for name in names:
            for copy in loads[name]:
                copy.start()

    loads = {}
    loads["tables"] = [load(coarse_hbm, coarse_ref, 0, 0), load(fine_hbm, fine_ref, 0, 1)]
    for i, (name, src, dst) in enumerate(
        (("geo", geo_hbm, geo_out), ("we", we_hbm, east_out), ("wn", wn_hbm, north_out), ("th", th_hbm, thick_out))
    ):
        for level in range(lev_dev):
            loads[(name, level)] = [load(src.at[:, level, :], dst.at[level], 1 + i, level)]
        loads[name] = [loads[(name, level)][0] for level in range(lev_dev)]
    loads["sg"] = [load(sg_hbm, sg, 5, 0), load(depth_hbm, depth_ref, 5, 1)]
    loads["rows"] = [load(kept_hbm, kept_ref, 6, 0), load(slot_hbm, slot_ref, 6, 1)]

    fetch("tables", *((name, level) for level in range(lev_dev) for name in ("geo", "we", "wn")))

    def arrive(*names):
        for name in names:
            for copy in loads[name]:
                copy.wait()

    def remote(src, dst, sems, target):
        return pltpu.make_async_remote_copy(
            src_ref=src, dst_ref=dst, send_sem=sems.at[0], recv_sem=sems.at[1],
            device_id=target, device_id_type=MESH,
        )

    row_id = lax.broadcasted_iota(jnp.int32, (pad_rows, 1), 0) + lat * lat_dev
    latitude = -0.5 * math.pi + (row_id.astype(jnp.float32) + 0.5) * phi_step
    cos_lat = jnp.cos(latitude)
    sin_lat = jnp.sin(latitude)
    east_coef = STEP_FACTOR / cos_lat
    flux_coef = north_coef / cos_lat
    turn_coef = CORIOLIS * sin_lat
    starts = range(0, pad_rows, BLOCK)

    def east_diff(x):
        return pltpu.roll(x, width - 1, 1) - pltpu.roll(x, 1, 1)

    def kept_rows(r):
        return slice(r, min(r + BLOCK, lat_dev)), min(BLOCK, lat_dev - r)

    def padded(x):
        count = x.shape[0]
        x = jnp.concatenate([x, jnp.zeros((count, width - lon_dev), jnp.float32)], axis=1)
        if count < BLOCK:
            x = jnp.concatenate([x, jnp.zeros((BLOCK - count, width), jnp.float32)], axis=0)
        return x

    def take_geo(levels):
        for level in levels:
            arrive(("geo", level))
            geo[level, 8 : 8 + lat_dev, 0:lon_dev] = geo_out[level]

    def east_rows(level, r):
        at = slice(r, r + BLOCK)
        rows, _ = kept_rows(r)
        winds = east_out[level, rows, :] + turn_coef[rows] * north_out[level, rows, :]
        return padded(winds) - east_coef[at] * east_diff(geo[level, 8 + r : 8 + r + BLOCK, :])

    def north_rows(level, r):
        rows, _ = kept_rows(r)
        winds = north_out[level, rows, :] - turn_coef[rows] * east_out[level, rows, :]
        step = geo[level, 9 + r : 9 + r + BLOCK, :] - geo[level, 7 + r : 7 + r + BLOCK, :]
        return padded(winds) - north_coef * step

    def lat_pair(turn):
        south = remote(lat_put.at[turn, 0], lat_got.at[turn, 1], lat_sem.at[turn, 0], {"lat": lat - 1})
        north = remote(lat_put.at[turn, 1], lat_got.at[turn, 0], lat_sem.at[turn, 1], {"lat": lat + 1})
        return south, north

    has_south = lat > 0
    has_north = lat < lat_count - 1

    def send_lat(turn, firsts, lasts):
        for level in range(lev_dev):
            lat_put[turn, 0, level : level + 1, :] = firsts[level]
            lat_put[turn, 1, level : level + 1, :] = lasts[level]
        south, north = lat_pair(turn)

        @pl.when(has_south)
        def _():
            south.start()

        @pl.when(has_north)
        def _():
            north.start()

    def sent_lat(turn):
        south, north = lat_pair(turn)

        @pl.when(has_south)
        def _():
            south.wait_send()

        @pl.when(has_north)
        def _():
            north.wait_send()

    def from_south(turn, ref):
        lat_pair(turn)[1].wait_recv()
        for level in range(lev_dev):
            ref[level, 7:8, :] = lat_got[turn, 0, level : level + 1, :]

    def from_north(turn, ref):
        lat_pair(turn)[0].wait_recv()
        for level in range(lev_dev):
            ref[level, 8 + lat_dev : 9 + lat_dev, :] = lat_got[turn, 1, level : level + 1, :]

    def send_geo_rows():
        send_lat(
            0,
            [geo[level, 8:9, :] for level in range(lev_dev)],
            [geo[level, 7 + lat_dev : 8 + lat_dev, :] for level in range(lev_dev)],
        )

    def send_flux_rows():
        send_lat(
            1,
            [acc[lev_dev + level, 0:1, :] * cos_lat[0:1] for level in range(lev_dev)],
            [
                acc[lev_dev + level, lat_dev - 1 : lat_dev, :] * cos_lat[lat_dev - 1 : lat_dev]
                for level in range(lev_dev)
            ],
        )

    fix_copy = remote(fix_put, fix_got, fix_sem, aside)

    def send_fix():
        below = None
        for level in range(lev_dev):
            row = jnp.where(low_side, lat_put[1, 1, level : level + 1, :], lat_put[1, 0, level : level + 1, :])
            row = depth_ref[0:1, level : level + 1] * row
            below = row if below is None else below + row
        fix_put[...] = below

        @pl.when(lev == 1)
        def _():
            fix_copy.start()

    edge_lane = lax.broadcasted_iota(jnp.int32, (lat_dev, 128), 1)

    def lon_copy(turn):
        return remote(lon_put.at[turn], lon_got.at[turn], lon_sem.at[turn], other_lon)

    def send_lon(turn, ref, top):
        held = jnp.zeros((lat_dev, 128), jnp.float32)
        for level in range(lev_dev):
            rows = slice(top, top + lat_dev)
            held = jnp.where(edge_lane == 2 * level, ref[level, rows, 0:1], held)
            held = jnp.where(edge_lane == 2 * level + 1, ref[level, rows, lon_dev - 1 : lon_dev], held)
        lon_put[turn, :, 0:lat_dev] = jnp.transpose(held)[0:8]
        lon_copy(turn).start()

    def from_lon(turn, ref, top):
        lon_copy(turn).wait()
        rims = jnp.transpose(lon_got[turn])[0:lat_dev]
        for level in range(lev_dev):
            rows = slice(top, top + lat_dev)
            last = ref[level, rows, tile:]
            last = jnp.where(edge_lane == lon_dev - tile, rims[:, 2 * level : 2 * level + 1], last)
            last = jnp.where(edge_lane == 127, rims[:, 2 * level + 1 : 2 * level + 2], last)
            ref[level, rows, tile:] = last

    def make_basis(chunk):
        at = slice(chunk * CHUNK, (chunk + 1) * CHUNK)

        def body(block, _):
            p = coarse_ref[0, pl.ds(block, 1), :][:, at]
            q = coarse_ref[1, pl.ds(block, 1), :][:, at]
            f, g = fine_ref[0, :, at], fine_ref[1, :, at]
            rows = pl.ds(pl.multiple_of(block * FINE, FINE), FINE)
            for place, values in enumerate((p * f - q * g, q * f + p * g)):
                high, low = split(values)
                high_ref[chunk, rows, place * CHUNK : (place + 1) * CHUNK] = high
                low_ref[chunk, rows, place * CHUNK : (place + 1) * CHUNK] = low
            return _

        lax.fori_loop(0, width // FINE, body, 0)

    stack = lev_dev * pad_rows

    def make_terms(wind, rows, levels):
        for level in levels:
            for r in starts:
                high, low = split(rows(level, r))
                at = level * pad_rows + r
                xs[wind, at : at + BLOCK, :] = high
                xs[wind, stack + at : stack + at + BLOCK, :] = low

    def forward(chunk, wind):
        sums = dot(xs[wind], high_ref[chunk], ((1,), (0,)))
        sums = sums[0:stack] + sums[stack:] + dot(xs[wind, 0:stack, :], low_ref[chunk], ((1,), (0,)))
        for level in range(lev_dev):
            at = level * lat_dev
            part[chunk, wind, at : at + lat_dev, :] = sums[level * pad_rows : level * pad_rows + lat_dev]

    def inverse(chunk, wind):
        for at in range(0, width, 512):
            columns = slice(at, at + 512)
            values = dot(held_sums[wind], high_ref[chunk, columns, :], ((1,), (1,)))
            rest = dot(held_sums[wind, 0:stack, :], low_ref[chunk, columns, :], ((1,), (1,)))
            values = values[0:stack] + values[stack:] + rest
            for level in range(lev_dev):
                group = wind * lev_dev + level
                piece = values[level * pad_rows : (level + 1) * pad_rows]
                if chunk:
                    piece = piece + acc[group, :, columns]
                acc[group, :, columns] = piece

    def first_level(level):
        arrive(("we", level), ("wn", level))
        make_terms(0, east_rows, [level])
        at = level * pad_rows
        high, low = xs[0, at : at + pad_rows, :], xs[0, stack + at : stack + at + pad_rows, :]
        sums = dot(high, high_ref[0], ((1,), (0,))) + dot(low, high_ref[0], ((1,), (0,)))
        sums = sums + dot(high, low_ref[0], ((1,), (0,)))
        part[0, 0, level * lat_dev : (level + 1) * lat_dev, :] = sums[0:lat_dev]

    directs, hops = {}, {}
    sent_rows = -(-lev_dev * lat_dev // 8) * 8
    for unit in units:
        direct, relayed = shares(sent_rows)
        cut = -(-lat_dev // 8) * 8 if unit == units[-1] else lat_dev // 8 * 8
        parts = ((0, cut), (cut, direct)) if unit in (units[0], units[-1]) and cut < direct else ((0, direct),)
        directs[unit] = []
        for i, (start, end) in enumerate(parts):
            at = (*unit, pl.ds(start, end - start))
            directs[unit].append(remote(part.at[at], came.at[at], direct_sem.at[(*unit, i)], other_lon))
        hops[unit] = []
        for i, (start, size) in enumerate(relayed):
            full, held = pl.ds(start, size), pl.ds(start - direct, size)
            hops[unit].append(
                (
                    remote(part.at[(*unit, full)], hop.at[(*unit, held)], hop_sem.at[(*unit, i, 0)], across),
                    remote(hop.at[(*unit, held)], came.at[(*unit, full)], hop_sem.at[(*unit, i, 1)], band),
                )
            )
    relays = [pair for unit in units for pair in hops[unit]]

    def send(unit):
        for out, _ in hops[unit]:
            out.start()
        for copy in directs[unit][1:] if unit == units[0] else directs[unit]:
            copy.start()

    def relay(first, last):
        for out, back in relays[first:last]:
            out.wait_recv()
            back.start()

    spec_copies = {}
    for unit in units:
        for level in range(lev_dev):
            at = (*unit, level)
            spec_copies[at] = remote(spec_put.at[at], spec_got.at[at], spec_sem.at[at], far)

    def spectra_width(chunk):
        return min(CHUNK, spectra_out.shape[3] - chunk * CHUNK)

    column_rows = 2 * BLOCK
    column_copies = [
        remote(
            column_put.at[pl.ds(r, column_rows)], column_got.at[pl.ds(r, column_rows)],
            column_sem.at[r // column_rows], other_lev,
        )
        for r in range(0, pad_rows, column_rows)
    ]

    def make_flux():
        for level in range(lev_dev):
            for r in starts:
                rows, count = kept_rows(r)
                north = acc[lev_dev + level, r : r + BLOCK, :]
                north_out[level, rows, :] = north[0:count, 0:lon_dev]
                flux[level, 8 + r : 8 + r + count, :] = (north * cos_lat[r : r + BLOCK])[0:count]

    def finish_east(levels):
        for level in levels:
            for r in starts:
                at = slice(r, r + BLOCK)
                rows, count = kept_rows(r)
                east = acc[level, at, :]
                east_out[level, rows, :] = east[0:count, 0:lon_dev]
                step = (east_coef[at] * east_diff(east))[0:count, 0:lon_dev]
                thick_out[level, rows, :] = thick_out[level, rows, :] - depth_ref[0:1, level : level + 1] * step

    def finish(some):
        for r in some:
            at = slice(r, r + BLOCK)
            rows, count = kept_rows(r)
            below = None
            for level in range(lev_dev - 1, -1, -1):
                step = flux[level, 9 + r : 9 + r + BLOCK, :] - flux[level, 7 + r : 7 + r + BLOCK, :]
                step = (flux_coef[at] * step)[0:count, 0:lon_dev]
                thick = thick_out[level, rows, :] - depth_ref[0:1, level : level + 1] * step
                below = thick if below is None else below + thick
                thick_out[level, rows, :] = thick
                geo_out[level, rows, :] = sg[rows, :] + GRAVITY * below
            column_put[rows, :] = below
            if (r + BLOCK) % column_rows == 0:

                @pl.when(lev == 1)
                def _():
                    column_copies[r // column_rows].start()

    def deepen():
        @pl.when(lev == 0)
        def _():
            for i, copy in enumerate(column_copies):
                copy.wait_recv()
                for r in range(i * column_rows, (i + 1) * column_rows, BLOCK):
                    rows, _ = kept_rows(r)
                    for level in range(lev_dev):
                        geo_out[level, rows, :] += GRAVITY * column_got[rows, :]

        @pl.when(lev == 1)
        def _():
            for copy in column_copies:
                copy.wait_send()

    @pl.when(polar)
    def _():
        arrive("tables")
        make_basis(0)
        take_geo([0])
        first_level(0)

    @pl.when(inner)
    def _():
        take_geo([0])

    pl.semaphore_wait(barrier, 5 + inner.astype(jnp.int32))

    @pl.when(polar)
    def _():
        directs[units[0]][0].start()

    take_geo(range(1, lev_dev))
    send_geo_rows()

    @pl.when(inner)
    def _():
        send_lon(0, geo, 8)
        fetch("rows", "th", "sg")
        arrive("we", "wn")
        from_lon(0, geo, 8)
        from_south(0, geo)
        from_north(0, geo)
        for level in range(lev_dev):
            for r in starts:
                acc[level, r : r + BLOCK, :] = east_rows(level, r)
                acc[lev_dev + level, r : r + BLOCK, :] = north_rows(level, r)
        send_flux_rows()
        send_lon(1, acc, 0)
        relay(0, 1)
        make_flux()
        relay(1, 3)
        from_lon(1, acc, 0)
        relay(3, 4)

        @pl.when(low_side)
        def _():
            from_north(1, flux)

        @pl.when(jnp.logical_not(low_side))
        def _():
            from_south(1, flux)

        arrive("th", "sg")
        done = 4
        for level in range(lev_dev):
            finish_east([level])
            relay(done, done + 1)
            done += 1
        for r in range(0, pad_rows, column_rows):
            finish(range(r, r + column_rows, BLOCK))
            relay(done, done + 1)
            done += 1
        relay(done, len(relays))
        deepen()

    @pl.when(polar)
    def _():
        for level in range(1, lev_dev):
            first_level(level)
        send((0, 0))
        fetch("rows", "th", "sg")
        made = {0}
        for unit in units[1:]:
            chunk, wind = unit
            if chunk not in made:
                make_basis(chunk)
                made.add(chunk)
            if unit == (0, 1):

                @pl.when(low_side)
                def _():
                    from_north(0, geo)

                @pl.when(jnp.logical_not(low_side))
                def _():
                    from_south(0, geo)

                make_terms(1, north_rows, range(lev_dev))
            forward(chunk, wind)
            send(unit)

        arrive("rows", "sg")
        sides = lax.broadcasted_iota(jnp.int32, table_ref.shape, 0)
        table_ref[...] = jnp.where(sides == 1, -1.0, 0.0)
        for side, here in enumerate((low_side, jnp.logical_not(low_side))):
            columns = slice(side * lat_dev, (side + 1) * lat_dev)

            @pl.when(here)
            def _():
                table_ref[0:1, 0:lat_dev] = kept_ref[:, columns].astype(jnp.float32)
                table_ref[1:2, 0:lat_dev] = slot_ref[:, columns].astype(jnp.float32)

        table = jnp.transpose(table_ref[...])
        kept = table[0:pad_rows, 0:1].astype(jnp.int32)
        slots = table[0:pad_rows, 1:2].astype(jnp.int32)
        place = lax.broadcasted_iota(jnp.int32, (pad_rows, 2 * half_rows), 1)
        own = place >= half_rows
        place = jnp.where(own, place - half_rows, place)
        named = jnp.where(own, lat, partner) * help_rows + place
        match = ((slots == named) & (place < help_rows)).astype(jnp.float32).astype(jnp.bfloat16)
        column = lax.broadcasted_iota(jnp.int32, (pad_rows, 2 * CHUNK), 1)
        local_number = jnp.where(column < CHUNK, column, column - CHUNK)
        odd = 1.0 - 2.0 * lax.rem(local_number[0:1], 2).astype(jnp.float32)
        for chunk, wind in units:
            unit = (chunk, wind)
            number = local_number + chunk * CHUNK
            weight = jnp.where(number == 0, 1.0 / nlon_total, 2.0 / nlon_total)
            waits = [copy.wait_recv for copy in directs[unit]] + [back.wait_recv for _, back in hops[unit]]
            ready = 1 if unit == units[-1] and len(directs[unit]) > 1 else len(waits)
            for wait in waits[:ready]:
                wait()
            whole = [list(range(lev_dev))]
            placed = []
            for levels in [[level] for level in range(lev_dev)] if unit == units[-1] else whole:
                picked = []
                if levels[0] > 0:
                    for wait in waits[ready:]:
                        wait()
                for level in levels:
                    rows = slice(level * lat_dev, level * lat_dev + pad_rows)
                    sums = (part[chunk, wind, rows, :] + odd * came[chunk, wind, rows, :]) * weight
                    sums = jnp.where(number < kept, sums, 0.0)
                    high, low = split(sums)
                    at = level * pad_rows
                    held_sums[wind, at : at + pad_rows, :] = high
                    held_sums[wind, stack + at : stack + at + pad_rows, :] = low
                    picked.append(jnp.where(lon == 0, sums[:, 0:CHUNK], (sums * odd)[:, CHUNK:]))
                picked = jnp.concatenate(picked, axis=1)
                high = picked.astype(jnp.bfloat16)
                mid, low = split(picked - high.astype(jnp.float32))
                both = dot(match, high, ((0,), (0,))) + dot(match, mid, ((0,), (0,))) + dot(match, low, ((0,), (0,)))
                for i, level in enumerate(levels):
                    placed.append(both[:, i * CHUNK : (i + 1) * CHUNK])
                    spec_put[chunk, wind, level] = placed[level][0:half_rows]
                    spec_copies[(chunk, wind, level)].start()
            inverse(chunk, wind)
            if unit == units[-1]:
                send_flux_rows()
                send_fix()
            count = spectra_width(chunk)
            for level in range(lev_dev):
                spectra_out[wind, level, :, chunk * CHUNK : chunk * CHUNK + count] = placed[level][
                    half_rows : half_rows + help_rows, 0:count
                ]
            if unit == (chunks - 1, 0):
                arrive("th")
                finish_east(range(lev_dev))

        sent_lat(0)
        make_flux()

        @pl.when(low_side)
        def _():
            from_north(1, flux)

        @pl.when(jnp.logical_not(low_side))
        def _():
            from_south(1, flux)

        finish(starts)
        deepen()
        for unit in units:
            for level in range(lev_dev):
                spec_copies[(*unit, level)].wait_send()
            for copy in directs[unit]:
                copy.wait_send()
            for out, _ in hops[unit]:
                out.wait_send()
        sent_lat(1)

        @pl.when(lev == 1)
        def _():
            fix_copy.wait_send()

    @pl.when(inner)
    def _():
        arrive("tables", "rows")
        for chunk, wind in units:
            count = spectra_width(chunk)
            for level in range(lev_dev):
                spec_copies[(chunk, wind, level)].wait_recv()
                spectra_out[wind, level, :, chunk * CHUNK : chunk * CHUNK + count] = spec_got[
                    chunk, wind, level, 0:help_rows, 0:count
                ]
        for _, back in relays:
            back.wait_send()
        sent_lat(0)
        sent_lat(1)

        def fix(side, row, sign):
            at = slice(row, row + 1)
            coef = sign * flux_coef[at]
            below = None
            for level in range(lev_dev - 1, -1, -1):
                delta = depth_ref[0:1, level : level + 1] * coef * lat_got[1, side, level : level + 1, :]
                below = delta if below is None else below + delta
                thick_out[level, at, :] += delta[:, 0:lon_dev]
                geo_out[level, at, :] += GRAVITY * below[:, 0:lon_dev]

            @pl.when(lev == 0)
            def _():
                fix_copy.wait_recv()
                for level in range(lev_dev):
                    geo_out[level, at, :] += (GRAVITY * coef * fix_got[...])[:, 0:lon_dev]

        @pl.when(low_side)
        def _():
            lat_pair(1)[1].wait_recv()
            fix(0, 0, 1.0)

        @pl.when(jnp.logical_not(low_side))
        def _():
            lat_pair(1)[0].wait_recv()
            fix(1, lat_dev - 1, -1.0)


def hand_on_kernel(*refs):
    half = (len(refs) - 1) // 2
    sems = refs[-1]
    copies = []
    for index, (src, dst) in enumerate(zip(refs[:half], refs[half:-1])):
        levels = src.shape[-3]
        for level in range(levels):
            if len(src.shape) == 3:
                pairs = [(src.at[level], dst.at[:, level, :])]
            else:
                pairs = [(src.at[wind, level], dst.at[wind, :, level, :]) for wind in range(src.shape[0])]
            for wind, (part, place) in enumerate(pairs):
                copies.append(pltpu.make_async_copy(part, place, sems.at[index, wind * levels + level]))
    for copy in copies:
        copy.start()
    for copy in copies:
        copy.wait()


def handed_on(held):
    def shape(x):
        return jax.ShapeDtypeStruct((*x.shape[:-3], x.shape[-2], x.shape[-3], x.shape[-1]), x.dtype)

    return pl.pallas_call(
        hand_on_kernel,
        out_shape=[shape(x) for x in held],
        in_specs=[pl.BlockSpec(memory_space=pltpu.VMEM)] * len(held),
        out_specs=[pl.BlockSpec(memory_space=pl.ANY)] * len(held),
        scratch_shapes=[pltpu.SemaphoreType.DMA((len(held), 2 * held[0].shape[0]))],
        compiler_params=pltpu.CompilerParams(vmem_limit_bytes=4 * 2**20),
    )(*(pltpu.with_memory_space_constraint(x, pltpu.VMEM) for x in held))


def one_kernel(
    wind_east, wind_north, thickness, geopot, surface_geopot, mean_depth, kept_modes, slot_table
):
    lev_dev, lat_dev, lon_dev = thickness.shape
    lat_count = lax.axis_size("lat")
    nlat_total = lat_dev * lat_count
    nlon_total = 2 * lon_dev
    help_rows = lat_dev // 2
    lam_step = 2.0 * math.pi / nlon_total
    phi_step = math.pi / nlat_total
    north_coef = STEP_FACTOR * lam_step / phi_step
    width = -(-(lon_dev + 2) // 512) * 512
    pad_rows = -(-lat_dev // 32) * 32
    half_rows = pad_rows // 2
    chunks = -(-KMAX // CHUNK)
    coarse, fine = angle_tables(width, chunks * CHUNK, nlon_total)
    f32 = jnp.float32
    field = pltpu.VMEM((lev_dev, lat_dev, lon_dev), f32)
    tall = pltpu.VMEM((lev_dev, pad_rows + 16, width), f32)
    groups = 2 * lev_dev
    basis = pltpu.VMEM((chunks, width, 2 * CHUNK), jnp.bfloat16)
    sums = pltpu.VMEM((chunks, 2, lev_dev * pad_rows, 2 * CHUNK), f32)
    sent_rows = -(-lev_dev * lat_dev // 8) * 8
    relayed = sent_rows - shares(sent_rows)[0]
    lat_rows = pltpu.VMEM((2, 2, lev_dev, width), f32)
    lon_rows = pltpu.VMEM((2, 8, 128), f32)
    column = pltpu.VMEM((pad_rows, lon_dev), f32)
    row = pltpu.VMEM((1, width), f32)
    specs = pltpu.VMEM((chunks, 2, lev_dev, half_rows, CHUNK), f32)
    dma = pltpu.SemaphoreType.DMA
    operands = (
        mean_depth.reshape(1, -1),
        kept_modes.reshape(1, -1),
        slot_table.reshape(1, -1),
        jnp.asarray(coarse),
        jnp.asarray(fine),
        *(jnp.transpose(x, (1, 0, 2)) for x in (wind_east, wind_north, thickness, geopot)),
        surface_geopot,
    )
    held = pl.pallas_call(
        functools.partial(substep_kernel, (lat_count, nlon_total, phi_step, north_coef)),
        out_shape=(field,) * 4 + (pltpu.VMEM((2, lev_dev, help_rows, KMAX), f32),),
        in_specs=[pl.BlockSpec(memory_space=pl.ANY)] * len(operands),
        out_specs=(pl.BlockSpec(memory_space=pltpu.VMEM),) * 5,
        scratch_shapes=[
            pltpu.VMEM((1, lev_dev), f32),
            pltpu.VMEM((1, kept_modes.shape[0]), jnp.int32),
            pltpu.VMEM((1, slot_table.shape[0]), jnp.int32),
            pltpu.VMEM(coarse.shape, f32),
            pltpu.VMEM(fine.shape, f32),
            tall,
            pltpu.VMEM((lat_dev, lon_dev), f32),
            pltpu.VMEM((2, 2 * lev_dev * pad_rows, width), jnp.bfloat16),
            basis, basis, sums, sums,
            pltpu.VMEM((chunks, 2, relayed, 2 * CHUNK), f32),
            pltpu.VMEM((2, groups * pad_rows, 2 * CHUNK), jnp.bfloat16),
            pltpu.VMEM((groups, pad_rows, width), f32),
            tall,
            lon_rows, lon_rows, lat_rows, lat_rows, column, column, row, row, specs, specs,
            pltpu.VMEM((8, 128), f32),
            dma((7, 2)), dma((2, 2)), dma((2, 2, 2)), dma((chunks, 2, 2, 2)), dma((chunks, 2, 2, 2, 2)),
            dma((pad_rows // (2 * BLOCK), 2)), dma((2,)), dma((chunks, 2, lev_dev, 2)),
        ],
        compiler_params=pltpu.CompilerParams(
            collective_id=0, has_side_effects=True, vmem_limit_bytes=VMEM_MIB * 2**20
        ),
    )(*(pltpu.with_memory_space_constraint(x, pltpu.HBM) for x in operands))
    *fields, spectra = handed_on(held)
    return (*(jnp.transpose(x, (1, 0, 2)) for x in fields), jnp.transpose(spectra, (0, 2, 1, 3)))


def solution(mesh):
    body = one_kernel if dict(mesh.shape, members=2) == dict(members=2, lat=4, lon=2, lev=2) else local
    return jax.shard_map(
        body,
        mesh=mesh,
        in_specs=(
            P(("members", "lev"), "lat", "lon"),
            P(("members", "lev"), "lat", "lon"),
            P(("members", "lev"), "lat", "lon"),
            P(("members", "lev"), "lat", "lon"),
            P("lat", "lon"),
            P("lev"),
            P(),
            P(),
        ),
        out_specs=(
            P(("members", "lev"), "lat", "lon"),
            P(("members", "lev"), "lat", "lon"),
            P(("members", "lev"), "lat", "lon"),
            P(("members", "lev"), "lat", "lon"),
            P(None, ("members", "lev"), "lat", "lon"),
        ),
        check_vma=False,
    )
```

```python
import math

import functools

import jax
import numpy as np
import jax.numpy as jnp
from jax import lax
from jax.experimental import pallas as pl
from jax.experimental.pallas import tpu as pltpu
from jax.sharding import PartitionSpec as P

KMAX = 360


STEP_FACTOR = 0.15
CORIOLIS = 0.2
GRAVITY = 0.25


def edges(block, axis, dim, periodic):
    count = lax.axis_size(axis)
    first = lax.slice_in_dim(block, 0, 1, axis=dim)
    last = lax.slice_in_dim(block, block.shape[dim] - 1, block.shape[dim], axis=dim)
    if periodic and count == 2:
        both = lax.ppermute(jnp.concatenate([last, first], axis=dim), axis, [(0, 1), (1, 0)])
        return lax.slice_in_dim(both, 0, 1, axis=dim), lax.slice_in_dim(both, 1, 2, axis=dim)
    forward = [(i, i + 1) for i in range(count - 1)]
    if periodic:
        forward.append((count - 1, 0))
    backward = [(target, source) for source, target in forward]
    return lax.ppermute(last, axis, forward), lax.ppermute(first, axis, backward)


def diff(block, low, high, dim):
    size = block.shape[dim]
    up = jnp.concatenate([lax.slice_in_dim(block, 1, size, axis=dim), high], axis=dim)
    down = jnp.concatenate([low, lax.slice_in_dim(block, 0, size - 1, axis=dim)], axis=dim)
    return up - down


def local_basis(count, nlon_total):
    fine = next(f for f in (24, 20, 18, 16, 12, 8, 6, 5, 4, 3, 2, 1) if count % f == 0)
    k = np.arange(KMAX, dtype=np.int64)[None, :]
    angle = 2.0 * np.pi / nlon_total

    def table(columns):
        phase = (columns[:, None] * k % nlon_total) * angle
        return np.cos(phase).astype(np.float32), np.sin(phase).astype(np.float32)

    cc, cs = (jnp.asarray(t)[:, None] for t in table(np.arange(0, count, fine)))
    fc, fs = (jnp.asarray(t)[None] for t in table(np.arange(fine)))
    return (
        (cc * fc - cs * fs).reshape(count, KMAX),
        (cs * fc + cc * fs).reshape(count, KMAX),
    )


def turned(pair, cos_shift, sin_shift):
    cos_part, sin_part = pair[..., :KMAX], pair[..., KMAX:]
    return jnp.concatenate(
        [cos_shift * cos_part - sin_shift * sin_part, sin_shift * cos_part + cos_shift * sin_part],
        axis=-1,
    )


def local(
    wind_east, wind_north, thickness, geopot, surface_geopot, mean_depth, kept_modes, slot_table
):
    lev_dev, lat_dev, lon_dev = thickness.shape
    lat_count = lax.axis_size("lat")
    lon_count = lax.axis_size("lon")
    lev_count = lax.axis_size("lev")
    lat_index = lax.axis_index("lat")
    lon_index = lax.axis_index("lon")
    nlat_total = lat_dev * lat_count
    nlon_total = lon_dev * lon_count
    polar_count = nlat_total // 4
    slot_count = 2 * polar_count
    help_rows = lat_dev // 2
    half_axis = lat_count // 2
    lam_step = 2.0 * math.pi / nlon_total
    phi_step = math.pi / nlat_total
    global_rows = lat_index * lat_dev + jnp.arange(lat_dev, dtype=jnp.int32)
    latitude = -0.5 * math.pi + (global_rows.astype(jnp.float32) + 0.5) * phi_step
    coslat = jnp.cos(latitude)[:, None]
    sinlat = jnp.sin(latitude)[:, None]
    east_coef = STEP_FACTOR / coslat
    north_coef = STEP_FACTOR * lam_step / phi_step
    geo_west, geo_east = edges(geopot, "lon", 2, True)
    geo_south, geo_north = edges(geopot, "lat", 1, False)
    east_new = (
        wind_east
        - east_coef * diff(geopot, geo_west, geo_east, 2)
        + CORIOLIS * sinlat * wind_north
    )
    north_new = (
        wind_north
        - north_coef * diff(geopot, geo_south, geo_north, 1)
        - CORIOLIS * sinlat * wind_east
    )
    is_polar = (lat_index < lat_count // 4) | (lat_index >= lat_count - lat_count // 4)
    first_row = lat_index * lat_dev
    first_rank = jnp.where(lat_index < lat_count // 4, first_row, first_row - (nlat_total - slot_count))
    first_rank = jnp.clip(first_rank, 0, slot_count - lat_dev)
    kept = lax.dynamic_slice(kept_modes, (first_rank,), (lat_dev,))
    slots = lax.dynamic_slice(slot_table, (first_rank,), (lat_dev,))
    wavenumber = jnp.arange(2 * KMAX, dtype=jnp.int32) % KMAX
    weight = (jnp.where(wavenumber == 0, 1.0, 2.0) / nlon_total).astype(jnp.float32)
    factor = jnp.where(wavenumber[None, :] < kept[:, None], weight[None, :], 0.0)
    cos_basis, sin_basis = local_basis(lon_dev, nlon_total)
    basis = jnp.concatenate([cos_basis, sin_basis], axis=1)
    shift = (lon_index * jnp.arange(KMAX, dtype=jnp.int32) % lon_count).astype(jnp.float32)
    shift = shift * (2.0 * math.pi / lon_count)
    if lon_count == 2:
        cos_shift = 1.0 - 2.0 * (lon_index * jnp.arange(KMAX, dtype=jnp.int32) % 2).astype(jnp.float32)
        sin_shift = jnp.zeros_like(cos_shift)
    else:
        cos_shift, sin_shift = jnp.cos(shift), jnp.sin(shift)
    pieces = [wind[level] for level in range(lev_dev) for wind in (east_new, north_new)]
    both_sums = []
    for piece in range(lev_dev):
        rows = jnp.concatenate(pieces[2 * piece : 2 * piece + 2], axis=0)
        part = jnp.dot(rows, basis, precision=lax.Precision.HIGH)
        part = turned(part, cos_shift, sin_shift)
        if lon_count == 2:
            sums = part + lax.ppermute(part, "lon", [(0, 1), (1, 0)])
        else:
            sums = lax.psum(part, "lon")
        both_sums.append(sums.reshape(2, lat_dev, 2 * KMAX) * factor[None])
    filtered = []
    for sums in both_sums:
        turned_back = turned(sums, cos_shift, -sin_shift)
        rows = lax.dot_general(
            turned_back.reshape(2 * lat_dev, 2 * KMAX),
            basis,
            (((1,), (1,)), ((), ())),
            precision=lax.Precision.HIGH,
        )
        filtered.append(rows.reshape(2, lat_dev, lon_dev))
    filtered = jnp.stack(filtered, axis=1)
    east_final = jnp.where(is_polar, filtered[0], east_new)
    north_final = jnp.where(is_polar, filtered[1], north_new)

    slice_width = 2 * KMAX // lon_count
    kept_sums = jnp.stack(both_sums, axis=1)
    own = lax.dynamic_slice_in_dim(kept_sums, lon_index * slice_width, slice_width, 3)
    places = jnp.arange(help_rows, dtype=jnp.int32)
    partner = (lat_index + half_axis) % lat_count

    def rows_named(device):
        match = slots[None, :] == (device * help_rows + places)[:, None]
        return jnp.einsum(
            "sr,abrc->absc", match.astype(jnp.float32), own, precision=lax.Precision.HIGHEST
        )

    route = [((i - half_axis) % lat_count, i) for i in range(lat_count)]
    route = [(s, t) for s, t in route if s < lat_count // 4 or s >= lat_count - lat_count // 4]
    arrived = lax.ppermute(rows_named(partner), "lat", route)
    spectra = jnp.where(is_polar, rows_named(lat_index), arrived)

    rim_west, rim_east = edges(east_final, "lon", 2, True)
    flux = north_final * coslat
    rim_south, rim_north = edges(flux, "lat", 1, False)
    divergence = east_coef * diff(east_final, rim_west, rim_east, 2) + north_coef / coslat * diff(
        flux, rim_south, rim_north, 1
    )
    thick_new = thickness - mean_depth[:, None, None] * divergence
    columns = [thick_new[lev_dev - 1]]
    for level in range(lev_dev - 2, -1, -1):
        columns.append(columns[-1] + thick_new[level])
    columns = columns[::-1]
    deeper = jnp.zeros_like(columns[0])
    for distance in range(1, lev_count):
        deeper = deeper + lax.ppermute(
            columns[0], "lev", [(i + distance, i) for i in range(lev_count - distance)]
        )
    geo_new = surface_geopot[None] + GRAVITY * (jnp.stack(columns) + deeper[None])
    return (east_final, north_final, thick_new, geo_new, spectra)


FINE = 32
VMEM_MIB = 30
CHUNK = 128
BLOCK = 16
DIRECT = 61
EXTRA = 8


def unit_order(chunks):
    last = chunks - 1
    return [(c, w) for w in range(2) for c in range(last)] + [(last, 0), (last, 1)]


def shares(rows, extra=0):
    direct = rows * DIRECT // 100 // 8 * 8 + extra
    first = direct + (rows - direct) // 16 * 8
    return direct, ((direct, first - direct), (first, rows - first))


def angle_tables(width, count, nlon_total):
    k = np.arange(count, dtype=np.int64)[None, :]
    angle = 2.0 * np.pi / nlon_total

    def table(columns):
        phase = (columns[:, None] * k % nlon_total) * angle
        return np.stack([np.cos(phase), np.sin(phase)]).astype(np.float32)

    starts = np.arange(0, width, FINE)
    starts[-1] = -FINE
    return table(starts), table(np.arange(FINE))


def split(x):
    high = x.astype(jnp.bfloat16)
    return high, (x - high.astype(jnp.float32)).astype(jnp.bfloat16)


def dot(a, b, dims):
    return lax.dot_general(a, b, (dims, ((), ())), preferred_element_type=jnp.float32)


def substep_kernel(
    sizes,
    depth_hbm, kept_hbm, slot_hbm, coarse_hbm, fine_hbm,
    we_hbm, wn_hbm, th_hbm, geo_hbm, sg_hbm,
    east_out, north_out, thick_out, geo_out, spectra_out,
    depth_ref, kept_ref, slot_ref, coarse_ref, fine_ref,
    geo, sg,
    xs, high_ref, low_ref, part, came, hop, held_sums, acc, flux,
    lon_put, lon_got, lat_put, lat_got, column_put, column_got, fix_put, fix_got,
    spec_put, spec_got, table_ref,
    in_sem, lon_sem, lat_sem, direct_sem, hop_sem, column_sem, fix_sem, spec_sem,
):
    lat_count, nlon_total, phi_step, north_coef = sizes
    lev_dev, lat_dev, lon_dev = east_out.shape
    help_rows = spectra_out.shape[2]
    _, pad_rows, width = acc.shape
    half_rows = spec_put.shape[-2]
    chunks = high_ref.shape[0]
    units = unit_order(chunks)
    lon = lax.axis_index("lon")
    lat = lax.axis_index("lat")
    lev = lax.axis_index("lev")
    polar = (lat == 0) | (lat == lat_count - 1)
    inner = jnp.logical_not(polar)
    low_side = lat < lat_count // 2
    band = {"lat": lat + 1 - 2 * lax.rem(lat, 2)}
    across = {"lon": 1 - lon, **band}
    aside = {"lev": 1 - lev, **band}
    other_lon = {"lon": 1 - lon}
    other_lev = {"lev": 1 - lev}
    middle = {"lat": lat_count - 1 - lat}
    partner = lax.rem(lat + lat_count // 2, lat_count)
    far = {"lat": partner}
    MESH = pl.DeviceIdType.MESH

    barrier = pltpu.get_barrier_semaphore()
    for target in (other_lon, other_lev, band, across, aside):
        pl.semaphore_signal(barrier, inc=1, device_id=target, device_id_type=MESH)

    @pl.when(inner)
    def _():
        pl.semaphore_signal(barrier, inc=1, device_id=middle, device_id_type=MESH)

    tile = width - 128
    for level in range(lev_dev):
        for ref in (geo, flux):
            start = 8 + lat_dev // 8 * 8
            ref[level, start:, :] = jnp.zeros((ref.shape[1] - start, width), jnp.float32)
            ref[level, 0:8, :] = jnp.zeros((8, width), jnp.float32)
        geo[level, :, tile:] = jnp.zeros((geo.shape[1], 128), jnp.float32)

    def load(src, dst, i, j):
        return pltpu.make_async_copy(src, dst, in_sem.at[i, j])

    def fetch(*names):
        for name in names:
            for copy in loads[name]:
                copy.start()

    loads = {}
    loads["tables"] = [load(coarse_hbm, coarse_ref, 0, 0), load(fine_hbm, fine_ref, 0, 1)]
    for i, (name, src, dst) in enumerate(
        (("geo", geo_hbm, geo_out), ("we", we_hbm, east_out), ("wn", wn_hbm, north_out), ("th", th_hbm, thick_out))
    ):
        for level in range(lev_dev):
            loads[(name, level)] = [load(src.at[:, level, :], dst.at[level], 1 + i, level)]
        loads[name] = [loads[(name, level)][0] for level in range(lev_dev)]
    loads["sg"] = [load(sg_hbm, sg, 5, 0), load(depth_hbm, depth_ref, 5, 1)]
    loads["rows"] = [load(kept_hbm, kept_ref, 6, 0), load(slot_hbm, slot_ref, 6, 1)]

    fetch("tables", *((name, level) for level in range(lev_dev) for name in ("geo", "we", "wn")))

    def arrive(*names):
        for name in names:
            for copy in loads[name]:
                copy.wait()

    def remote(src, dst, sems, target):
        return pltpu.make_async_remote_copy(
            src_ref=src, dst_ref=dst, send_sem=sems.at[0], recv_sem=sems.at[1],
            device_id=target, device_id_type=MESH,
        )

    row_id = lax.broadcasted_iota(jnp.int32, (pad_rows, 1), 0) + lat * lat_dev
    latitude = -0.5 * math.pi + (row_id.astype(jnp.float32) + 0.5) * phi_step
    cos_lat = jnp.cos(latitude)
    sin_lat = jnp.sin(latitude)
    east_coef = STEP_FACTOR / cos_lat
    flux_coef = north_coef / cos_lat
    turn_coef = CORIOLIS * sin_lat
    starts = range(0, pad_rows, BLOCK)

    def east_diff(x):
        return pltpu.roll(x, width - 1, 1) - pltpu.roll(x, 1, 1)

    def kept_rows(r):
        return slice(r, min(r + BLOCK, lat_dev)), min(BLOCK, lat_dev - r)

    def padded(x):
        count = x.shape[0]
        x = jnp.concatenate([x, jnp.zeros((count, width - lon_dev), jnp.float32)], axis=1)
        if count < BLOCK:
            x = jnp.concatenate([x, jnp.zeros((BLOCK - count, width), jnp.float32)], axis=0)
        return x

    def take_geo(levels):
        for level in levels:
            arrive(("geo", level))
            geo[level, 8 : 8 + lat_dev, 0:lon_dev] = geo_out[level]

    def east_rows(level, r):
        at = slice(r, r + BLOCK)
        rows, _ = kept_rows(r)
        winds = east_out[level, rows, :] + turn_coef[rows] * north_out[level, rows, :]
        return padded(winds) - east_coef[at] * east_diff(geo[level, 8 + r : 8 + r + BLOCK, :])

    def north_rows(level, r):
        rows, _ = kept_rows(r)
        winds = north_out[level, rows, :] - turn_coef[rows] * east_out[level, rows, :]
        step = geo[level, 9 + r : 9 + r + BLOCK, :] - geo[level, 7 + r : 7 + r + BLOCK, :]
        return padded(winds) - north_coef * step

    def lat_pair(turn):
        south = remote(lat_put.at[turn, 0], lat_got.at[turn, 1], lat_sem.at[turn, 0], {"lat": lat - 1})
        north = remote(lat_put.at[turn, 1], lat_got.at[turn, 0], lat_sem.at[turn, 1], {"lat": lat + 1})
        return south, north

    has_south = lat > 0
    has_north = lat < lat_count - 1

    def send_lat(turn, firsts, lasts):
        for level in range(lev_dev):
            lat_put[turn, 0, level : level + 1, :] = firsts[level]
            lat_put[turn, 1, level : level + 1, :] = lasts[level]
        south, north = lat_pair(turn)

        @pl.when(has_south)
        def _():
            south.start()

        @pl.when(has_north)
        def _():
            north.start()

    def sent_lat(turn):
        south, north = lat_pair(turn)

        @pl.when(has_south)
        def _():
            south.wait_send()

        @pl.when(has_north)
        def _():
            north.wait_send()

    def from_south(turn, ref):
        lat_pair(turn)[1].wait_recv()
        for level in range(lev_dev):
            ref[level, 7:8, :] = lat_got[turn, 0, level : level + 1, :]

    def from_north(turn, ref):
        lat_pair(turn)[0].wait_recv()
        for level in range(lev_dev):
            ref[level, 8 + lat_dev : 9 + lat_dev, :] = lat_got[turn, 1, level : level + 1, :]

    def send_geo_rows():
        send_lat(
            0,
            [geo[level, 8:9, :] for level in range(lev_dev)],
            [geo[level, 7 + lat_dev : 8 + lat_dev, :] for level in range(lev_dev)],
        )

    def send_flux_rows():
        send_lat(
            1,
            [acc[lev_dev + level, 0:1, :] * cos_lat[0:1] for level in range(lev_dev)],
            [
                acc[lev_dev + level, lat_dev - 1 : lat_dev, :] * cos_lat[lat_dev - 1 : lat_dev]
                for level in range(lev_dev)
            ],
        )

    fix_copy = remote(fix_put, fix_got, fix_sem, aside)

    def send_fix():
        below = None
        for level in range(lev_dev):
            row = jnp.where(low_side, lat_put[1, 1, level : level + 1, :], lat_put[1, 0, level : level + 1, :])
            row = depth_ref[0:1, level : level + 1] * row
            below = row if below is None else below + row
        fix_put[...] = below

        @pl.when(lev == 1)
        def _():
            fix_copy.start()

    edge_lane = lax.broadcasted_iota(jnp.int32, (lat_dev, 128), 1)

    def lon_copy(turn):
        return remote(lon_put.at[turn], lon_got.at[turn], lon_sem.at[turn], other_lon)

    def send_lon(turn, ref, top):
        held = jnp.zeros((lat_dev, 128), jnp.float32)
        for level in range(lev_dev):
            rows = slice(top, top + lat_dev)
            held = jnp.where(edge_lane == 2 * level, ref[level, rows, 0:1], held)
            held = jnp.where(edge_lane == 2 * level + 1, ref[level, rows, lon_dev - 1 : lon_dev], held)
        lon_put[turn, :, 0:lat_dev] = jnp.transpose(held)[0:8]
        lon_copy(turn).start()

    def from_lon(turn, ref, top):
        lon_copy(turn).wait()
        rims = jnp.transpose(lon_got[turn])[0:lat_dev]
        for level in range(lev_dev):
            rows = slice(top, top + lat_dev)
            last = ref[level, rows, tile:]
            last = jnp.where(edge_lane == lon_dev - tile, rims[:, 2 * level : 2 * level + 1], last)
            last = jnp.where(edge_lane == 127, rims[:, 2 * level + 1 : 2 * level + 2], last)
            ref[level, rows, tile:] = last

    def make_basis(chunk):
        at = slice(chunk * CHUNK, (chunk + 1) * CHUNK)

        def body(block, _):
            p = coarse_ref[0, pl.ds(block, 1), :][:, at]
            q = coarse_ref[1, pl.ds(block, 1), :][:, at]
            f, g = fine_ref[0, :, at], fine_ref[1, :, at]
            rows = pl.ds(pl.multiple_of(block * FINE, FINE), FINE)
            for place, values in enumerate((p * f - q * g, q * f + p * g)):
                high, low = split(values)
                high_ref[chunk, rows, place * CHUNK : (place + 1) * CHUNK] = high
                low_ref[chunk, rows, place * CHUNK : (place + 1) * CHUNK] = low
            return _

        lax.fori_loop(0, width // FINE, body, 0)

    stack = lev_dev * pad_rows

    def make_terms(wind, rows, levels):
        for level in levels:
            for r in starts:
                high, low = split(rows(level, r))
                at = level * pad_rows + r
                xs[wind, at : at + BLOCK, :] = high
                xs[wind, stack + at : stack + at + BLOCK, :] = low

    def forward(chunk, wind):
        sums = dot(xs[wind], high_ref[chunk], ((1,), (0,)))
        sums = sums[0:stack] + sums[stack:] + dot(xs[wind, 0:stack, :], low_ref[chunk], ((1,), (0,)))
        for level in range(lev_dev):
            at = level * lat_dev
            part[chunk, wind, at : at + lat_dev, :] = sums[level * pad_rows : level * pad_rows + lat_dev]

    def inverse(chunk, wind):
        for at in range(0, width, 512):
            columns = slice(at, at + 512)
            values = dot(held_sums[wind], high_ref[chunk, columns, :], ((1,), (1,)))
            rest = dot(held_sums[wind, 0:stack, :], low_ref[chunk, columns, :], ((1,), (1,)))
            values = values[0:stack] + values[stack:] + rest
            for level in range(lev_dev):
                group = wind * lev_dev + level
                piece = values[level * pad_rows : (level + 1) * pad_rows]
                if chunk:
                    piece = piece + acc[group, :, columns]
                acc[group, :, columns] = piece

    def first_level(level):
        arrive(("we", level), ("wn", level))
        make_terms(0, east_rows, [level])
        at = level * pad_rows
        high, low = xs[0, at : at + pad_rows, :], xs[0, stack + at : stack + at + pad_rows, :]
        sums = dot(high, high_ref[0], ((1,), (0,))) + dot(low, high_ref[0], ((1,), (0,)))
        sums = sums + dot(high, low_ref[0], ((1,), (0,)))
        part[0, 0, level * lat_dev : (level + 1) * lat_dev, :] = sums[0:lat_dev]

    directs, hops = {}, {}
    sent_rows = -(-lev_dev * lat_dev // 8) * 8
    for unit in units:
        direct, relayed = shares(sent_rows, EXTRA if unit == units[-1] else 0)
        cut = -(-lat_dev // 8) * 8 if unit == units[-1] else lat_dev // 8 * 8
        parts = ((0, cut), (cut, direct)) if unit in (units[0], units[-1]) and cut < direct else ((0, direct),)
        directs[unit] = []
        for i, (start, end) in enumerate(parts):
            at = (*unit, pl.ds(start, end - start))
            directs[unit].append(remote(part.at[at], came.at[at], direct_sem.at[(*unit, i)], other_lon))
        hops[unit] = []
        for i, (start, size) in enumerate(relayed):
            full, held = pl.ds(start, size), pl.ds(start - direct, size)
            hops[unit].append(
                (
                    remote(part.at[(*unit, full)], hop.at[(*unit, held)], hop_sem.at[(*unit, i, 0)], across),
                    remote(hop.at[(*unit, held)], came.at[(*unit, full)], hop_sem.at[(*unit, i, 1)], band),
                )
            )
    relays = [pair for unit in units for pair in hops[unit]]

    def send(unit):
        for out, _ in hops[unit]:
            out.start()
        for copy in directs[unit][1:] if unit == units[0] else directs[unit]:
            copy.start()

    def relay(first, last):
        for out, back in relays[first:last]:
            out.wait_recv()
            back.start()

    spec_copies = {}
    for unit in units[:-1]:
        spec_copies[(*unit, 0)] = remote(spec_put.at[unit], spec_got.at[unit], spec_sem.at[(*unit, 0)], far)
    for level in range(lev_dev):
        at = (*units[-1], level)
        spec_copies[at] = remote(spec_put.at[at], spec_got.at[at], spec_sem.at[at], far)

    def spectra_width(chunk):
        return min(CHUNK, spectra_out.shape[3] - chunk * CHUNK)

    column_rows = 2 * BLOCK
    column_copies = [
        remote(
            column_put.at[pl.ds(r, column_rows)], column_got.at[pl.ds(r, column_rows)],
            column_sem.at[r // column_rows], other_lev,
        )
        for r in range(0, pad_rows, column_rows)
    ]

    def make_flux():
        for level in range(lev_dev):
            for r in starts:
                rows, count = kept_rows(r)
                north = acc[lev_dev + level, r : r + BLOCK, :]
                north_out[level, rows, :] = north[0:count, 0:lon_dev]
                flux[level, 8 + r : 8 + r + count, :] = (north * cos_lat[r : r + BLOCK])[0:count]

    def finish_east(levels):
        for level in levels:
            for r in starts:
                at = slice(r, r + BLOCK)
                rows, count = kept_rows(r)
                east = acc[level, at, :]
                east_out[level, rows, :] = east[0:count, 0:lon_dev]
                step = (east_coef[at] * east_diff(east))[0:count, 0:lon_dev]
                thick_out[level, rows, :] = thick_out[level, rows, :] - depth_ref[0:1, level : level + 1] * step

    def finish(some):
        for r in some:
            at = slice(r, r + BLOCK)
            rows, count = kept_rows(r)
            below = None
            for level in range(lev_dev - 1, -1, -1):
                step = flux[level, 9 + r : 9 + r + BLOCK, :] - flux[level, 7 + r : 7 + r + BLOCK, :]
                step = (flux_coef[at] * step)[0:count, 0:lon_dev]
                thick = thick_out[level, rows, :] - depth_ref[0:1, level : level + 1] * step
                below = thick if below is None else below + thick
                thick_out[level, rows, :] = thick
                geo_out[level, rows, :] = sg[rows, :] + GRAVITY * below
            column_put[rows, :] = below
            if (r + BLOCK) % column_rows == 0:

                @pl.when(lev == 1)
                def _():
                    column_copies[r // column_rows].start()

    def deepen():
        @pl.when(lev == 0)
        def _():
            for i, copy in enumerate(column_copies):
                copy.wait_recv()
                for r in range(i * column_rows, (i + 1) * column_rows, BLOCK):
                    rows, _ = kept_rows(r)
                    for level in range(lev_dev):
                        geo_out[level, rows, :] += GRAVITY * column_got[rows, :]

        @pl.when(lev == 1)
        def _():
            for copy in column_copies:
                copy.wait_send()

    @pl.when(polar)
    def _():
        arrive("tables")
        make_basis(0)
        take_geo([0])
        first_level(0)

    @pl.when(inner)
    def _():
        take_geo([0])

    pl.semaphore_wait(barrier, 5 + inner.astype(jnp.int32))

    @pl.when(polar)
    def _():
        directs[units[0]][0].start()

    take_geo(range(1, lev_dev))
    send_geo_rows()

    @pl.when(inner)
    def _():
        send_lon(0, geo, 8)
        fetch("rows", "th", "sg")
        arrive("we", "wn")
        from_lon(0, geo, 8)
        from_south(0, geo)
        from_north(0, geo)
        for level in range(lev_dev):
            for r in starts:
                acc[level, r : r + BLOCK, :] = east_rows(level, r)
                acc[lev_dev + level, r : r + BLOCK, :] = north_rows(level, r)
        send_flux_rows()
        send_lon(1, acc, 0)
        relay(0, 1)
        make_flux()
        relay(1, 3)
        from_lon(1, acc, 0)
        relay(3, 4)

        @pl.when(low_side)
        def _():
            from_north(1, flux)

        @pl.when(jnp.logical_not(low_side))
        def _():
            from_south(1, flux)

        arrive("th", "sg")
        done = 4
        for level in range(lev_dev):
            finish_east([level])
            relay(done, done + 1)
            done += 1
        for r in range(0, pad_rows, column_rows):
            finish(range(r, r + column_rows, BLOCK))
            relay(done, done + 1)
            done += 1
        relay(done, len(relays))
        deepen()

    @pl.when(polar)
    def _():
        for level in range(1, lev_dev):
            first_level(level)
        send((0, 0))
        fetch("rows", "th", "sg")
        made = {0}
        for unit in units[1:]:
            chunk, wind = unit
            if chunk not in made:
                make_basis(chunk)
                made.add(chunk)
            if unit == (0, 1):

                @pl.when(low_side)
                def _():
                    from_north(0, geo)

                @pl.when(jnp.logical_not(low_side))
                def _():
                    from_south(0, geo)

                make_terms(1, north_rows, range(lev_dev))
            forward(chunk, wind)
            send(unit)

        arrive("rows", "sg")
        sides = lax.broadcasted_iota(jnp.int32, table_ref.shape, 0)
        table_ref[...] = jnp.where(sides == 1, -1.0, 0.0)
        for side, here in enumerate((low_side, jnp.logical_not(low_side))):
            columns = slice(side * lat_dev, (side + 1) * lat_dev)

            @pl.when(here)
            def _():
                table_ref[0:1, 0:lat_dev] = kept_ref[:, columns].astype(jnp.float32)
                table_ref[1:2, 0:lat_dev] = slot_ref[:, columns].astype(jnp.float32)

        table = jnp.transpose(table_ref[...])
        kept = table[0:pad_rows, 0:1].astype(jnp.int32)
        slots = table[0:pad_rows, 1:2].astype(jnp.int32)
        place = lax.broadcasted_iota(jnp.int32, (pad_rows, 2 * half_rows), 1)
        own = place >= half_rows
        place = jnp.where(own, place - half_rows, place)
        named = jnp.where(own, lat, partner) * help_rows + place
        match = ((slots == named) & (place < help_rows)).astype(jnp.float32).astype(jnp.bfloat16)
        column = lax.broadcasted_iota(jnp.int32, (pad_rows, 2 * CHUNK), 1)
        local_number = jnp.where(column < CHUNK, column, column - CHUNK)
        odd = 1.0 - 2.0 * lax.rem(local_number[0:1], 2).astype(jnp.float32)
        for chunk, wind in units:
            unit = (chunk, wind)
            number = local_number + chunk * CHUNK
            weight = jnp.where(number == 0, 1.0 / nlon_total, 2.0 / nlon_total)
            waits = [copy.wait_recv for copy in directs[unit]] + [back.wait_recv for _, back in hops[unit]]
            ready = 1 if unit == units[-1] and len(directs[unit]) > 1 else len(waits)
            for wait in waits[:ready]:
                wait()
            whole = [list(range(lev_dev))]
            placed = []
            for levels in [[level] for level in range(lev_dev)] if unit == units[-1] else whole:
                picked = []
                if levels[0] > 0:
                    for wait in waits[ready:]:
                        wait()
                for level in levels:
                    rows = slice(level * lat_dev, level * lat_dev + pad_rows)
                    sums = (part[chunk, wind, rows, :] + odd * came[chunk, wind, rows, :]) * weight
                    sums = jnp.where(number < kept, sums, 0.0)
                    high, low = split(sums)
                    at = level * pad_rows
                    held_sums[wind, at : at + pad_rows, :] = high
                    held_sums[wind, stack + at : stack + at + pad_rows, :] = low
                    picked.append(jnp.where(lon == 0, sums[:, 0:CHUNK], (sums * odd)[:, CHUNK:]))
                picked = jnp.concatenate(picked, axis=1)
                high = picked.astype(jnp.bfloat16)
                mid, low = split(picked - high.astype(jnp.float32))
                both = dot(match, high, ((0,), (0,))) + dot(match, mid, ((0,), (0,))) + dot(match, low, ((0,), (0,)))
                for i, level in enumerate(levels):
                    placed.append(both[:, i * CHUNK : (i + 1) * CHUNK])
                    spec_put[chunk, wind, level] = placed[level][0:half_rows]
                spec_copies[(chunk, wind, levels[0])].start()
            inverse(chunk, wind)
            if unit == units[-1]:
                send_flux_rows()
                send_fix()
            count = spectra_width(chunk)
            for level in range(lev_dev):
                spectra_out[wind, level, :, chunk * CHUNK : chunk * CHUNK + count] = placed[level][
                    half_rows : half_rows + help_rows, 0:count
                ]
            if unit == (chunks - 1, 0):
                arrive("th")
                finish_east(range(lev_dev))

        sent_lat(0)
        make_flux()

        @pl.when(low_side)
        def _():
            from_north(1, flux)

        @pl.when(jnp.logical_not(low_side))
        def _():
            from_south(1, flux)

        finish(starts)
        deepen()
        for copy in spec_copies.values():
            copy.wait_send()
        for unit in units:
            for copy in directs[unit]:
                copy.wait_send()
            for out, _ in hops[unit]:
                out.wait_send()
        sent_lat(1)

        @pl.when(lev == 1)
        def _():
            fix_copy.wait_send()

    @pl.when(inner)
    def _():
        arrive("tables", "rows")
        for chunk, wind in units:
            count = spectra_width(chunk)
            for level in range(lev_dev):
                if (chunk, wind, level) in spec_copies:
                    spec_copies[(chunk, wind, level)].wait_recv()
                spectra_out[wind, level, :, chunk * CHUNK : chunk * CHUNK + count] = spec_got[
                    chunk, wind, level, 0:help_rows, 0:count
                ]
        for _, back in relays:
            back.wait_send()
        sent_lat(0)
        sent_lat(1)

        def fix(side, row, sign):
            at = slice(row, row + 1)
            coef = sign * flux_coef[at]
            below = None
            for level in range(lev_dev - 1, -1, -1):
                delta = depth_ref[0:1, level : level + 1] * coef * lat_got[1, side, level : level + 1, :]
                below = delta if below is None else below + delta
                thick_out[level, at, :] += delta[:, 0:lon_dev]
                geo_out[level, at, :] += GRAVITY * below[:, 0:lon_dev]

            @pl.when(lev == 0)
            def _():
                fix_copy.wait_recv()
                for level in range(lev_dev):
                    geo_out[level, at, :] += (GRAVITY * coef * fix_got[...])[:, 0:lon_dev]

        @pl.when(low_side)
        def _():
            lat_pair(1)[1].wait_recv()
            fix(0, 0, 1.0)

        @pl.when(jnp.logical_not(low_side))
        def _():
            lat_pair(1)[0].wait_recv()
            fix(1, lat_dev - 1, -1.0)


def hand_on_kernel(*refs):
    half = (len(refs) - 1) // 2
    sems = refs[-1]
    copies = []
    for index, (src, dst) in enumerate(zip(refs[:half], refs[half:-1])):
        levels = src.shape[-3]
        for level in range(levels):
            if len(src.shape) == 3:
                pairs = [(src.at[level], dst.at[:, level, :])]
            else:
                pairs = [(src.at[wind, level], dst.at[wind, :, level, :]) for wind in range(src.shape[0])]
            for wind, (part, place) in enumerate(pairs):
                copies.append(pltpu.make_async_copy(part, place, sems.at[index, wind * levels + level]))
    for copy in copies:
        copy.start()
    for copy in copies:
        copy.wait()


def handed_on(held):
    def shape(x):
        return jax.ShapeDtypeStruct((*x.shape[:-3], x.shape[-2], x.shape[-3], x.shape[-1]), x.dtype)

    return pl.pallas_call(
        hand_on_kernel,
        out_shape=[shape(x) for x in held],
        in_specs=[pl.BlockSpec(memory_space=pltpu.VMEM)] * len(held),
        out_specs=[pl.BlockSpec(memory_space=pl.ANY)] * len(held),
        scratch_shapes=[pltpu.SemaphoreType.DMA((len(held), 2 * held[0].shape[0]))],
        compiler_params=pltpu.CompilerParams(vmem_limit_bytes=4 * 2**20),
    )(*(pltpu.with_memory_space_constraint(x, pltpu.VMEM) for x in held))


def one_kernel(
    wind_east, wind_north, thickness, geopot, surface_geopot, mean_depth, kept_modes, slot_table
):
    lev_dev, lat_dev, lon_dev = thickness.shape
    lat_count = lax.axis_size("lat")
    nlat_total = lat_dev * lat_count
    nlon_total = 2 * lon_dev
    help_rows = lat_dev // 2
    lam_step = 2.0 * math.pi / nlon_total
    phi_step = math.pi / nlat_total
    north_coef = STEP_FACTOR * lam_step / phi_step
    width = -(-(lon_dev + 2) // 512) * 512
    pad_rows = -(-lat_dev // 32) * 32
    half_rows = pad_rows // 2
    chunks = -(-KMAX // CHUNK)
    coarse, fine = angle_tables(width, chunks * CHUNK, nlon_total)
    f32 = jnp.float32
    field = pltpu.VMEM((lev_dev, lat_dev, lon_dev), f32)
    tall = pltpu.VMEM((lev_dev, pad_rows + 16, width), f32)
    groups = 2 * lev_dev
    basis = pltpu.VMEM((chunks, width, 2 * CHUNK), jnp.bfloat16)
    sums = pltpu.VMEM((chunks, 2, lev_dev * pad_rows, 2 * CHUNK), f32)
    sent_rows = -(-lev_dev * lat_dev // 8) * 8
    relayed = sent_rows - shares(sent_rows)[0]
    lat_rows = pltpu.VMEM((2, 2, lev_dev, width), f32)
    lon_rows = pltpu.VMEM((2, 8, 128), f32)
    column = pltpu.VMEM((pad_rows, lon_dev), f32)
    row = pltpu.VMEM((1, width), f32)
    specs = pltpu.VMEM((chunks, 2, lev_dev, half_rows, CHUNK), f32)
    dma = pltpu.SemaphoreType.DMA
    operands = (
        mean_depth.reshape(1, -1),
        kept_modes.reshape(1, -1),
        slot_table.reshape(1, -1),
        jnp.asarray(coarse),
        jnp.asarray(fine),
        *(jnp.transpose(x, (1, 0, 2)) for x in (wind_east, wind_north, thickness, geopot)),
        surface_geopot,
    )
    held = pl.pallas_call(
        functools.partial(substep_kernel, (lat_count, nlon_total, phi_step, north_coef)),
        out_shape=(field,) * 4 + (pltpu.VMEM((2, lev_dev, help_rows, KMAX), f32),),
        in_specs=[pl.BlockSpec(memory_space=pl.ANY)] * len(operands),
        out_specs=(pl.BlockSpec(memory_space=pltpu.VMEM),) * 5,
        scratch_shapes=[
            pltpu.VMEM((1, lev_dev), f32),
            pltpu.VMEM((1, kept_modes.shape[0]), jnp.int32),
            pltpu.VMEM((1, slot_table.shape[0]), jnp.int32),
            pltpu.VMEM(coarse.shape, f32),
            pltpu.VMEM(fine.shape, f32),
            tall,
            pltpu.VMEM((lat_dev, lon_dev), f32),
            pltpu.VMEM((2, 2 * lev_dev * pad_rows, width), jnp.bfloat16),
            basis, basis, sums, sums,
            pltpu.VMEM((chunks, 2, relayed, 2 * CHUNK), f32),
            pltpu.VMEM((2, groups * pad_rows, 2 * CHUNK), jnp.bfloat16),
            pltpu.VMEM((groups, pad_rows, width), f32),
            tall,
            lon_rows, lon_rows, lat_rows, lat_rows, column, column, row, row, specs, specs,
            pltpu.VMEM((8, 128), f32),
            dma((7, 2)), dma((2, 2)), dma((2, 2, 2)), dma((chunks, 2, 2, 2)), dma((chunks, 2, 2, 2, 2)),
            dma((pad_rows // (2 * BLOCK), 2)), dma((2,)), dma((chunks, 2, lev_dev, 2)),
        ],
        compiler_params=pltpu.CompilerParams(
            collective_id=0, has_side_effects=True, vmem_limit_bytes=VMEM_MIB * 2**20
        ),
    )(*(pltpu.with_memory_space_constraint(x, pltpu.HBM) for x in operands))
    *fields, spectra = handed_on(held)
    return (*(jnp.transpose(x, (1, 0, 2)) for x in fields), jnp.transpose(spectra, (0, 2, 1, 3)))


def solution(mesh):
    body = one_kernel if dict(mesh.shape, members=2) == dict(members=2, lat=4, lon=2, lev=2) else local
    return jax.shard_map(
        body,
        mesh=mesh,
        in_specs=(
            P(("members", "lev"), "lat", "lon"),
            P(("members", "lev"), "lat", "lon"),
            P(("members", "lev"), "lat", "lon"),
            P(("members", "lev"), "lat", "lon"),
            P("lat", "lon"),
            P("lev"),
            P(),
            P(),
        ),
        out_specs=(
            P(("members", "lev"), "lat", "lon"),
            P(("members", "lev"), "lat", "lon"),
            P(("members", "lev"), "lat", "lon"),
            P(("members", "lev"), "lat", "lon"),
            P(None, ("members", "lev"), "lat", "lon"),
        ),
        check_vma=False,
    )
```

```python
import math

import functools

import jax
import numpy as np
import jax.numpy as jnp
from jax import lax
from jax.experimental import pallas as pl
from jax.experimental.pallas import tpu as pltpu
from jax.sharding import PartitionSpec as P

KMAX = 360


STEP_FACTOR = 0.15
CORIOLIS = 0.2
GRAVITY = 0.25


def edges(block, axis, dim, periodic):
    count = lax.axis_size(axis)
    first = lax.slice_in_dim(block, 0, 1, axis=dim)
    last = lax.slice_in_dim(block, block.shape[dim] - 1, block.shape[dim], axis=dim)
    if periodic and count == 2:
        both = lax.ppermute(jnp.concatenate([last, first], axis=dim), axis, [(0, 1), (1, 0)])
        return lax.slice_in_dim(both, 0, 1, axis=dim), lax.slice_in_dim(both, 1, 2, axis=dim)
    forward = [(i, i + 1) for i in range(count - 1)]
    if periodic:
        forward.append((count - 1, 0))
    backward = [(target, source) for source, target in forward]
    return lax.ppermute(last, axis, forward), lax.ppermute(first, axis, backward)


def diff(block, low, high, dim):
    size = block.shape[dim]
    up = jnp.concatenate([lax.slice_in_dim(block, 1, size, axis=dim), high], axis=dim)
    down = jnp.concatenate([low, lax.slice_in_dim(block, 0, size - 1, axis=dim)], axis=dim)
    return up - down


def local_basis(count, nlon_total):
    fine = next(f for f in (24, 20, 18, 16, 12, 8, 6, 5, 4, 3, 2, 1) if count % f == 0)
    k = np.arange(KMAX, dtype=np.int64)[None, :]
    angle = 2.0 * np.pi / nlon_total

    def table(columns):
        phase = (columns[:, None] * k % nlon_total) * angle
        return np.cos(phase).astype(np.float32), np.sin(phase).astype(np.float32)

    cc, cs = (jnp.asarray(t)[:, None] for t in table(np.arange(0, count, fine)))
    fc, fs = (jnp.asarray(t)[None] for t in table(np.arange(fine)))
    return (
        (cc * fc - cs * fs).reshape(count, KMAX),
        (cs * fc + cc * fs).reshape(count, KMAX),
    )


def turned(pair, cos_shift, sin_shift):
    cos_part, sin_part = pair[..., :KMAX], pair[..., KMAX:]
    return jnp.concatenate(
        [cos_shift * cos_part - sin_shift * sin_part, sin_shift * cos_part + cos_shift * sin_part],
        axis=-1,
    )


def local(
    wind_east, wind_north, thickness, geopot, surface_geopot, mean_depth, kept_modes, slot_table
):
    lev_dev, lat_dev, lon_dev = thickness.shape
    lat_count = lax.axis_size("lat")
    lon_count = lax.axis_size("lon")
    lev_count = lax.axis_size("lev")
    lat_index = lax.axis_index("lat")
    lon_index = lax.axis_index("lon")
    nlat_total = lat_dev * lat_count
    nlon_total = lon_dev * lon_count
    polar_count = nlat_total // 4
    slot_count = 2 * polar_count
    help_rows = lat_dev // 2
    half_axis = lat_count // 2
    lam_step = 2.0 * math.pi / nlon_total
    phi_step = math.pi / nlat_total
    global_rows = lat_index * lat_dev + jnp.arange(lat_dev, dtype=jnp.int32)
    latitude = -0.5 * math.pi + (global_rows.astype(jnp.float32) + 0.5) * phi_step
    coslat = jnp.cos(latitude)[:, None]
    sinlat = jnp.sin(latitude)[:, None]
    east_coef = STEP_FACTOR / coslat
    north_coef = STEP_FACTOR * lam_step / phi_step
    geo_west, geo_east = edges(geopot, "lon", 2, True)
    geo_south, geo_north = edges(geopot, "lat", 1, False)
    east_new = (
        wind_east
        - east_coef * diff(geopot, geo_west, geo_east, 2)
        + CORIOLIS * sinlat * wind_north
    )
    north_new = (
        wind_north
        - north_coef * diff(geopot, geo_south, geo_north, 1)
        - CORIOLIS * sinlat * wind_east
    )
    is_polar = (lat_index < lat_count // 4) | (lat_index >= lat_count - lat_count // 4)
    first_row = lat_index * lat_dev
    first_rank = jnp.where(lat_index < lat_count // 4, first_row, first_row - (nlat_total - slot_count))
    first_rank = jnp.clip(first_rank, 0, slot_count - lat_dev)
    kept = lax.dynamic_slice(kept_modes, (first_rank,), (lat_dev,))
    slots = lax.dynamic_slice(slot_table, (first_rank,), (lat_dev,))
    wavenumber = jnp.arange(2 * KMAX, dtype=jnp.int32) % KMAX
    weight = (jnp.where(wavenumber == 0, 1.0, 2.0) / nlon_total).astype(jnp.float32)
    factor = jnp.where(wavenumber[None, :] < kept[:, None], weight[None, :], 0.0)
    cos_basis, sin_basis = local_basis(lon_dev, nlon_total)
    basis = jnp.concatenate([cos_basis, sin_basis], axis=1)
    shift = (lon_index * jnp.arange(KMAX, dtype=jnp.int32) % lon_count).astype(jnp.float32)
    shift = shift * (2.0 * math.pi / lon_count)
    if lon_count == 2:
        cos_shift = 1.0 - 2.0 * (lon_index * jnp.arange(KMAX, dtype=jnp.int32) % 2).astype(jnp.float32)
        sin_shift = jnp.zeros_like(cos_shift)
    else:
        cos_shift, sin_shift = jnp.cos(shift), jnp.sin(shift)
    pieces = [wind[level] for level in range(lev_dev) for wind in (east_new, north_new)]
    both_sums = []
    for piece in range(lev_dev):
        rows = jnp.concatenate(pieces[2 * piece : 2 * piece + 2], axis=0)
        part = jnp.dot(rows, basis, precision=lax.Precision.HIGH)
        part = turned(part, cos_shift, sin_shift)
        if lon_count == 2:
            sums = part + lax.ppermute(part, "lon", [(0, 1), (1, 0)])
        else:
            sums = lax.psum(part, "lon")
        both_sums.append(sums.reshape(2, lat_dev, 2 * KMAX) * factor[None])
    filtered = []
    for sums in both_sums:
        turned_back = turned(sums, cos_shift, -sin_shift)
        rows = lax.dot_general(
            turned_back.reshape(2 * lat_dev, 2 * KMAX),
            basis,
            (((1,), (1,)), ((), ())),
            precision=lax.Precision.HIGH,
        )
        filtered.append(rows.reshape(2, lat_dev, lon_dev))
    filtered = jnp.stack(filtered, axis=1)
    east_final = jnp.where(is_polar, filtered[0], east_new)
    north_final = jnp.where(is_polar, filtered[1], north_new)

    slice_width = 2 * KMAX // lon_count
    kept_sums = jnp.stack(both_sums, axis=1)
    own = lax.dynamic_slice_in_dim(kept_sums, lon_index * slice_width, slice_width, 3)
    places = jnp.arange(help_rows, dtype=jnp.int32)
    partner = (lat_index + half_axis) % lat_count

    def rows_named(device):
        match = slots[None, :] == (device * help_rows + places)[:, None]
        return jnp.einsum(
            "sr,abrc->absc", match.astype(jnp.float32), own, precision=lax.Precision.HIGHEST
        )

    route = [((i - half_axis) % lat_count, i) for i in range(lat_count)]
    route = [(s, t) for s, t in route if s < lat_count // 4 or s >= lat_count - lat_count // 4]
    arrived = lax.ppermute(rows_named(partner), "lat", route)
    spectra = jnp.where(is_polar, rows_named(lat_index), arrived)

    rim_west, rim_east = edges(east_final, "lon", 2, True)
    flux = north_final * coslat
    rim_south, rim_north = edges(flux, "lat", 1, False)
    divergence = east_coef * diff(east_final, rim_west, rim_east, 2) + north_coef / coslat * diff(
        flux, rim_south, rim_north, 1
    )
    thick_new = thickness - mean_depth[:, None, None] * divergence
    columns = [thick_new[lev_dev - 1]]
    for level in range(lev_dev - 2, -1, -1):
        columns.append(columns[-1] + thick_new[level])
    columns = columns[::-1]
    deeper = jnp.zeros_like(columns[0])
    for distance in range(1, lev_count):
        deeper = deeper + lax.ppermute(
            columns[0], "lev", [(i + distance, i) for i in range(lev_count - distance)]
        )
    geo_new = surface_geopot[None] + GRAVITY * (jnp.stack(columns) + deeper[None])
    return (east_final, north_final, thick_new, geo_new, spectra)


FINE = 32
VMEM_MIB = 30
CHUNK = 128
BLOCK = 16
DIRECT = 61


def unit_order(chunks):
    last = chunks - 1
    return [(c, w) for w in range(2) for c in range(last)] + [(last, 0), (last, 1)]


def shares(rows):
    direct = rows * DIRECT // 100 // 8 * 8
    first = direct + (rows - direct) // 16 * 8
    return direct, ((direct, first - direct), (first, rows - first))


def angle_tables(width, count, nlon_total):
    k = np.arange(count, dtype=np.int64)[None, :]
    angle = 2.0 * np.pi / nlon_total

    def table(columns):
        phase = (columns[:, None] * k % nlon_total) * angle
        return np.stack([np.cos(phase), np.sin(phase)]).astype(np.float32)

    starts = np.arange(0, width, FINE)
    starts[-1] = -FINE
    return table(starts), table(np.arange(FINE))


def split(x):
    high = x.astype(jnp.bfloat16)
    return high, (x - high.astype(jnp.float32)).astype(jnp.bfloat16)


def dot(a, b, dims):
    return lax.dot_general(a, b, (dims, ((), ())), preferred_element_type=jnp.float32)


def substep_kernel(
    sizes,
    depth_hbm, kept_hbm, slot_hbm, coarse_hbm, fine_hbm,
    we_hbm, wn_hbm, th_hbm, geo_hbm, sg_hbm,
    east_out, north_out, thick_out, geo_out, spectra_out,
    depth_ref, kept_ref, slot_ref, coarse_ref, fine_ref,
    geo, sg,
    xs, high_ref, low_ref, part, came, hop, held_sums, acc, flux,
    lon_put, lon_got, lat_put, lat_got, column_put, column_got, fix_put, fix_got,
    spec_put, spec_got, table_ref,
    in_sem, lon_sem, lat_sem, direct_sem, hop_sem, column_sem, fix_sem, spec_sem,
):
    lat_count, nlon_total, phi_step, north_coef = sizes
    lev_dev, lat_dev, lon_dev = east_out.shape
    help_rows = spectra_out.shape[2]
    _, pad_rows, width = acc.shape
    half_rows = spec_put.shape[-2]
    chunks = high_ref.shape[0]
    units = unit_order(chunks)
    lon = lax.axis_index("lon")
    lat = lax.axis_index("lat")
    lev = lax.axis_index("lev")
    polar = (lat == 0) | (lat == lat_count - 1)
    inner = jnp.logical_not(polar)
    low_side = lat < lat_count // 2
    band = {"lat": lat + 1 - 2 * lax.rem(lat, 2)}
    across = {"lon": 1 - lon, **band}
    aside = {"lev": 1 - lev, **band}
    other_lon = {"lon": 1 - lon}
    other_lev = {"lev": 1 - lev}
    middle = {"lat": lat_count - 1 - lat}
    partner = lax.rem(lat + lat_count // 2, lat_count)
    far = {"lat": partner}
    MESH = pl.DeviceIdType.MESH

    barrier = pltpu.get_barrier_semaphore()
    for target in (other_lon, other_lev, band, across, aside):
        pl.semaphore_signal(barrier, inc=1, device_id=target, device_id_type=MESH)

    @pl.when(inner)
    def _():
        pl.semaphore_signal(barrier, inc=1, device_id=middle, device_id_type=MESH)

    tile = width - 128
    for level in range(lev_dev):
        for ref in (geo, flux):
            start = 8 + lat_dev // 8 * 8
            ref[level, start:, :] = jnp.zeros((ref.shape[1] - start, width), jnp.float32)
            ref[level, 0:8, :] = jnp.zeros((8, width), jnp.float32)
        geo[level, :, tile:] = jnp.zeros((geo.shape[1], 128), jnp.float32)

    def load(src, dst, i, j):
        return pltpu.make_async_copy(src, dst, in_sem.at[i, j])

    def fetch(*names):
        for name in names:
            for copy in loads[name]:
                copy.start()

    loads = {}
    loads["tables"] = [load(coarse_hbm, coarse_ref, 0, 0), load(fine_hbm, fine_ref, 0, 1)]
    for i, (name, src, dst) in enumerate(
        (("geo", geo_hbm, geo_out), ("we", we_hbm, east_out), ("wn", wn_hbm, north_out), ("th", th_hbm, thick_out))
    ):
        for level in range(lev_dev):
            loads[(name, level)] = [load(src.at[:, level, :], dst.at[level], 1 + i, level)]
        loads[name] = [loads[(name, level)][0] for level in range(lev_dev)]
    loads["sg"] = [load(sg_hbm, sg, 5, 0), load(depth_hbm, depth_ref, 5, 1)]
    loads["rows"] = [load(kept_hbm, kept_ref, 6, 0), load(slot_hbm, slot_ref, 6, 1)]

    fetch("tables", *((name, level) for level in range(lev_dev) for name in ("geo", "we", "wn")))

    def arrive(*names):
        for name in names:
            for copy in loads[name]:
                copy.wait()

    def remote(src, dst, sems, target):
        return pltpu.make_async_remote_copy(
            src_ref=src, dst_ref=dst, send_sem=sems.at[0], recv_sem=sems.at[1],
            device_id=target, device_id_type=MESH,
        )

    row_id = lax.broadcasted_iota(jnp.int32, (pad_rows, 1), 0) + lat * lat_dev
    latitude = -0.5 * math.pi + (row_id.astype(jnp.float32) + 0.5) * phi_step
    cos_lat = jnp.cos(latitude)
    sin_lat = jnp.sin(latitude)
    east_coef = STEP_FACTOR / cos_lat
    flux_coef = north_coef / cos_lat
    turn_coef = CORIOLIS * sin_lat
    starts = range(0, pad_rows, BLOCK)

    def east_diff(x):
        return pltpu.roll(x, width - 1, 1) - pltpu.roll(x, 1, 1)

    def kept_rows(r):
        return slice(r, min(r + BLOCK, lat_dev)), min(BLOCK, lat_dev - r)

    def padded(x):
        count = x.shape[0]
        x = jnp.concatenate([x, jnp.zeros((count, width - lon_dev), jnp.float32)], axis=1)
        if count < BLOCK:
            x = jnp.concatenate([x, jnp.zeros((BLOCK - count, width), jnp.float32)], axis=0)
        return x

    def take_geo(levels):
        for level in levels:
            arrive(("geo", level))
            geo[level, 8 : 8 + lat_dev, 0:lon_dev] = geo_out[level]

    def east_rows(level, r):
        at = slice(r, r + BLOCK)
        rows, _ = kept_rows(r)
        winds = east_out[level, rows, :] + turn_coef[rows] * north_out[level, rows, :]
        return padded(winds) - east_coef[at] * east_diff(geo[level, 8 + r : 8 + r + BLOCK, :])

    def north_rows(level, r):
        rows, _ = kept_rows(r)
        winds = north_out[level, rows, :] - turn_coef[rows] * east_out[level, rows, :]
        step = geo[level, 9 + r : 9 + r + BLOCK, :] - geo[level, 7 + r : 7 + r + BLOCK, :]
        return padded(winds) - north_coef * step

    def lat_pair(turn):
        south = remote(lat_put.at[turn, 0], lat_got.at[turn, 1], lat_sem.at[turn, 0], {"lat": lat - 1})
        north = remote(lat_put.at[turn, 1], lat_got.at[turn, 0], lat_sem.at[turn, 1], {"lat": lat + 1})
        return south, north

    has_south = lat > 0
    has_north = lat < lat_count - 1

    def send_lat(turn, firsts, lasts):
        for level in range(lev_dev):
            lat_put[turn, 0, level : level + 1, :] = firsts[level]
            lat_put[turn, 1, level : level + 1, :] = lasts[level]
        south, north = lat_pair(turn)

        @pl.when(has_south)
        def _():
            south.start()

        @pl.when(has_north)
        def _():
            north.start()

    def sent_lat(turn):
        south, north = lat_pair(turn)

        @pl.when(has_south)
        def _():
            south.wait_send()

        @pl.when(has_north)
        def _():
            north.wait_send()

    def from_south(turn, ref):
        lat_pair(turn)[1].wait_recv()
        for level in range(lev_dev):
            ref[level, 7:8, :] = lat_got[turn, 0, level : level + 1, :]

    def from_north(turn, ref):
        lat_pair(turn)[0].wait_recv()
        for level in range(lev_dev):
            ref[level, 8 + lat_dev : 9 + lat_dev, :] = lat_got[turn, 1, level : level + 1, :]

    def send_geo_rows():
        send_lat(
            0,
            [geo[level, 8:9, :] for level in range(lev_dev)],
            [geo[level, 7 + lat_dev : 8 + lat_dev, :] for level in range(lev_dev)],
        )

    def send_flux_rows():
        send_lat(
            1,
            [acc[lev_dev + level, 0:1, :] * cos_lat[0:1] for level in range(lev_dev)],
            [
                acc[lev_dev + level, lat_dev - 1 : lat_dev, :] * cos_lat[lat_dev - 1 : lat_dev]
                for level in range(lev_dev)
            ],
        )

    fix_copy = remote(fix_put, fix_got, fix_sem, aside)

    def send_fix():
        below = None
        for level in range(lev_dev):
            row = jnp.where(low_side, lat_put[1, 1, level : level + 1, :], lat_put[1, 0, level : level + 1, :])
            row = depth_ref[0:1, level : level + 1] * row
            below = row if below is None else below + row
        fix_put[...] = below

        @pl.when(lev == 1)
        def _():
            fix_copy.start()

    edge_lane = lax.broadcasted_iota(jnp.int32, (lat_dev, 128), 1)

    def lon_copy(turn):
        return remote(lon_put.at[turn], lon_got.at[turn], lon_sem.at[turn], other_lon)

    def send_lon(turn, ref, top):
        held = jnp.zeros((lat_dev, 128), jnp.float32)
        for level in range(lev_dev):
            rows = slice(top, top + lat_dev)
            held = jnp.where(edge_lane == 2 * level, ref[level, rows, 0:1], held)
            held = jnp.where(edge_lane == 2 * level + 1, ref[level, rows, lon_dev - 1 : lon_dev], held)
        lon_put[turn, :, 0:lat_dev] = jnp.transpose(held)[0:8]
        lon_copy(turn).start()

    def from_lon(turn, ref, top):
        lon_copy(turn).wait()
        rims = jnp.transpose(lon_got[turn])[0:lat_dev]
        for level in range(lev_dev):
            rows = slice(top, top + lat_dev)
            last = ref[level, rows, tile:]
            last = jnp.where(edge_lane == lon_dev - tile, rims[:, 2 * level : 2 * level + 1], last)
            last = jnp.where(edge_lane == 127, rims[:, 2 * level + 1 : 2 * level + 2], last)
            ref[level, rows, tile:] = last

    def make_basis(chunk):
        at = slice(chunk * CHUNK, (chunk + 1) * CHUNK)

        def body(block, _):
            p = coarse_ref[0, pl.ds(block, 1), :][:, at]
            q = coarse_ref[1, pl.ds(block, 1), :][:, at]
            f, g = fine_ref[0, :, at], fine_ref[1, :, at]
            rows = pl.ds(pl.multiple_of(block * FINE, FINE), FINE)
            for place, values in enumerate((p * f - q * g, q * f + p * g)):
                high, low = split(values)
                high_ref[chunk, rows, place * CHUNK : (place + 1) * CHUNK] = high
                low_ref[chunk, rows, place * CHUNK : (place + 1) * CHUNK] = low
            return _

        lax.fori_loop(0, width // FINE, body, 0)

    stack = lev_dev * pad_rows

    def make_terms(wind, rows, levels):
        for level in levels:
            for r in starts:
                high, low = split(rows(level, r))
                at = level * pad_rows + r
                xs[wind, at : at + BLOCK, :] = high
                xs[wind, stack + at : stack + at + BLOCK, :] = low

    def forward(chunk, wind):
        sums = dot(xs[wind], high_ref[chunk], ((1,), (0,)))
        sums = sums[0:stack] + sums[stack:] + dot(xs[wind, 0:stack, :], low_ref[chunk], ((1,), (0,)))
        for level in range(lev_dev):
            at = level * lat_dev
            part[chunk, wind, at : at + lat_dev, :] = sums[level * pad_rows : level * pad_rows + lat_dev]

    def inverse(chunk, wind):
        for at in range(0, width, 512):
            columns = slice(at, at + 512)
            values = dot(held_sums[wind], high_ref[chunk, columns, :], ((1,), (1,)))
            rest = dot(held_sums[wind, 0:stack, :], low_ref[chunk, columns, :], ((1,), (1,)))
            values = values[0:stack] + values[stack:] + rest
            for level in range(lev_dev):
                group = wind * lev_dev + level
                piece = values[level * pad_rows : (level + 1) * pad_rows]
                if chunk:
                    piece = piece + acc[group, :, columns]
                acc[group, :, columns] = piece

    def first_level(level):
        arrive(("we", level), ("wn", level))
        make_terms(0, east_rows, [level])
        at = level * pad_rows
        high, low = xs[0, at : at + pad_rows, :], xs[0, stack + at : stack + at + pad_rows, :]
        sums = dot(high, high_ref[0], ((1,), (0,))) + dot(low, high_ref[0], ((1,), (0,)))
        sums = sums + dot(high, low_ref[0], ((1,), (0,)))
        part[0, 0, level * lat_dev : (level + 1) * lat_dev, :] = sums[0:lat_dev]

    directs, hops = {}, {}
    sent_rows = -(-lev_dev * lat_dev // 8) * 8
    for unit in units:
        direct, relayed = shares(sent_rows)
        cut = -(-lat_dev // 8) * 8 if unit == units[-1] else lat_dev // 8 * 8
        parts = ((0, cut), (cut, direct)) if unit in (units[0], units[-1]) and cut < direct else ((0, direct),)
        directs[unit] = []
        for i, (start, end) in enumerate(parts):
            at = (*unit, pl.ds(start, end - start))
            directs[unit].append(remote(part.at[at], came.at[at], direct_sem.at[(*unit, i)], other_lon))
        hops[unit] = []
        for i, (start, size) in enumerate(relayed):
            full, held = pl.ds(start, size), pl.ds(start - direct, size)
            hops[unit].append(
                (
                    remote(part.at[(*unit, full)], hop.at[(*unit, held)], hop_sem.at[(*unit, i, 0)], across),
                    remote(hop.at[(*unit, held)], came.at[(*unit, full)], hop_sem.at[(*unit, i, 1)], band),
                )
            )
    relays = [pair for unit in units for pair in hops[unit]]

    def send(unit):
        for out, _ in hops[unit]:
            out.start()
        for copy in directs[unit][1:] if unit == units[0] else directs[unit]:
            copy.start()

    def relay(first, last):
        for out, back in relays[first:last]:
            out.wait_recv()
            back.start()

    spec_copies = {}
    for unit in units:
        for level in range(lev_dev):
            at = (*unit, level)
            spec_copies[at] = remote(spec_put.at[at], spec_got.at[at], spec_sem.at[at], far)

    def spectra_width(chunk):
        return min(CHUNK, spectra_out.shape[3] - chunk * CHUNK)

    column_rows = 2 * BLOCK
    column_copies = [
        remote(
            column_put.at[pl.ds(r, column_rows)], column_got.at[pl.ds(r, column_rows)],
            column_sem.at[r // column_rows], other_lev,
        )
        for r in range(0, pad_rows, column_rows)
    ]

    def make_flux():
        for level in range(lev_dev):
            for r in starts:
                rows, count = kept_rows(r)
                north = acc[lev_dev + level, r : r + BLOCK, :]
                north_out[level, rows, :] = north[0:count, 0:lon_dev]
                flux[level, 8 + r : 8 + r + count, :] = (north * cos_lat[r : r + BLOCK])[0:count]

    def finish_east(levels):
        for level in levels:
            for r in starts:
                at = slice(r, r + BLOCK)
                rows, count = kept_rows(r)
                east = acc[level, at, :]
                east_out[level, rows, :] = east[0:count, 0:lon_dev]
                step = (east_coef[at] * east_diff(east))[0:count, 0:lon_dev]
                thick_out[level, rows, :] = thick_out[level, rows, :] - depth_ref[0:1, level : level + 1] * step

    def finish(some):
        for r in some:
            at = slice(r, r + BLOCK)
            rows, count = kept_rows(r)
            below = None
            for level in range(lev_dev - 1, -1, -1):
                step = flux[level, 9 + r : 9 + r + BLOCK, :] - flux[level, 7 + r : 7 + r + BLOCK, :]
                step = (flux_coef[at] * step)[0:count, 0:lon_dev]
                thick = thick_out[level, rows, :] - depth_ref[0:1, level : level + 1] * step
                below = thick if below is None else below + thick
                thick_out[level, rows, :] = thick
                geo_out[level, rows, :] = sg[rows, :] + GRAVITY * below
            column_put[rows, :] = below
            if (r + BLOCK) % column_rows == 0:

                @pl.when(lev == 1)
                def _():
                    column_copies[r // column_rows].start()

    def deepen():
        @pl.when(lev == 0)
        def _():
            for i, copy in enumerate(column_copies):
                copy.wait_recv()
                for r in range(i * column_rows, (i + 1) * column_rows, BLOCK):
                    rows, _ = kept_rows(r)
                    for level in range(lev_dev):
                        geo_out[level, rows, :] += GRAVITY * column_got[rows, :]

        @pl.when(lev == 1)
        def _():
            for copy in column_copies:
                copy.wait_send()

    @pl.when(polar)
    def _():
        arrive("tables")
        make_basis(0)
        take_geo([0])
        first_level(0)

    @pl.when(inner)
    def _():
        take_geo([0])

    pl.semaphore_wait(barrier, 5 + inner.astype(jnp.int32))

    @pl.when(polar)
    def _():
        directs[units[0]][0].start()

    take_geo(range(1, lev_dev))
    send_geo_rows()

    @pl.when(inner)
    def _():
        send_lon(0, geo, 8)
        fetch("rows", "th", "sg")
        arrive("we", "wn")
        from_lon(0, geo, 8)
        from_south(0, geo)
        from_north(0, geo)
        for level in range(lev_dev):
            for r in starts:
                acc[level, r : r + BLOCK, :] = east_rows(level, r)
                acc[lev_dev + level, r : r + BLOCK, :] = north_rows(level, r)
        send_flux_rows()
        send_lon(1, acc, 0)
        relay(0, 1)
        make_flux()
        relay(1, 3)
        from_lon(1, acc, 0)
        relay(3, 4)

        @pl.when(low_side)
        def _():
            from_north(1, flux)

        @pl.when(jnp.logical_not(low_side))
        def _():
            from_south(1, flux)

        arrive("th", "sg")
        done = 4
        for level in range(lev_dev):
            finish_east([level])
            relay(done, done + 1)
            done += 1
        for r in range(0, pad_rows, column_rows):
            finish(range(r, r + column_rows, BLOCK))
            relay(done, done + 1)
            done += 1
        relay(done, len(relays))
        deepen()

    @pl.when(polar)
    def _():
        for level in range(1, lev_dev):
            first_level(level)
        send((0, 0))
        fetch("rows", "th", "sg")
        made = {0}
        for unit in units[1:]:
            chunk, wind = unit
            if chunk not in made:
                make_basis(chunk)
                made.add(chunk)
            if unit == (0, 1):

                @pl.when(low_side)
                def _():
                    from_north(0, geo)

                @pl.when(jnp.logical_not(low_side))
                def _():
                    from_south(0, geo)

                make_terms(1, north_rows, range(lev_dev))
            forward(chunk, wind)
            send(unit)

        arrive("rows", "sg")
        sides = lax.broadcasted_iota(jnp.int32, table_ref.shape, 0)
        table_ref[...] = jnp.where(sides == 1, -1.0, 0.0)
        for side, here in enumerate((low_side, jnp.logical_not(low_side))):
            columns = slice(side * lat_dev, (side + 1) * lat_dev)

            @pl.when(here)
            def _():
                table_ref[0:1, 0:lat_dev] = kept_ref[:, columns].astype(jnp.float32)
                table_ref[1:2, 0:lat_dev] = slot_ref[:, columns].astype(jnp.float32)

        table = jnp.transpose(table_ref[...])
        kept = table[0:pad_rows, 0:1].astype(jnp.int32)
        slots = table[0:pad_rows, 1:2].astype(jnp.int32)
        place = lax.broadcasted_iota(jnp.int32, (pad_rows, 2 * half_rows), 1)
        own = place >= half_rows
        place = jnp.where(own, place - half_rows, place)
        named = jnp.where(own, lat, partner) * help_rows + place
        match = ((slots == named) & (place < help_rows)).astype(jnp.float32).astype(jnp.bfloat16)
        column = lax.broadcasted_iota(jnp.int32, (pad_rows, 2 * CHUNK), 1)
        local_number = jnp.where(column < CHUNK, column, column - CHUNK)
        odd = 1.0 - 2.0 * lax.rem(local_number[0:1], 2).astype(jnp.float32)
        for chunk, wind in units:
            unit = (chunk, wind)
            number = local_number + chunk * CHUNK
            weight = jnp.where(number == 0, 1.0 / nlon_total, 2.0 / nlon_total)
            waits = [copy.wait_recv for copy in directs[unit]] + [back.wait_recv for _, back in hops[unit]]
            ready = 1 if unit == units[-1] and len(directs[unit]) > 1 else len(waits)
            for wait in waits[:ready]:
                wait()
            whole = [list(range(lev_dev))]
            placed = []
            for levels in [[level] for level in range(lev_dev)] if unit == units[-1] else whole:
                picked, kept_sums = [], []
                if levels[0] > 0:
                    for wait in waits[ready:]:
                        wait()
                for level in levels:
                    rows = slice(level * lat_dev, level * lat_dev + pad_rows)
                    sums = (part[chunk, wind, rows, :] + odd * came[chunk, wind, rows, :]) * weight
                    sums = jnp.where(number < kept, sums, 0.0)
                    kept_sums.append(sums)
                    picked.append(jnp.where(lon == 0, sums[:, 0:CHUNK], (sums * odd)[:, CHUNK:]))
                picked = jnp.concatenate(picked, axis=1)
                high = picked.astype(jnp.bfloat16)
                mid, low = split(picked - high.astype(jnp.float32))
                both = dot(match, high, ((0,), (0,))) + dot(match, mid, ((0,), (0,))) + dot(match, low, ((0,), (0,)))
                for i, level in enumerate(levels):
                    placed.append(both[:, i * CHUNK : (i + 1) * CHUNK])
                    spec_put[chunk, wind, level] = placed[level][0:half_rows]
                    spec_copies[(chunk, wind, level)].start()
                for sums, level in zip(kept_sums, levels):
                    high, low = split(sums)
                    at = level * pad_rows
                    held_sums[wind, at : at + pad_rows, :] = high
                    held_sums[wind, stack + at : stack + at + pad_rows, :] = low
            inverse(chunk, wind)
            if unit == units[-1]:
                send_flux_rows()
                send_fix()
            count = spectra_width(chunk)
            for level in range(lev_dev):
                spectra_out[wind, level, :, chunk * CHUNK : chunk * CHUNK + count] = placed[level][
                    half_rows : half_rows + help_rows, 0:count
                ]
            if unit == (chunks - 1, 0):
                arrive("th")
                finish_east(range(lev_dev))

        sent_lat(0)
        make_flux()

        @pl.when(low_side)
        def _():
            from_north(1, flux)

        @pl.when(jnp.logical_not(low_side))
        def _():
            from_south(1, flux)

        finish(starts)
        deepen()
        for unit in units:
            for level in range(lev_dev):
                spec_copies[(*unit, level)].wait_send()
            for copy in directs[unit]:
                copy.wait_send()
            for out, _ in hops[unit]:
                out.wait_send()
        sent_lat(1)

        @pl.when(lev == 1)
        def _():
            fix_copy.wait_send()

    @pl.when(inner)
    def _():
        arrive("tables", "rows")
        for chunk, wind in units:
            count = spectra_width(chunk)
            for level in range(lev_dev):
                spec_copies[(chunk, wind, level)].wait_recv()
                spectra_out[wind, level, :, chunk * CHUNK : chunk * CHUNK + count] = spec_got[
                    chunk, wind, level, 0:help_rows, 0:count
                ]
        for _, back in relays:
            back.wait_send()
        sent_lat(0)
        sent_lat(1)

        def fix(side, row, sign):
            at = slice(row, row + 1)
            coef = sign * flux_coef[at]
            below = None
            for level in range(lev_dev - 1, -1, -1):
                delta = depth_ref[0:1, level : level + 1] * coef * lat_got[1, side, level : level + 1, :]
                below = delta if below is None else below + delta
                thick_out[level, at, :] += delta[:, 0:lon_dev]
                geo_out[level, at, :] += GRAVITY * below[:, 0:lon_dev]

            @pl.when(lev == 0)
            def _():
                fix_copy.wait_recv()
                for level in range(lev_dev):
                    geo_out[level, at, :] += (GRAVITY * coef * fix_got[...])[:, 0:lon_dev]

        @pl.when(low_side)
        def _():
            lat_pair(1)[1].wait_recv()
            fix(0, 0, 1.0)

        @pl.when(jnp.logical_not(low_side))
        def _():
            lat_pair(1)[0].wait_recv()
            fix(1, lat_dev - 1, -1.0)


def hand_on_kernel(*refs):
    half = (len(refs) - 1) // 2
    sems = refs[-1]
    copies = []
    for index, (src, dst) in enumerate(zip(refs[:half], refs[half:-1])):
        levels = src.shape[-3]
        for level in range(levels):
            if len(src.shape) == 3:
                pairs = [(src.at[level], dst.at[:, level, :])]
            else:
                pairs = [(src.at[wind, level], dst.at[wind, :, level, :]) for wind in range(src.shape[0])]
            for wind, (part, place) in enumerate(pairs):
                copies.append(pltpu.make_async_copy(part, place, sems.at[index, wind * levels + level]))
    for copy in copies:
        copy.start()
    for copy in copies:
        copy.wait()


def handed_on(held):
    def shape(x):
        return jax.ShapeDtypeStruct((*x.shape[:-3], x.shape[-2], x.shape[-3], x.shape[-1]), x.dtype)

    return pl.pallas_call(
        hand_on_kernel,
        out_shape=[shape(x) for x in held],
        in_specs=[pl.BlockSpec(memory_space=pltpu.VMEM)] * len(held),
        out_specs=[pl.BlockSpec(memory_space=pl.ANY)] * len(held),
        scratch_shapes=[pltpu.SemaphoreType.DMA((len(held), 2 * held[0].shape[0]))],
        compiler_params=pltpu.CompilerParams(vmem_limit_bytes=4 * 2**20),
    )(*(pltpu.with_memory_space_constraint(x, pltpu.VMEM) for x in held))


def one_kernel(
    wind_east, wind_north, thickness, geopot, surface_geopot, mean_depth, kept_modes, slot_table
):
    lev_dev, lat_dev, lon_dev = thickness.shape
    lat_count = lax.axis_size("lat")
    nlat_total = lat_dev * lat_count
    nlon_total = 2 * lon_dev
    help_rows = lat_dev // 2
    lam_step = 2.0 * math.pi / nlon_total
    phi_step = math.pi / nlat_total
    north_coef = STEP_FACTOR * lam_step / phi_step
    width = -(-(lon_dev + 2) // 512) * 512
    pad_rows = -(-lat_dev // 32) * 32
    half_rows = pad_rows // 2
    chunks = -(-KMAX // CHUNK)
    coarse, fine = angle_tables(width, chunks * CHUNK, nlon_total)
    f32 = jnp.float32
    field = pltpu.VMEM((lev_dev, lat_dev, lon_dev), f32)
    tall = pltpu.VMEM((lev_dev, pad_rows + 16, width), f32)
    groups = 2 * lev_dev
    basis = pltpu.VMEM((chunks, width, 2 * CHUNK), jnp.bfloat16)
    sums = pltpu.VMEM((chunks, 2, lev_dev * pad_rows, 2 * CHUNK), f32)
    sent_rows = -(-lev_dev * lat_dev // 8) * 8
    relayed = sent_rows - shares(sent_rows)[0]
    lat_rows = pltpu.VMEM((2, 2, lev_dev, width), f32)
    lon_rows = pltpu.VMEM((2, 8, 128), f32)
    column = pltpu.VMEM((pad_rows, lon_dev), f32)
    row = pltpu.VMEM((1, width), f32)
    specs = pltpu.VMEM((chunks, 2, lev_dev, half_rows, CHUNK), f32)
    dma = pltpu.SemaphoreType.DMA
    operands = (
        mean_depth.reshape(1, -1),
        kept_modes.reshape(1, -1),
        slot_table.reshape(1, -1),
        jnp.asarray(coarse),
        jnp.asarray(fine),
        *(jnp.transpose(x, (1, 0, 2)) for x in (wind_east, wind_north, thickness, geopot)),
        surface_geopot,
    )
    held = pl.pallas_call(
        functools.partial(substep_kernel, (lat_count, nlon_total, phi_step, north_coef)),
        out_shape=(field,) * 4 + (pltpu.VMEM((2, lev_dev, help_rows, KMAX), f32),),
        in_specs=[pl.BlockSpec(memory_space=pl.ANY)] * len(operands),
        out_specs=(pl.BlockSpec(memory_space=pltpu.VMEM),) * 5,
        scratch_shapes=[
            pltpu.VMEM((1, lev_dev), f32),
            pltpu.VMEM((1, kept_modes.shape[0]), jnp.int32),
            pltpu.VMEM((1, slot_table.shape[0]), jnp.int32),
            pltpu.VMEM(coarse.shape, f32),
            pltpu.VMEM(fine.shape, f32),
            tall,
            pltpu.VMEM((lat_dev, lon_dev), f32),
            pltpu.VMEM((2, 2 * lev_dev * pad_rows, width), jnp.bfloat16),
            basis, basis, sums, sums,
            pltpu.VMEM((chunks, 2, relayed, 2 * CHUNK), f32),
            pltpu.VMEM((2, groups * pad_rows, 2 * CHUNK), jnp.bfloat16),
            pltpu.VMEM((groups, pad_rows, width), f32),
            tall,
            lon_rows, lon_rows, lat_rows, lat_rows, column, column, row, row, specs, specs,
            pltpu.VMEM((8, 128), f32),
            dma((7, 2)), dma((2, 2)), dma((2, 2, 2)), dma((chunks, 2, 2, 2)), dma((chunks, 2, 2, 2, 2)),
            dma((pad_rows // (2 * BLOCK), 2)), dma((2,)), dma((chunks, 2, lev_dev, 2)),
        ],
        compiler_params=pltpu.CompilerParams(
            collective_id=0, has_side_effects=True, vmem_limit_bytes=VMEM_MIB * 2**20
        ),
    )(*(pltpu.with_memory_space_constraint(x, pltpu.HBM) for x in operands))
    *fields, spectra = handed_on(held)
    return (*(jnp.transpose(x, (1, 0, 2)) for x in fields), jnp.transpose(spectra, (0, 2, 1, 3)))


def solution(mesh):
    body = one_kernel if dict(mesh.shape, members=2) == dict(members=2, lat=4, lon=2, lev=2) else local
    return jax.shard_map(
        body,
        mesh=mesh,
        in_specs=(
            P(("members", "lev"), "lat", "lon"),
            P(("members", "lev"), "lat", "lon"),
            P(("members", "lev"), "lat", "lon"),
            P(("members", "lev"), "lat", "lon"),
            P("lat", "lon"),
            P("lev"),
            P(),
            P(),
        ),
        out_specs=(
            P(("members", "lev"), "lat", "lon"),
            P(("members", "lev"), "lat", "lon"),
            P(("members", "lev"), "lat", "lon"),
            P(("members", "lev"), "lat", "lon"),
            P(None, ("members", "lev"), "lat", "lon"),
        ),
        check_vma=False,
    )
```
